32 devices in a mesh: fsdp: 32 (over z, y, x, core).
Axes of the slice: x: 2, y: 2, z: 4, core: 2. Of those that a mesh axis runs over, the one named last changes fastest.
Arguments:
- tokens: bfloat16 [32768, 768], P('fsdp'), may hold values from -6 to 6
- neighbours: bfloat16 [32768, 768], P('fsdp'), may hold values from -6 to 6
- block_lengths: int32 [64, 4], P('fsdp'), may hold values from 1 to 256, 512 in all within a row
- chosen: int32 [64, 8, 2], P('fsdp'), may hold values from 0 to 3
- cotangent: bfloat16 [32768, 768], P('fsdp'), may hold values from -6 to 6
- w_qkv: bfloat16 [768, 2304], P('fsdp'), may hold values from -0.21875 to 0.21875
- w_out: bfloat16 [768, 768], P('fsdp'), may hold values from -2 to 2
- w_cross_q: bfloat16 [768, 768], P('fsdp'), may hold values from -0.21875 to 0.21875
- w_cross_kv: bfloat16 [768, 1536], P('fsdp'), may hold values from -0.21875 to 0.21875
- w_cross_out: bfloat16 [768, 768], P('fsdp'), may hold values from -2 to 2
- w_up: bfloat16 [768, 3072], P('fsdp'), may hold values from -0.21875 to 0.21875
- w_down: bfloat16 [3072, 768], P('fsdp'), may hold values from -0.109375 to 0.109375
- biases: bfloat16 [8, 768], P(None, 'fsdp'), may hold values from -1.5 to 1.5
- up_bias: bfloat16 [3072], P('fsdp'), may hold values from -1.5 to 1.5
- norm_gains: bfloat16 [3, 768], P(None, 'fsdp'), may hold values from 0.25 to 1.75
- norm_shifts: bfloat16 [3, 768], P(None, 'fsdp'), may hold values from -1.5 to 1.5
Outputs:
- output: bfloat16 [32768, 768], P('fsdp')
- token_grad: float32 [32768, 768], P('fsdp')
- neighbour_grad: float32 [32768, 768], P('fsdp')
- grad_w_qkv: float32 [768, 2304], P('fsdp')
- grad_w_out: float32 [768, 768], P('fsdp')
- grad_w_cross_q: float32 [768, 768], P('fsdp')
- grad_w_cross_kv: float32 [768, 1536], P('fsdp')
- grad_w_cross_out: float32 [768, 768], P('fsdp')
- grad_w_up: float32 [768, 3072], P('fsdp')
- grad_w_down: float32 [3072, 768], P('fsdp')
- grad_biases: float32 [8, 768], P(None, 'fsdp')
- grad_up_bias: float32 [3072], P('fsdp')
- grad_norm_gains: float32 [3, 768], P(None, 'fsdp')
- grad_norm_shifts: float32 [3, 768], P(None, 'fsdp')
The draws below stay inside these ranges and needn't reach their ends.
Inputs may be any that keep to these rules, and one draw needn't show every extreme that they name: `block_lengths`: each row holds the lengths of the 4 consecutive attention blocks of one sequence; they sum to 512, and the longest in every row is exactly 256. chosen[s, c, i] is an entry of sequence s's own 4 neighbours; two slots of a span may name the same entry.
All inputs are finite; a program needn't handle non-finite values.
Results may differ from the reference program's by a relative error of at most 0.02.
Values may be sent and summed in bfloat16 or wider, within the bound.
No kernel may reach another device: no remote copies, remote signals or barrier semaphores. Data moves between devices by JAX's collectives and lax.ppermute only.
A program may use at most 320 MiB of HBM per device.

```python
import math
import jax
import jax.numpy as jnp
import numpy as np
from jax import lax

D = 768
HEADS = 12
HEAD_DIM = 64
FF = 3072
SEQ_LEN = 512
BLOCK = 256
NBLK = 4
SPAN = 64
NBR_LEN = 128
K_NBR = 2
POOL = 4
SPANS = 8
SEQS = 64
TOKENS = 32768
NBR_ROWS = 32768


def place_ends(entries, stream_key, smallest, largest):
    index_at = [jax.random.randint(jax.random.fold_in(stream_key, axis), (), 0, length) for axis, length in enumerate(entries.shape)]
    main_axis = entries.shape.index(max(entries.shape))
    beside = index_at[:main_axis] + [(index_at[main_axis] + 1) % entries.shape[main_axis]] + index_at[main_axis + 1:]
    return entries.at[tuple(index_at)].set(smallest).at[tuple(beside)].set(largest)


def with_spikes(values, stream_key, source, target, blocks, factor):
    def block_of(position):
        return (jnp.arange(values.shape[position]) // (values.shape[position] // blocks)).reshape((-1,) + (1,) * (values.ndim - 1 - position))

    near = jax.random.permutation(stream_key, blocks)[block_of(target)]
    second = (block_of(target) + blocks // 2) % blocks
    return jnp.where((block_of(source) == near) | (block_of(source) == second), factor * values, values)


def levels(rng, extent, cuts, low, high):
    level = 1.0
    for position, parts in cuts:
        heights = jax.random.uniform(jax.random.fold_in(jax.random.fold_in(rng, 6), position), (parts,), jnp.float32, low / len(cuts), high / len(cuts))
        level = level * jnp.repeat(jnp.exp(heights), extent[position] // parts).reshape((-1,) + (1,) * (len(extent) - 1 - position))
    return level


def profile(number_of, total, limit, slope):
    weights = [(1 << 20) // math.isqrt(grade ** slope) + 1 for grade in range(2, number_of + 1)]
    rest, holding = total - limit - (number_of - 1), [1] * (number_of - 1)
    while rest > 0:
        candidates = [i for i in range(number_of - 1) if holding[i] < limit]
        mass, budget = sum([weights[i] for i in candidates]), rest
        for i in candidates:
            more = min(limit - holding[i], max(1, budget * weights[i] // mass), rest)
            holding[i] = holding[i] + more
            rest = rest - more
    return np.array([limit] + holding)


def uneven(stream_key, count, total, most, slope):
    if count == 2:
        one = jax.random.randint(stream_key, (), max(1, total - most), min(most, total - 1) + 1)
        return jnp.stack([one, total - one])
    sizes = jnp.asarray(profile(count, total, most, slope), jnp.int32)
    twos = (count - 1) // 2
    giver, sink = sizes[1:1 + 2 * twos:2], sizes[2:2 + 2 * twos:2]
    margin = jnp.minimum(giver - 1, most - sink)
    passed = jax.random.randint(jax.random.fold_in(stream_key, 1), (twos,), 0, 1 << 20) % (margin + 1)
    sizes = sizes.at[1:1 + 2 * twos:2].set(giver - passed).at[2:2 + 2 * twos:2].set(sink + passed)
    return sizes[jax.random.permutation(jax.random.fold_in(stream_key, 2), count)]


def scatter_about(key, shape, deviation, reach, shards=(), held_as=jnp.bfloat16):
    level = levels(key, shape, shards, -0.22, 0.18) if shards else 1.0
    drawn = jax.random.normal(key, shape, jnp.float32) * deviation * level
    return jnp.minimum(jnp.maximum(drawn, -reach), reach).astype(held_as)


def bell_draw_with(rng, shape, scale, limit, shards, heavy, kind=jnp.bfloat16):
    values = scale * jax.random.normal(rng, shape, jnp.float32)
    if shards:
        values = values * levels(rng, shape, shards, -0.22, 0.18)
    return jnp.clip(with_spikes(values, jax.random.fold_in(rng, 3), *heavy), -limit, limit).astype(kind)


def setup_inputs(seed: int = 0) -> dict:
    splits = jax.random.split(jax.random.key(seed), 17)
    return {
        "tokens": scatter_about(splits[0], (TOKENS, D), 1.0, 6.0, ((0, 32),)),
        "neighbours": bell_draw_with(splits[1], (NBR_ROWS, D), 1.0, 6.0, ((0, 32),), (0, 1, 32, 2.75)),
        "block_lengths": jax.vmap(lambda own: uneven(own, NBLK, SEQ_LEN, BLOCK, 0))(jax.random.split(splits[2], SEQS)).reshape((SEQS, NBLK)).astype(jnp.int32),
        "chosen": place_ends(jax.random.randint(splits[3], (SEQS, SPANS, K_NBR), 0, POOL), jax.random.fold_in(splits[3], 1), 0, POOL - 1).astype(jnp.int32),
        "cotangent": bell_draw_with(splits[4], (TOKENS, D), 1.0, 6.0, ((0, 32),), (0, 1, 32, 2.75)),
        "w_qkv": scatter_about(splits[5], (D, 3 * D), D ** -0.5, 0.21875, ((0, 32),)),
        "w_out": scatter_about(splits[6], (D, D), (max(D // 96, 1)) ** -0.5, 2.0, ((0, 32),)),
        "w_cross_q": scatter_about(splits[7], (D, D), D ** -0.5, 0.21875, ((0, 32),)),
        "w_cross_kv": scatter_about(splits[8], (D, 2 * D), D ** -0.5, 0.21875, ((0, 32),)),
        "w_cross_out": scatter_about(splits[9], (D, D), (max(D // 96, 1)) ** -0.5, 2.0, ((0, 32),)),
        "w_up": scatter_about(splits[10], (D, FF), D ** -0.5, 0.21875, ((0, 32),)),
        "w_down": scatter_about(splits[11], (FF, D), FF ** -0.5, 0.109375, ((0, 32),)),
        "biases": scatter_about(splits[12], (8, D), 0.3, 1.5, ((1, 32),)),
        "up_bias": scatter_about(splits[13], (FF,), 0.3, 1.5, ((0, 32),)),
        "norm_gains": jnp.clip(1.0 + 0.15 * jax.random.normal(splits[14], (3, D), jnp.float32), 0.25, 1.75).astype(jnp.bfloat16),
        "norm_shifts": scatter_about(splits[15], (3, D), 0.3, 1.5, ((1, 32),)),
    }


@jax.custom_vjp
def low(v):
    return lax.optimization_barrier(v.astype(jnp.bfloat16)).astype(jnp.float32)

@jax.custom_vjp
def low_back(v):
    return v

def low_keep(v):
    return (low(v), None)

def low_pass(kept, grad):
    return (grad,)

def back_keep(v):
    return (v, None)

def back_low(kept, grad):
    return (low(grad),)
low.defvjp(low_keep, low_pass)
low_back.defvjp(back_keep, back_low)
highest = lax.Precision.HIGHEST
epsilon = 1e-05
rope_base = 10000.0
gelu_coeff = 0.044715

def product(left, right):
    return jnp.dot(left, right, precision=highest, preferred_element_type=jnp.float32)

def round_both(values):
    return low(low_back(values))

def layer_norm(inputs, gain_row, shift_row):
    average = lax.optimization_barrier(jnp.mean(inputs, -1, keepdims=True))
    centred = inputs - average
    return centred * lax.rsqrt(lax.optimization_barrier(jnp.mean(centred * centred, -1, keepdims=True)) + epsilon) * gain_row + shift_row

def rotary_tables():
    half_dim = HEAD_DIM // 2
    inverse = jnp.exp(jnp.arange(half_dim, dtype=jnp.float32) * (-2.0 * math.log(rope_base) / HEAD_DIM))
    angles = jnp.arange(SEQ_LEN, dtype=jnp.float32)[:, None] * inverse[None, :]
    return (jnp.cos(angles)[:, None, :], jnp.sin(angles)[:, None, :])

def rotate(inputs, cosine, sine):
    half_dim = HEAD_DIM // 2
    first_half = inputs[..., :half_dim]
    second_half = inputs[..., half_dim:]
    return jnp.concatenate([first_half * cosine - second_half * sine, second_half * cosine + first_half * sine], -1)

def gelu(inputs):
    inner = math.sqrt(2.0 / math.pi) * (inputs + gelu_coeff * inputs ** 3)
    return 0.5 * inputs * (1.0 + jnp.tanh(inner))

def softmax_rows(scores):
    row_max = lax.optimization_barrier(jnp.max(scores, -1, keepdims=True))
    exponent = jnp.exp(scores - row_max)
    return exponent / lax.optimization_barrier(jnp.sum(exponent, -1, keepdims=True))

def block_index(lengths):
    block_ends = jnp.cumsum(lengths)
    positions = jnp.arange(SEQ_LEN, dtype=jnp.int32)
    return lax.optimization_barrier(jnp.sum((positions[:, None] >= block_ends[None, :]).astype(jnp.int32), -1))

def self_attend(packed):
    queries, key_rows, value_rows, lengths = packed
    block_ids = block_index(lengths)
    allowed = block_ids[None, :] <= block_ids[:, None]
    scores = low_back(jnp.einsum('qhe,khe->hqk', queries, key_rows, precision=highest) * HEAD_DIM ** (-0.5))
    weights = softmax_rows(jnp.where(allowed[None], scores, -1e+30))
    return jnp.einsum('hqk,khe->qhe', low(weights), value_rows, precision=highest)

def cross_attend(packed):
    queries, key_pool, value_pool, chosen_rows = packed
    query_blocks = queries.reshape(SPANS, SPAN, HEADS, HEAD_DIM)
    key_rows = jnp.take(key_pool, chosen_rows, axis=0).reshape(SPANS, K_NBR * NBR_LEN, HEADS, HEAD_DIM)
    value_rows = jnp.take(value_pool, chosen_rows, axis=0).reshape(SPANS, K_NBR * NBR_LEN, HEADS, HEAD_DIM)
    scores = low_back(jnp.einsum('cqhe,ckhe->chqk', query_blocks, key_rows, precision=highest) * HEAD_DIM ** (-0.5))
    weights = softmax_rows(scores)
    attended = jnp.einsum('chqk,ckhe->cqhe', low(weights), value_rows, precision=highest)
    return attended.reshape(SEQ_LEN, HEADS, HEAD_DIM)

def forward(inputs, neighbour_rows, lengths, chosen_rows, w_qkv, w_out, w_cross_q, w_cross_kv, w_cross_out, w_up, w_down, biases, up_bias, norm_gains, norm_shifts):
    seq_count = lengths.shape[0]
    cosine, sine = rotary_tables()
    attn_in = low(layer_norm(inputs, norm_gains[0], norm_shifts[0]))
    bias_qkv = jnp.concatenate([biases[0], biases[1], biases[2]])
    mixed_rows = low_back(product(attn_in, w_qkv) + bias_qkv).reshape(seq_count, SEQ_LEN, 3, HEADS, HEAD_DIM)
    queries = low(rotate(mixed_rows[:, :, 0], cosine, sine))
    key_rows = low(rotate(mixed_rows[:, :, 1], cosine, sine))
    value_rows = low(mixed_rows[:, :, 2])
    attended = lax.map(jax.checkpoint(self_attend), (queries, key_rows, value_rows, lengths))
    attended = round_both(attended.reshape(seq_count * SEQ_LEN, D))
    first_sum = inputs + low_back(product(attended, w_out) + biases[3])
    cross_in = low(layer_norm(first_sum, norm_gains[1], norm_shifts[1]))
    cross_queries = round_both(product(cross_in, w_cross_q) + biases[4]).reshape(seq_count, SEQ_LEN, HEADS, HEAD_DIM)
    kv_bias = jnp.concatenate([jnp.zeros_like(biases[5]), biases[5]])
    kv_pool = round_both(product(neighbour_rows, w_cross_kv) + kv_bias).reshape(seq_count, POOL, NBR_LEN, 2, HEADS, HEAD_DIM)
    crossed = lax.map(jax.checkpoint(cross_attend), (cross_queries, kv_pool[:, :, :, 0], kv_pool[:, :, :, 1], chosen_rows))
    crossed = round_both(crossed.reshape(seq_count * SEQ_LEN, D))
    second_sum = first_sum + low_back(product(crossed, w_cross_out) + biases[6])
    mlp_in = low(layer_norm(second_sum, norm_gains[2], norm_shifts[2]))
    hidden = low_back(product(mlp_in, w_up) + up_bias)
    return second_sum + product(low(gelu(hidden)), w_down) + biases[7]

def reference(tokens, neighbours, block_lengths, chosen, cotangent, w_qkv, w_out, w_cross_q, w_cross_kv, w_cross_out, w_up, w_down, biases, up_bias, norm_gains, norm_shifts):
    weights_all = (w_qkv.astype(jnp.float32), w_out.astype(jnp.float32), w_cross_q.astype(jnp.float32), w_cross_kv.astype(jnp.float32), w_cross_out.astype(jnp.float32), w_up.astype(jnp.float32), w_down.astype(jnp.float32), biases.astype(jnp.float32), up_bias.astype(jnp.float32), norm_gains.astype(jnp.float32), norm_shifts.astype(jnp.float32))
    group = math.gcd(SEQS, max(1, 4096 // SEQ_LEN))
    steps_count = SEQS // group
    token_groups = tokens.astype(jnp.float32).reshape(steps_count, group * SEQ_LEN, D)
    neighbour_groups = neighbours.astype(jnp.float32).reshape(steps_count, group * POOL * NBR_LEN, D)
    length_groups = block_lengths.reshape(steps_count, group, NBLK)
    chosen_groups = chosen.reshape(steps_count, group, SPANS, K_NBR)
    upstream_groups = cotangent.astype(jnp.float32).reshape(steps_count, group * SEQ_LEN, D)

    def one_group(totals, packed):
        token_rows, neighbour_rows, lengths, chosen_rows, upstream = packed

        def local_layer(token_in, neighbour_in, *weight_list):
            return forward(token_in, neighbour_in, lengths, chosen_rows, *weight_list)
        result, pullback = jax.vjp(local_layer, token_rows, neighbour_rows, *weights_all)
        gradients = pullback(upstream)
        totals = tuple((running + addition for running, addition in zip(totals, gradients[2:])))
        return (totals, (result.astype(jnp.bfloat16), gradients[0], gradients[1]))
    zeros_all = tuple((jnp.zeros_like(weight) for weight in weights_all))
    totals, (results, token_grads, neighbour_grads) = lax.scan(one_group, zeros_all, (token_groups, neighbour_groups, length_groups, chosen_groups, upstream_groups))
    return (results.reshape(TOKENS, D), token_grads.reshape(TOKENS, D), neighbour_grads.reshape(NBR_ROWS, D), totals[0], totals[1], totals[2], totals[3], totals[4], totals[5], totals[6], totals[7], totals[8], totals[9], totals[10])
```

```python
import functools
import math

import jax
import jax.numpy as jnp
from jax import lax
from jax.experimental import pallas as pl
from jax.experimental.pallas import tpu as pltpu
from jax.sharding import PartitionSpec as P

D = 768
HEADS = 12
HEAD_DIM = 64
FF = 3072
SEQ_LEN = 512
SPAN = 64
SPANS = 8
NBR_LEN = 128
K_NBR = 2
POOL = 4
PAIRS = HEADS // 2
LANES = 128
ROWS = 256
SMALL = 18
TILE_F = 512

epsilon = 1e-05
rope_base = 10000.0
gelu_coeff = 0.044715
scale = HEAD_DIM ** (-0.5)
f32 = jnp.float32
bf16 = jnp.bfloat16


def geometry(count):
    side = round((count / 4) ** (1 / 3))
    sizes = (2 * side, side, side, 2)
    assert math.prod(sizes) == count
    return sizes


def coords_of(index, sizes):
    found = []
    for size in reversed(sizes):
        found.append(index % size)
        index = index // size
    return tuple(reversed(found))


def index_of(coords, sizes):
    index = 0
    for coord, size in zip(coords, sizes):
        index = index * size + coord
    return index


def shift_pairs(sizes, axis, step):
    pairs = []
    for source in range(math.prod(sizes)):
        coords = list(coords_of(source, sizes))
        coords[axis] = (coords[axis] + step) % sizes[axis]
        pairs.append((source, index_of(coords, sizes)))
    return pairs


def shift(values, sizes, axis, step):
    return lax.ppermute(values, "fsdp", shift_pairs(sizes, axis, step))


def after(values, *anchors):
    return lax.optimization_barrier((values,) + anchors)[0]


def gather_z(block, sizes):
    parts = [block] + [shift(block, sizes, 0, d) for d in range(1, sizes[0])]
    return jnp.stack(parts)


def gather_rest(own, sizes):
    half = own.shape[-1] // 2
    nz, ny, nx, nc = sizes
    pieces = {}
    along_x = {d: shift(own, sizes, 2, d) for d in range(1, nx)}
    along_y = {e: shift(own, sizes, 1, e) for e in range(1, ny)}
    pieces[0, 0, 0] = (own,)
    for d in range(1, nx):
        pieces[0, 0, d] = (along_x[d],)
    for e in range(1, ny):
        pieces[0, e, 0] = (along_y[e],)
    for d in range(1, nx):
        for e in range(1, ny):
            first = shift(along_x[d][..., :half], sizes, 1, e)
            second = shift(along_y[e][..., half:], sizes, 2, d)
            pieces[0, e, d] = (first, second)
    for (_, e, d), held in list(pieces.items()):
        for c in range(1, nc):
            pieces[c, e, d] = tuple(shift(part, sizes, 3, c) for part in held)
    return pieces


def place_kernel(keys, counts, sizes, me_ref, *refs):
    out_ref = refs[-1]
    at = 0
    half = out_ref.shape[-1] // 2
    for (c, e, d), count in zip(keys, counts):
        y = lax.rem(me_ref[1] - e + sizes[1], sizes[1])
        x = lax.rem(me_ref[2] - d + sizes[2], sizes[2])
        k = lax.rem(me_ref[3] - c + sizes[3], sizes[3])
        slot = (y * sizes[2] + x) * sizes[3] + k
        if count == 1:
            out_ref[0, slot] = refs[at][0]
        else:
            out_ref[0, slot, :, :half] = refs[at][0]
            out_ref[0, slot, :, half:] = refs[at + 1][0]
        at += count


def place(pieces, sizes, me):
    keys = sorted(pieces)
    counts = [len(pieces[key]) for key in keys]
    arrays = [part for key in keys for part in pieces[key]]
    rows, width = pieces[0, 0, 0][0].shape[1:]
    inner = sizes[1] * sizes[2] * sizes[3]
    nz = sizes[0]

    def source(z, me_ref):
        return (lax.rem(me_ref[0] - z + nz, nz), 0, 0)

    moved = 2 * nz * inner * rows * width * 2
    out = pl.pallas_call(
        functools.partial(place_kernel, keys, counts, sizes),
        out_shape=jax.ShapeDtypeStruct((nz, inner, rows, width), arrays[0].dtype),
        grid_spec=pltpu.PrefetchScalarGridSpec(
            num_scalar_prefetch=1,
            grid=(nz,),
            in_specs=[pl.BlockSpec((1,) + a.shape[1:], source) for a in arrays],
            out_specs=pl.BlockSpec((1, inner, rows, width), lambda z, me_ref: (z, 0, 0, 0)),
        ),
        cost_estimate=pl.CostEstimate(flops=0, transcendentals=0, bytes_accessed=moved),
        name="place",
    )(me, *arrays)
    return out.reshape(nz * inner * rows, width)


def take(values, axis, index):
    return lax.dynamic_index_in_dim(values, index, axis, keepdims=False)


def reduce_axis(values, sizes, axis, at, me, kind):
    size = sizes[axis]
    total = take(values, at, me[axis]).astype(f32)
    for step in range(1, size):
        target = lax.rem(me[axis] + step, size)
        got = shift(take(values, at, target), sizes, axis, step)
        total = total + got.astype(f32)
    return total.astype(kind)


def scatter_sum(values, sizes, me):
    count = math.prod(sizes)
    rows, width = values.shape[0] // count, values.shape[1]
    kind = values.dtype
    blocks = values.reshape(tuple(sizes) + (rows, width))
    summed = reduce_axis(blocks, sizes, 3, 3, me, kind)
    half = width // 2
    first, second = summed[..., :half], summed[..., half:]
    first = reduce_axis(first, sizes, 1, 1, me, kind)
    second = reduce_axis(second, sizes, 2, 2, me, kind)
    first = reduce_axis(first, sizes, 2, 1, me, kind)
    second = reduce_axis(second, sizes, 1, 1, me, kind)
    return reduce_axis(jnp.concatenate([first, second], -1), sizes, 0, 0, me, f32)


def dot_nn(a, b):
    return lax.dot_general(a, b, (((1,), (0,)), ((), ())), preferred_element_type=f32)


def dot_nt(a, b):
    return lax.dot_general(a, b, (((1,), (1,)), ((), ())), preferred_element_type=f32)


def dot_tn(a, b):
    return lax.dot_general(a, b, (((0,), (0,)), ((), ())), preferred_element_type=f32)


def normed_of(values):
    average = jnp.mean(values, -1, keepdims=True)
    centred = values - average
    inverse = lax.rsqrt(jnp.mean(centred * centred, -1, keepdims=True) + epsilon)
    return centred * inverse, inverse


def norm_back(incoming, normed, inverse, gain):
    scaled = incoming * gain
    inner = (
        scaled
        - jnp.mean(scaled, -1, keepdims=True)
        - normed * jnp.mean(scaled * normed, -1, keepdims=True)
    )
    return inner * inverse


def sum_rows(values):
    return jnp.sum(values, 0, keepdims=True)


def lane_halves(kind):
    lane = lax.broadcasted_iota(jnp.int32, (1, LANES), 1)
    low = jnp.where(lane < HEAD_DIM, 1.0, 0.0)
    return (low.astype(kind), (1.0 - low).astype(kind))


def turn(tile, cosine, sine):
    lane = lax.broadcasted_iota(jnp.int32, (1, LANES), 1)
    half_dim = HEAD_DIM // 2
    lower = (lane & half_dim) == 0
    other = jnp.where(
        lower, pltpu.roll(tile, LANES - half_dim, 1), pltpu.roll(tile, half_dim, 1)
    )
    return tile * cosine + other * sine


def rotary_tables():
    half_dim = HEAD_DIM // 2
    inverse = jnp.exp(
        jnp.arange(half_dim, dtype=f32) * (-2.0 * math.log(rope_base) / HEAD_DIM)
    )
    angles = jnp.arange(SEQ_LEN, dtype=f32)[:, None] * inverse[None, :]
    cosine, sine = jnp.cos(angles), jnp.sin(angles)
    return (
        jnp.concatenate([cosine] * 4, 1),
        jnp.concatenate([-sine, sine, -sine, sine], 1),
    )


def call(kernel, name, grid, ins, in_specs, outs, out_specs, flops, scratch=(), scalars=(), exps=0):
    arrays = jax.tree.leaves((ins, outs))
    nbytes = sum(math.prod(a.shape) * a.dtype.itemsize for a in arrays)
    return pl.pallas_call(
        kernel,
        out_shape=outs,
        grid_spec=pltpu.PrefetchScalarGridSpec(
            num_scalar_prefetch=len(scalars),
            grid=grid,
            in_specs=in_specs,
            out_specs=out_specs,
            scratch_shapes=scratch,
        ),
        compiler_params=pltpu.CompilerParams(
            dimension_semantics=("arbitrary",) * len(grid), vmem_limit_bytes=60 << 20
        ),
        cost_estimate=pl.CostEstimate(flops=flops, transcendentals=exps, bytes_accessed=nbytes),
        name=name,
    )(*scalars, *ins)


def like(shape, kind):
    return jax.ShapeDtypeStruct(shape, kind)


def whole(shape):
    return pl.BlockSpec(shape, lambda *_: (0,) * len(shape))


def qkv_kernel(x_ref, w_ref, vec_ref, cos_ref, sin_ref, a1_ref, out_ref):
    part = pl.program_id(0)
    rows = x_ref.shape[0]

    @pl.when(part == 0)
    def _():
        for r in range(0, rows, ROWS):
            normed, _ = normed_of(x_ref[r : r + ROWS].astype(f32))
            a1_ref[r : r + ROWS] = (normed * vec_ref[8:9] + vec_ref[11:12]).astype(bf16)

    bias = vec_ref[pl.ds(part, 1), :]
    for r in range(0, rows, ROWS):
        mixed = dot_nn(a1_ref[r : r + ROWS], w_ref[...]) + bias
        at = r % SEQ_LEN

        @pl.when(part < 2)
        def _():
            cosine, sine = cos_ref[at : at + ROWS], sin_ref[at : at + ROWS]
            for c in range(0, D, LANES):
                turned = turn(mixed[:, c : c + LANES], cosine, sine)
                out_ref[r : r + ROWS, c : c + LANES] = turned.astype(bf16)

        @pl.when(part == 2)
        def _():
            out_ref[r : r + ROWS] = mixed.astype(bf16)


def qkv_project(x, weight, vec, cosine, sine):
    rows = x.shape[0]
    return call(
        qkv_kernel,
        "qkv_project",
        (3,),
        (x, weight, vec, cosine, sine),
        [
            whole((rows, D)),
            pl.BlockSpec((D, D), lambda j: (0, j)),
            whole(vec.shape),
            whole((SEQ_LEN, LANES)),
            whole((SEQ_LEN, LANES)),
        ],
        (like((rows, D), bf16), like((rows, 3 * D), bf16)),
        (whole((rows, D)), pl.BlockSpec((rows, D), lambda j: (0, j))),
        2 * rows * D * 3 * D,
    )


def limits(lengths_ref, seq, positions):
    first = lengths_ref[seq, 0]
    second = first + lengths_ref[seq, 1]
    third = second + lengths_ref[seq, 2]
    tail = jnp.where(positions < third, third, SEQ_LEN)
    tail = jnp.where(positions < second, second, tail)
    return jnp.where(positions < first, first, tail)


def self_kernel(lengths_ref, q_ref, k_ref, v_ref, o_ref, lse_ref):
    seq = pl.program_id(0)
    keep = lane_halves(bf16)
    low_lane = lax.broadcasted_iota(jnp.int32, (1, LANES), 1) < HEAD_DIM
    for r in range(0, SEQ_LEN, ROWS):
        rows = lax.broadcasted_iota(jnp.int32, (ROWS, 1), 0) + r
        columns = lax.broadcasted_iota(jnp.int32, (ROWS, SEQ_LEN), 1)
        allowed = columns < limits(lengths_ref, seq, rows)
        query = q_ref[r : r + ROWS] * scale
        outs, totals = [], []
        for h in range(2):
            scores = dot_nt(query * keep[h], k_ref[...])
            scores = jnp.where(allowed, scores, -1e30)
            row_max = jnp.max(scores, -1, keepdims=True)
            exponent = jnp.exp(scores - row_max)
            total = jnp.sum(exponent, -1, keepdims=True)
            weights = (exponent * (1.0 / total)).astype(bf16)
            outs.append(dot_nn(weights, v_ref[...]))
            totals.append(row_max + jnp.log(total))
        o_ref[r : r + ROWS] = jnp.where(low_lane, outs[0], outs[1]).astype(bf16)
        lse_ref[r : r + ROWS] = jnp.where(low_lane, totals[0], totals[1])


def self_attend(lengths, qkv):
    rows = qkv.shape[0]
    seqs = rows // SEQ_LEN
    block = (SEQ_LEN, LANES)

    def at(offset):
        return pl.BlockSpec(block, lambda s, p, _: (s, offset + p))

    return call(
        self_kernel,
        "self_attend",
        (seqs, PAIRS),
        (qkv, qkv, qkv),
        [at(0), at(PAIRS), at(2 * PAIRS)],
        (like((rows, D), bf16), like((rows, D), f32)),
        (at(0), at(0)),
        4 * rows * SEQ_LEN * D,
        scalars=(lengths,),
        exps=rows * SEQ_LEN * HEADS,
    )


def self_back_kernel(lengths_ref, q_ref, k_ref, v_ref, do_ref, lse_ref, cos_ref, sin_ref, out_ref):
    seq, pair = pl.program_id(0), pl.program_id(1)
    keep = lane_halves(bf16)
    low_lane = lax.broadcasted_iota(jnp.int32, (1, LANES), 1) < HEAD_DIM
    lse = lse_ref[...].T
    positions = lax.broadcasted_iota(jnp.int32, (1, SEQ_LEN), 1)
    ends = limits(lengths_ref, seq, positions)
    key_at = lax.broadcasted_iota(jnp.int32, (SEQ_LEN, SEQ_LEN), 0)
    allowed = key_at < ends
    dqs, dks, dvs = [], [], []
    for h in range(2):
        total = lse[h * HEAD_DIM : h * HEAD_DIM + 1]
        scores = dot_nt(k_ref[...] * (keep[h] * scale), q_ref[...])
        prob = jnp.exp(jnp.where(allowed, scores - total, -1e30))
        dprob = dot_nt(v_ref[...] * keep[h], do_ref[...])
        inner = jnp.sum(prob * dprob, 0, keepdims=True)
        dscore = (prob * (dprob - inner)).astype(bf16)
        dvs.append(dot_nn(prob.astype(bf16), do_ref[...]))
        dks.append(dot_nn(dscore, q_ref[...]))
        dqs.append(dot_tn(dscore, k_ref[...]))
    cosine, sine = cos_ref[...], -sin_ref[...]
    dq = jnp.where(low_lane, dqs[0], dqs[1]) * scale
    dk = jnp.where(low_lane, dks[0], dks[1]) * scale
    dv = jnp.where(low_lane, dvs[0], dvs[1])
    for part, value in enumerate((turn(dq, cosine, sine), turn(dk, cosine, sine), dv)):
        column = pl.multiple_of((part * PAIRS + pair) * LANES, LANES)
        out_ref[:, pl.ds(column, LANES)] = value.astype(bf16)


def self_back(lengths, qkv, do, lse, cosine, sine):
    rows = qkv.shape[0]
    seqs = rows // SEQ_LEN
    block = (SEQ_LEN, LANES)

    def at(offset):
        return pl.BlockSpec(block, lambda s, p, _: (s, offset + p))

    return call(
        self_back_kernel,
        "self_back",
        (seqs, PAIRS),
        (qkv, qkv, qkv, do, lse, cosine, sine),
        [at(0), at(PAIRS), at(2 * PAIRS), at(0), at(0), whole(block), whole(block)],
        like((rows, 3 * D), bf16),
        pl.BlockSpec((SEQ_LEN, 3 * D), lambda s, p, _: (s, 0)),
        10 * rows * SEQ_LEN * D,
        scalars=(lengths,),
        exps=rows * SEQ_LEN * HEADS,
    )


def mid_kernel(o_ref, x_ref, wo_ref, wq_ref, vec_ref, h1_ref, a2_ref, cq_ref):
    h1 = x_ref[...].astype(f32) + dot_nn(o_ref[...], wo_ref[...]) + vec_ref[3:4]
    h1_ref[...] = h1
    normed, _ = normed_of(h1)
    a2 = (normed * vec_ref[9:10] + vec_ref[12:13]).astype(bf16)
    a2_ref[...] = a2
    cq_ref[...] = (dot_nn(a2, wq_ref[...]) + vec_ref[4:5]).astype(bf16)


def mid_forward(o, x, mid, vec):
    rows = x.shape[0]
    block = pl.BlockSpec((ROWS, D), lambda r: (r, 0))
    return call(
        mid_kernel,
        "mid_forward",
        (rows // ROWS,),
        (o, x, mid, mid, vec),
        [
            block,
            block,
            pl.BlockSpec((D, D), lambda r: (0, 2)),
            pl.BlockSpec((D, D), lambda r: (0, 3)),
            whole(vec.shape),
        ],
        (like((rows, D), f32), like((rows, D), bf16), like((rows, D), bf16)),
        (block, block, block),
        4 * rows * D * D,
    )


def ckv_kernel(n_ref, w_ref, vec_ref, out_ref):
    mixed = dot_nn(n_ref[...], w_ref[...])
    out_ref[:, :D] = mixed[:, :D].astype(bf16)
    out_ref[:, D:] = (mixed[:, D:] + vec_ref[5:6]).astype(bf16)


def ckv_project(n, mid, vec):
    rows = n.shape[0]
    return call(
        ckv_kernel,
        "ckv_project",
        (rows // ROWS,),
        (n, mid, vec),
        [
            pl.BlockSpec((ROWS, D), lambda r: (r, 0)),
            pl.BlockSpec((D, 2 * D), lambda r: (0, 0)),
            whole(vec.shape),
        ],
        like((rows, 2 * D), bf16),
        pl.BlockSpec((ROWS, 2 * D), lambda r: (r, 0)),
        4 * rows * D * D,
    )


def slots(chosen_ref, seq, span):
    found = []
    for i in range(K_NBR):
        entry = chosen_ref[seq, span * K_NBR + i]
        found.append(pl.multiple_of(entry * NBR_LEN, NBR_LEN))
    return found


def chosen_rows(ref, starts):
    return jnp.concatenate([ref[pl.ds(start, NBR_LEN), :] for start in starts], 0)


def cross_kernel(chosen_ref, q_ref, k_ref, v_ref, o_ref):
    seq = pl.program_id(0)
    keep = lane_halves(bf16)
    low_lane = lax.broadcasted_iota(jnp.int32, (1, LANES), 1) < HEAD_DIM
    for c in range(SPANS):
        starts = slots(chosen_ref, seq, c)
        query = q_ref[c * SPAN : (c + 1) * SPAN] * scale
        both = jnp.concatenate([query * keep[0], query * keep[1]], 0)
        scores = dot_nt(both, chosen_rows(k_ref, starts))
        exponent = jnp.exp(scores - jnp.max(scores, -1, keepdims=True))
        total = jnp.sum(exponent, -1, keepdims=True)
        weights = (exponent * (1.0 / total)).astype(bf16)
        out = dot_nn(weights, chosen_rows(v_ref, starts))
        o_ref[c * SPAN : (c + 1) * SPAN] = jnp.where(low_lane, out[:SPAN], out[SPAN:]).astype(bf16)


def cross_attend(chosen, cq, ckv):
    rows = cq.shape[0]
    seqs = rows // SEQ_LEN
    block = (SEQ_LEN, LANES)

    def at(offset):
        return pl.BlockSpec(block, lambda s, p, _: (s, offset + p))

    return call(
        cross_kernel,
        "cross_attend",
        (seqs, PAIRS),
        (cq, ckv, ckv),
        [at(0), at(0), at(PAIRS)],
        like((rows, D), bf16),
        at(0),
        2 * rows * SEQ_LEN * D,
        scalars=(chosen,),
        exps=rows * K_NBR * NBR_LEN * HEADS,
    )


def cross_back_kernel(chosen_ref, q_ref, k_ref, v_ref, do_ref, dq_ref, dkv_ref, dk_acc, dv_acc):
    seq, pair = pl.program_id(0), pl.program_id(1)
    keep = lane_halves(bf16)
    low_lane = lax.broadcasted_iota(jnp.int32, (1, LANES), 1) < HEAD_DIM
    dk_acc[...] = jnp.zeros_like(dk_acc)
    dv_acc[...] = jnp.zeros_like(dv_acc)
    for c in range(SPANS):
        starts = slots(chosen_ref, seq, c)
        span = slice(c * SPAN, (c + 1) * SPAN)
        query, upstream = q_ref[span], do_ref[span]
        query = jnp.concatenate([query * keep[0], query * keep[1]], 0)
        upstream = jnp.concatenate([upstream * keep[0], upstream * keep[1]], 0)
        keys, values = chosen_rows(k_ref, starts), chosen_rows(v_ref, starts)
        scores = dot_nt(keys, query) * scale
        exponent = jnp.exp(scores - jnp.max(scores, 0, keepdims=True))
        prob = exponent * (1.0 / jnp.sum(exponent, 0, keepdims=True))
        dprob = dot_nt(values, upstream)
        inner = jnp.sum(prob * dprob, 0, keepdims=True)
        dscore = (prob * (dprob - inner)).astype(bf16)
        dv = dot_nn(prob.astype(bf16), upstream)
        dk = dot_nn(dscore, query) * scale
        dq = dot_tn(dscore, keys) * scale
        dq_ref[span] = jnp.where(low_lane, dq[:SPAN], dq[SPAN:]).astype(bf16)
        for i, start in enumerate(starts):
            rows = slice(i * NBR_LEN, (i + 1) * NBR_LEN)
            dk_acc[pl.ds(start, NBR_LEN), :] += dk[rows]
            dv_acc[pl.ds(start, NBR_LEN), :] += dv[rows]
    for part, acc in enumerate((dk_acc, dv_acc)):
        column = pl.multiple_of((part * PAIRS + pair) * LANES, LANES)
        dkv_ref[:, pl.ds(column, LANES)] = acc[...].astype(bf16)


def cross_back(chosen, cq, ckv, dco):
    rows = cq.shape[0]
    seqs = rows // SEQ_LEN
    block = (SEQ_LEN, LANES)

    def at(offset):
        return pl.BlockSpec(block, lambda s, p, _: (s, offset + p))

    return call(
        cross_back_kernel,
        "cross_back",
        (seqs, PAIRS),
        (cq, ckv, ckv, dco),
        [at(0), at(0), at(PAIRS), at(0)],
        (like((rows, D), bf16), like((rows, 2 * D), bf16)),
        (at(0), pl.BlockSpec((SEQ_LEN, 2 * D), lambda s, p, _: (s, 0))),
        5 * rows * SEQ_LEN * D,
        scratch=[pltpu.VMEM(block, f32), pltpu.VMEM(block, f32)],
        scalars=(chosen,),
        exps=rows * K_NBR * NBR_LEN * HEADS,
    )


def gelu_pair(hidden):
    root_coeff = math.sqrt(2.0 / math.pi)
    square = hidden * hidden
    tangent = jnp.tanh(root_coeff * hidden * (1.0 + gelu_coeff * square))
    upper = 0.5 * (1.0 + tangent)
    slope = upper + (0.5 * root_coeff) * hidden * (1.0 - tangent * tangent) * (
        1.0 + (3.0 * gelu_coeff) * square
    )
    return hidden * upper, slope


def mlp_kernel(
    h1_ref,
    co_ref,
    dy_ref,
    wco_ref,
    wu_ref,
    wd_ref,
    bu_ref,
    vec_ref,
    a3_ref,
    g_ref,
    du_ref,
    out_ref,
    dh2_ref,
    e2_ref,
    dco_ref,
    sums_ref,
    dbu_ref,
    y_acc,
    da_acc,
    h2_ref,
):
    step = pl.program_id(0)
    rows = h1_ref.shape[0]
    chunks = range(0, rows, ROWS)

    @pl.when(step == 0)
    def _():
        for r in chunks:
            part = slice(r, r + ROWS)
            h2 = h1_ref[part] + dot_nn(co_ref[part], wco_ref[...]) + vec_ref[6:7]
            h2_ref[part] = h2
            normed, _ = normed_of(h2)
            a3_ref[part] = (normed * vec_ref[10:11] + vec_ref[13:14]).astype(bf16)
            y_acc[part] = h2 + vec_ref[7:8]
            da_acc[part] = jnp.zeros_like(h2)

    bias_sum = jnp.zeros((1, TILE_F), f32)
    for r in chunks:
        part = slice(r, r + ROWS)
        hidden = dot_nn(a3_ref[part], wu_ref[...]) + bu_ref[...]
        dg = dot_nt(dy_ref[part], wd_ref[...])
        value, slope = gelu_pair(hidden)
        g = value.astype(bf16)
        du = (dg * slope).astype(bf16)
        g_ref[part] = g
        du_ref[part] = du
        bias_sum += sum_rows(du.astype(f32))
        y_acc[part] += dot_nn(g, wd_ref[...])
        da_acc[part] += dot_nt(du, wu_ref[...])
    dbu_ref[...] = bias_sum

    @pl.when(step == pl.num_programs(0) - 1)
    def _():
        gain_sum = jnp.zeros((1, D), f32)
        shift_sum = jnp.zeros((1, D), f32)
        e_sum = jnp.zeros((1, D), f32)
        y_sum = jnp.zeros((1, D), f32)
        for r in chunks:
            part = slice(r, r + ROWS)
            out_ref[part] = y_acc[part].astype(bf16)
            normed, inverse = normed_of(h2_ref[part])
            da3 = da_acc[part]
            upstream = dy_ref[part].astype(f32)
            dh2 = upstream + norm_back(da3, normed, inverse, vec_ref[10:11])
            dh2_ref[part] = dh2
            e2 = dh2.astype(bf16)
            e2_ref[part] = e2
            dco_ref[part] = dot_nt(e2, wco_ref[...]).astype(bf16)
            gain_sum += sum_rows(da3 * normed)
            shift_sum += sum_rows(da3)
            e_sum += sum_rows(e2.astype(f32))
            y_sum += sum_rows(upstream)
        sums_ref[0:1] = gain_sum
        sums_ref[1:2] = shift_sum
        sums_ref[2:3] = e_sum
        sums_ref[3:4] = y_sum


def mlp_both(h1, co, dy, mid, wu, wd, bu, vec):
    rows = h1.shape[0]
    full = whole((rows, D))
    wide = pl.BlockSpec((rows, TILE_F), lambda f: (0, f))
    return call(
        mlp_kernel,
        "mlp_both",
        (FF // TILE_F,),
        (h1, co, dy, mid, wu, wd, bu, vec),
        [
            full,
            full,
            full,
            pl.BlockSpec((D, D), lambda f: (0, 4)),
            pl.BlockSpec((D, TILE_F), lambda f: (0, f)),
            pl.BlockSpec((TILE_F, D), lambda f: (f, 0)),
            pl.BlockSpec((1, TILE_F), lambda f: (0, f)),
            whole(vec.shape),
        ],
        (
            like((rows, D), bf16),
            like((rows, FF), bf16),
            like((rows, FF), bf16),
            like((rows, D), bf16),
            like((rows, D), f32),
            like((rows, D), bf16),
            like((rows, D), bf16),
            like((8, D), f32),
            like((1, FF), f32),
        ),
        (
            full,
            wide,
            wide,
            full,
            full,
            full,
            full,
            whole((8, D)),
            pl.BlockSpec((1, TILE_F), lambda f: (0, f)),
        ),
        2 * rows * D * (4 * FF + 2 * D),
        scratch=[pltpu.VMEM((rows, D), f32)] * 3,
        exps=rows * FF,
    )


def mid_back_kernel(
    dcq_ref, dh2_ref, h1_ref, wq_ref, wo_ref, vec_ref, dh1_ref, e1_ref, do_ref, sums_ref
):
    @pl.when(pl.program_id(0) == 0)
    def _():
        sums_ref[...] = jnp.zeros_like(sums_ref)

    da2 = dot_nt(dcq_ref[...], wq_ref[...])
    normed, inverse = normed_of(h1_ref[...])
    dh1 = dh2_ref[...] + norm_back(da2, normed, inverse, vec_ref[9:10])
    dh1_ref[...] = dh1
    e1 = dh1.astype(bf16)
    e1_ref[...] = e1
    do_ref[...] = dot_nt(e1, wo_ref[...]).astype(bf16)
    sums_ref[0:1] += sum_rows(da2 * normed)
    sums_ref[1:2] += sum_rows(da2)
    sums_ref[2:3] += sum_rows(dcq_ref[...].astype(f32))
    sums_ref[3:4] += sum_rows(e1.astype(f32))


def mid_back(dcq, dh2, h1, mid, vec):
    rows = h1.shape[0]
    block = pl.BlockSpec((ROWS, D), lambda r: (r, 0))
    return call(
        mid_back_kernel,
        "mid_back",
        (rows // ROWS,),
        (dcq, dh2, h1, mid, mid, vec),
        [
            block,
            block,
            block,
            pl.BlockSpec((D, D), lambda r: (0, 3)),
            pl.BlockSpec((D, D), lambda r: (0, 2)),
            whole(vec.shape),
        ],
        (
            like((rows, D), f32),
            like((rows, D), bf16),
            like((rows, D), bf16),
            like((8, D), f32),
        ),
        (block, block, block, whole((8, D))),
        4 * rows * D * D,
    )


def token_back_kernel(dqkv_ref, dh1_ref, x_ref, w_ref, vec_ref, dx_ref, sums_ref, qkv_sums_ref):
    @pl.when(pl.program_id(0) == 0)
    def _():
        sums_ref[...] = jnp.zeros_like(sums_ref)
        qkv_sums_ref[...] = jnp.zeros_like(qkv_sums_ref)

    da1 = dot_nt(dqkv_ref[...], w_ref[...])
    normed, inverse = normed_of(x_ref[...].astype(f32))
    dx_ref[...] = dh1_ref[...] + norm_back(da1, normed, inverse, vec_ref[8:9])
    sums_ref[0:1] += sum_rows(da1 * normed)
    sums_ref[1:2] += sum_rows(da1)
    qkv_sums_ref[...] += sum_rows(dqkv_ref[...].astype(f32))


def token_back(dqkv, dh1, x, weight, vec):
    rows = x.shape[0]
    block = pl.BlockSpec((ROWS, D), lambda r: (r, 0))
    return call(
        token_back_kernel,
        "token_back",
        (rows // ROWS,),
        (dqkv, dh1, x, weight, vec),
        [
            pl.BlockSpec((ROWS, 3 * D), lambda r: (r, 0)),
            block,
            block,
            pl.BlockSpec((D, 3 * D), lambda r: (0, 0)),
            whole(vec.shape),
        ],
        (like((rows, D), f32), like((8, D), f32), like((1, 3 * D), f32)),
        (block, whole((8, D)), whole((1, 3 * D))),
        6 * rows * D * D,
    )


def neighbour_kernel(dkv_ref, w_ref, dn_ref, sums_ref):
    @pl.when(pl.program_id(0) == 0)
    def _():
        sums_ref[...] = jnp.zeros_like(sums_ref)

    dn_ref[...] = dot_nt(dkv_ref[...], w_ref[...])
    sums_ref[...] += sum_rows(dkv_ref[:, D:].astype(f32))


def neighbour_back(dckv, mid):
    rows = dckv.shape[0]
    return call(
        neighbour_kernel,
        "neighbour_back",
        (rows // ROWS,),
        (dckv, mid),
        [
            pl.BlockSpec((ROWS, 2 * D), lambda r: (r, 0)),
            pl.BlockSpec((D, 2 * D), lambda r: (0, 0)),
        ],
        (like((rows, D), f32), like((1, D), f32)),
        (pl.BlockSpec((ROWS, D), lambda r: (r, 0)), whole((1, D))),
        4 * rows * D * D,
    )


def weight_grad(left, right):
    return dot_tn(left, right).astype(bf16)


def local(
    sizes,
    tokens,
    neighbours,
    block_lengths,
    chosen,
    cotangent,
    w_qkv,
    w_out,
    w_cross_q,
    w_cross_kv,
    w_cross_out,
    w_up,
    w_down,
    biases,
    up_bias,
    norm_gains,
    norm_shifts,
):
    me = coords_of(lax.axis_index("fsdp"), sizes)
    me_array = jnp.stack(me).astype(jnp.int32)
    shard = w_qkv.shape[0]
    small = jnp.concatenate(
        [biases.T, norm_gains.T, norm_shifts.T, up_bias.reshape(shard, FF // D)], 1
    )
    small = jnp.pad(small, ((0, 0), (0, LANES - SMALL)))
    first = jnp.concatenate([w_qkv, small], 1)
    middle = jnp.concatenate([w_cross_kv, w_out, w_cross_q, w_cross_out], 1)

    first_z = gather_z(first, sizes)
    middle_z = gather_z(after(middle, first_z), sizes)
    first_pieces = gather_rest(first_z, sizes)
    up_z = gather_z(after(w_up, middle_z), sizes)
    middle_pieces = gather_rest(middle_z, sizes)
    down_z = gather_z(after(w_down, up_z), sizes)
    up_pieces = gather_rest(up_z, sizes)
    down_pieces = gather_rest(down_z, sizes)

    cosine, sine = rotary_tables()
    qkv_weight = place(first_pieces, sizes, me_array)
    gathered = qkv_weight[:, 3 * D :]
    vec = gathered[:, :16].T.astype(f32)
    up_shift = gathered[:, 14:SMALL].reshape(1, FF).astype(f32)
    picks = chosen.reshape(chosen.shape[0], SPANS * K_NBR)

    a1, qkv = qkv_project(tokens, qkv_weight, vec, cosine, sine)
    o, lse = self_attend(block_lengths, qkv)
    mid = place(middle_pieces, sizes, me_array)
    ckv = ckv_project(neighbours, mid, vec)
    h1, a2, cq = mid_forward(o, tokens, mid, vec)
    co = cross_attend(picks, cq, ckv)
    up_weight = place(up_pieces, sizes, me_array)
    down_weight = place(down_pieces, sizes, me_array)
    a3, g, du, output, dh2, e2, dco, sums3, grad_bu = mlp_both(
        h1, co, cotangent, mid, up_weight, down_weight, up_shift, vec
    )
    grad_down = scatter_sum(weight_grad(g, cotangent), sizes, me)
    grad_up = scatter_sum(weight_grad(a3, du), sizes, me)
    grad_co = scatter_sum(weight_grad(co, e2), sizes, me)
    dcq, dckv = cross_back(picks, cq, ckv, dco)
    dh1, e1, do, sums2 = mid_back(dcq, dh2, h1, mid, vec)
    grad_cq = scatter_sum(weight_grad(a2, dcq), sizes, me)
    grad_ckv = scatter_sum(weight_grad(neighbours, dckv), sizes, me)
    grad_out = scatter_sum(weight_grad(o, e1), sizes, me)
    dqkv = self_back(block_lengths, qkv, do, lse, cosine, sine)
    grad_qkv = scatter_sum(weight_grad(a1, dqkv), sizes, me)
    token_grad, sums1, qkv_sums = token_back(dqkv, dh1, tokens, qkv_weight, vec)
    neighbour_grad, value_sums = neighbour_back(dckv, mid)

    rows = jnp.concatenate(
        [
            qkv_sums.reshape(3, D),
            sums2[3:4],
            sums2[2:3],
            value_sums,
            sums3[2:4],
            sums1[0:1],
            sums2[0:1],
            sums3[0:1],
            sums1[1:2],
            sums2[1:2],
            sums3[1:2],
        ],
        0,
    )
    spread = jnp.concatenate([rows.T, grad_bu.reshape(D, FF // D)], 1)
    spread = jnp.pad(spread, ((0, 0), (0, 2 * LANES - SMALL)))
    small_sum = scatter_sum(spread, sizes, me)
    return (
        output,
        token_grad,
        neighbour_grad,
        grad_qkv,
        grad_out,
        grad_cq,
        grad_ckv,
        grad_co,
        grad_up,
        grad_down,
        small_sum[:, :8].T,
        small_sum[:, 14:SMALL].reshape(-1),
        small_sum[:, 8:11].T,
        small_sum[:, 11:14].T,
    )


def solution(mesh):
    rowwise, columnwise = P("fsdp", None), P(None, "fsdp")
    return jax.shard_map(
        functools.partial(local, geometry(mesh.shape["fsdp"])),
        mesh=mesh,
        in_specs=(rowwise,) * 3
        + (P("fsdp", None, None),)
        + (rowwise,) * 8
        + (columnwise, P("fsdp"), columnwise, columnwise),
        out_specs=(rowwise,) * 10 + (columnwise, P("fsdp"), columnwise, columnwise),
        check_vma=False,
    )
```

```python
import functools
import math

import jax
import jax.numpy as jnp
from jax import lax
from jax.experimental import pallas as pl
from jax.experimental.pallas import tpu as pltpu
from jax.sharding import PartitionSpec as P

D = 768
HEADS = 12
HEAD_DIM = 64
FF = 3072
SEQ_LEN = 512
SPAN = 64
SPANS = 8
NBR_LEN = 128
K_NBR = 2
POOL = 4
PAIRS = HEADS // 2
LANES = 128
ROWS = 256
SMALL = 18
TILE_F = 512
QKV_TILE = 384
WIDE = 3

epsilon = 1e-05
rope_base = 10000.0
gelu_coeff = 0.044715
scale = HEAD_DIM ** (-0.5)
f32 = jnp.float32
bf16 = jnp.bfloat16


def geometry(count):
    side = round((count / 4) ** (1 / 3))
    sizes = (2 * side, side, side, 2)
    assert math.prod(sizes) == count
    return sizes


def coords_of(index, sizes):
    found = []
    for size in reversed(sizes):
        found.append(index % size)
        index = index // size
    return tuple(reversed(found))


def index_of(coords, sizes):
    index = 0
    for coord, size in zip(coords, sizes):
        index = index * size + coord
    return index


def shift_pairs(sizes, axis, step):
    pairs = []
    for source in range(math.prod(sizes)):
        coords = list(coords_of(source, sizes))
        coords[axis] = (coords[axis] + step) % sizes[axis]
        pairs.append((source, index_of(coords, sizes)))
    return pairs


def shift(values, sizes, axis, step):
    return lax.ppermute(values, "fsdp", shift_pairs(sizes, axis, step))


def after(values, *anchors):
    return lax.optimization_barrier((values, anchors))[0]


def gather_z(block, sizes):
    return jnp.stack([block] + [shift(block, sizes, 0, d) for d in range(1, sizes[0])])


def gather_side(own, sizes):
    along_x = {d: shift(own, sizes, 2, d) for d in range(1, sizes[2])}
    along_y = {e: shift(own, sizes, 1, e) for e in range(1, sizes[1])}
    return along_x, along_y


def gather_corner(side, sizes):
    along_x, along_y = side
    corner = {}
    for d, first in along_x.items():
        for e, second in along_y.items():
            half = first.shape[-1] // 2
            corner[e, d] = (
                shift(first[..., :half], sizes, 1, e),
                shift(second[..., half:], sizes, 2, d),
            )
    return corner


def gather_core(pieces, sizes):
    return {
        (c,) + key: tuple(shift(part, sizes, 3, c) for part in held)
        for key, held in pieces.items()
        for c in range(1, sizes[3])
    }


def near_pieces(own, side):
    pieces = {(0, 0): (own,)}
    pieces.update({(0, d): (part,) for d, part in side[0].items()})
    pieces.update({(e, 0): (part,) for e, part in side[1].items()})
    return pieces


def place_kernel(keys, counts, sizes, split, me_ref, *refs):
    outs = refs[sum(counts) :]
    at = 0
    for (c, e, d), count in zip(keys, counts):
        y = lax.rem(me_ref[1] - e + sizes[1], sizes[1])
        x = lax.rem(me_ref[2] - d + sizes[2], sizes[2])
        k = lax.rem(me_ref[3] - c + sizes[3], sizes[3])
        slot = (y * sizes[2] + x) * sizes[3] + k
        held = refs[at : at + count]
        rows, width = held[0].shape[1:]
        width = width * count
        half = width // 2
        if split:
            low, high = held if count == 2 else (held[0], held[0])
            for m in range(FF // D):
                outs[0][0, slot, m * rows : (m + 1) * rows] = low[0, :, m * D : (m + 1) * D]
            outs[1][0, slot] = high[0, :, 0 if count == 2 else half :]
        elif count == 1:
            outs[0][0, slot] = held[0][0]
        else:
            outs[0][0, slot, :, :half] = held[0][0]
            outs[0][0, slot, :, half:] = held[1][0]
        at += count


def place(pieces, sizes, me, split=False):
    keys = sorted(pieces)
    counts = [len(pieces[key]) for key in keys]
    arrays = [part for key in keys for part in pieces[key]]
    rows, width = pieces[0, 0, 0][0].shape[1:]
    nz = sizes[0]
    inner = sizes[1] * sizes[2] * sizes[3]
    shapes = [(rows * (FF // D), D), (rows, FF)] if split else [(rows, width)]

    def source(z, me_ref):
        return (lax.rem(me_ref[0] - z + nz, nz), 0, 0)

    moved = 2 * nz * inner * rows * width * 2
    outs = pl.pallas_call(
        functools.partial(place_kernel, keys, counts, sizes, split),
        out_shape=[like((nz, inner) + shape, bf16) for shape in shapes],
        grid_spec=pltpu.PrefetchScalarGridSpec(
            num_scalar_prefetch=1,
            grid=(nz,),
            in_specs=[pl.BlockSpec((1,) + a.shape[1:], source) for a in arrays],
            out_specs=[
                pl.BlockSpec((1, inner) + shape, lambda z, me_ref: (z, 0, 0, 0)) for shape in shapes
            ],
        ),
        cost_estimate=pl.CostEstimate(flops=0, transcendentals=0, bytes_accessed=moved),
        name="place",
    )(me, *arrays)
    outs = [out.reshape(nz * inner * out.shape[2], out.shape[3]) for out in outs]
    return outs if split else outs[0]


def spread_kernel(sizes, split, me_ref, *refs):
    keep_ref, send_ref = refs[-2:]
    ny, nx, nc = sizes[1:]
    for ry in range(ny):
        for rx in range(nx):
            y, x = lax.rem(me_ref[1] + ry, ny), lax.rem(me_ref[2] + rx, nx)
            base = (y * nx + x) * nc
            for out_ref, core in ((keep_ref, me_ref[3]), (send_ref, 1 - me_ref[3])):
                column = 0
                rows = out_ref.shape[3]
                for at, ref in enumerate(refs[:-2]):
                    width = ref.shape[3]
                    if split and at == 0:
                        for m in range(FF // D):
                            part = ref[0, base + core, m * rows : (m + 1) * rows]
                            out_ref[0, ry, rx, :, column + m * D : column + (m + 1) * D] = part
                        column += FF
                    else:
                        out_ref[0, ry, rx, :, column : column + width] = ref[0, base + core]
                        column += width


def spread(grads, sizes, me, split=False):
    nz, ny, nx, nc = sizes
    inner = ny * nx * nc
    rows = D // math.prod(sizes)
    blocks = [g.reshape(nz, inner, g.shape[0] // (nz * inner), g.shape[1]) for g in grads]
    width = sum(b.shape[2] * b.shape[3] for b in blocks) // rows
    kind = grads[0].dtype
    shape = like((nz, ny, nx, rows, width), kind)
    block = pl.BlockSpec((1, ny, nx, rows, width), lambda z, me_ref: (z, 0, 0, 0, 0))

    def source(z, me_ref):
        return (lax.rem(me_ref[0] + z, nz), 0, 0, 0)

    moved = 2 * D * width * kind.itemsize
    return pl.pallas_call(
        functools.partial(spread_kernel, sizes, split),
        out_shape=[shape, shape],
        grid_spec=pltpu.PrefetchScalarGridSpec(
            num_scalar_prefetch=1,
            grid=(nz,),
            in_specs=[pl.BlockSpec((1,) + b.shape[1:], source) for b in blocks],
            out_specs=[block, block],
        ),
        cost_estimate=pl.CostEstimate(flops=0, transcendentals=0, bytes_accessed=moved),
        name="spread",
    )(me, *blocks)


def plus(first, *others):
    total = first.astype(f32)
    for other in others:
        total = total + other.astype(f32)
    return total


def fold_core(kept, got, sizes):
    half = kept.shape[-1] // 2
    kind = kept.dtype

    def part(*index):
        return plus(kept[index], got[index]).astype(kind)

    every = slice(None)
    low, high = slice(None, half), slice(half, None)
    first = [part(every, e, every, every, low) for e in range(sizes[1])]
    second = [part(every, every, d, every, high) for d in range(sizes[2])]
    return first, second


def send_side(parts, sizes):
    first, second = parts
    return (
        [first[0]] + [shift(first[e], sizes, 1, e) for e in range(1, sizes[1])],
        [second[0]] + [shift(second[d], sizes, 2, d) for d in range(1, sizes[2])],
    )


def fold_side(got, sizes):
    kind = got[0][0].dtype
    first = [plus(*[g[:, d] for g in got[0]]).astype(kind) for d in range(sizes[2])]
    second = [plus(*[g[:, e] for g in got[1]]).astype(kind) for e in range(sizes[1])]
    return first, second


def send_corner(parts, sizes):
    first, second = parts
    return (
        [first[0]] + [shift(first[d], sizes, 2, d) for d in range(1, sizes[2])],
        [second[0]] + [shift(second[e], sizes, 1, e) for e in range(1, sizes[1])],
    )


def fold_corner(got, sizes):
    kind = got[0][0].dtype
    return [
        jnp.concatenate([plus(*[g[z] for g in half]).astype(kind) for half in got], -1)
        for z in range(sizes[0])
    ]


def send_z(parts, sizes):
    return [parts[0]] + [shift(parts[z], sizes, 0, z) for z in range(1, sizes[0])]


def scatter_small(kept, sent, sizes):
    total = plus(kept, shift(sent, sizes, 3, 1))
    for axis, at in ((1, 1), (2, 1), (0, 0)):
        parts = [lax.index_in_dim(total, step, at, keepdims=False) for step in range(sizes[axis])]
        total = plus(*[parts[0]] + [shift(p, sizes, axis, k) for k, p in enumerate(parts) if k])
    return total


def dot_nn(a, b):
    return lax.dot_general(a, b, (((1,), (0,)), ((), ())), preferred_element_type=f32)


def dot_nt(a, b):
    return lax.dot_general(a, b, (((1,), (1,)), ((), ())), preferred_element_type=f32)


def dot_tn(a, b):
    return lax.dot_general(a, b, (((0,), (0,)), ((), ())), preferred_element_type=f32)


def normed_of(values):
    average = jnp.mean(values, -1, keepdims=True)
    centred = values - average
    inverse = lax.rsqrt(jnp.mean(centred * centred, -1, keepdims=True) + epsilon)
    return centred * inverse, inverse


def norm_back(incoming, normed, inverse, gain):
    scaled = incoming * gain
    inner = (
        scaled
        - jnp.mean(scaled, -1, keepdims=True)
        - normed * jnp.mean(scaled * normed, -1, keepdims=True)
    )
    return inner * inverse


def sum_rows(values):
    return jnp.sum(values, 0, keepdims=True)


def lane_halves(kind):
    lane = lax.broadcasted_iota(jnp.int32, (1, LANES), 1)
    low = jnp.where(lane < HEAD_DIM, 1.0, 0.0)
    return (low.astype(kind), (1.0 - low).astype(kind))


def turn(tile, cosine, sine):
    lane = lax.broadcasted_iota(jnp.int32, (1, LANES), 1)
    half_dim = HEAD_DIM // 2
    lower = (lane & half_dim) == 0
    other = jnp.where(
        lower, pltpu.roll(tile, LANES - half_dim, 1), pltpu.roll(tile, half_dim, 1)
    )
    return tile * cosine + other * sine


def rotary_tables():
    half_dim = HEAD_DIM // 2
    inverse = jnp.exp(
        jnp.arange(half_dim, dtype=f32) * (-2.0 * math.log(rope_base) / HEAD_DIM)
    )
    angles = jnp.arange(SEQ_LEN, dtype=f32)[:, None] * inverse[None, :]
    cosine, sine = jnp.cos(angles), jnp.sin(angles)
    return (
        jnp.concatenate([cosine] * 4, 1),
        jnp.concatenate([-sine, sine, -sine, sine], 1),
    )


def call(
    kernel,
    name,
    grid,
    ins,
    in_specs,
    outs,
    out_specs,
    flops,
    scratch=(),
    scalars=(),
    exps=0,
    aliases={},
):
    arrays = jax.tree.leaves((ins, outs))
    nbytes = sum(math.prod(a.shape) * a.dtype.itemsize for a in arrays)
    return pl.pallas_call(
        kernel,
        out_shape=outs,
        grid_spec=pltpu.PrefetchScalarGridSpec(
            num_scalar_prefetch=len(scalars),
            grid=grid,
            in_specs=in_specs,
            out_specs=out_specs,
            scratch_shapes=scratch,
        ),
        compiler_params=pltpu.CompilerParams(
            dimension_semantics=("arbitrary",) * len(grid), vmem_limit_bytes=60 << 20
        ),
        input_output_aliases=aliases,
        cost_estimate=pl.CostEstimate(flops=flops, transcendentals=exps, bytes_accessed=nbytes),
        name=name,
    )(*scalars, *ins)


def like(shape, kind):
    return jax.ShapeDtypeStruct(shape, kind)


def whole(shape):
    return pl.BlockSpec(shape, lambda *_: (0,) * len(shape))


def qkv_kernel(x_ref, w_ref, vec_ref, cos_ref, sin_ref, a1_ref, out_ref):
    part = pl.program_id(0)
    rows = x_ref.shape[0]
    width = w_ref.shape[1]

    @pl.when(part == 0)
    def _():
        for r in range(0, rows, ROWS):
            normed, _ = normed_of(x_ref[r : r + ROWS].astype(f32))
            a1_ref[r : r + ROWS] = (normed * vec_ref[8:9, :D] + vec_ref[11:12, :D]).astype(bf16)

    column = pl.multiple_of(lax.rem(part, D // width) * width, width)
    bias = vec_ref[pl.ds(part // (D // width), 1), pl.ds(column, width)]
    for r in range(0, rows, ROWS):
        mixed = dot_nn(a1_ref[r : r + ROWS], w_ref[...]) + bias
        at = r % SEQ_LEN
        cosine, sine = cos_ref[0, at : at + ROWS], sin_ref[0, at : at + ROWS]
        for c in range(0, width, LANES):
            turned = turn(mixed[:, c : c + LANES], cosine, sine)
            out_ref[r : r + ROWS, c : c + LANES] = turned.astype(bf16)


def qkv_project(x, weight, vec, cosine, sine):
    rows = x.shape[0]
    width = QKV_TILE
    tables = (
        jnp.stack([cosine, jnp.ones_like(cosine)]),
        jnp.stack([sine, jnp.zeros_like(sine)]),
    )
    table = pl.BlockSpec((1, SEQ_LEN, LANES), lambda j: (j // (2 * D // width), 0, 0))
    return call(
        qkv_kernel,
        "qkv_project",
        (3 * D // width,),
        (x, weight, vec) + tables,
        [
            whole((rows, D)),
            pl.BlockSpec((D, width), lambda j: (0, j)),
            whole(vec.shape),
            table,
            table,
        ],
        (like((rows, D), bf16), like((rows, 3 * D), bf16)),
        (whole((rows, D)), pl.BlockSpec((rows, width), lambda j: (0, j))),
        2 * rows * D * 3 * D,
    )


def blocks_of(lengths_ref, seq, positions):
    end, found = 0, jnp.zeros(positions.shape, jnp.int32)
    for i in range(3):
        end = end + lengths_ref[seq, i]
        found = found + (positions >= end).astype(jnp.int32)
    return found


def mask_features(lengths_ref, seq):
    rows = lax.broadcasted_iota(jnp.int32, (SEQ_LEN, LANES), 0)
    slot = lax.broadcasted_iota(jnp.int32, (SEQ_LEN, LANES), 1) & (HEAD_DIM - 1)
    block = blocks_of(lengths_ref, seq, rows)
    later = (slot > block) & (slot < 4)
    return (
        jnp.where(later, -1e30, 0.0).astype(bf16),
        jnp.where(slot == block, 1.0, 0.0).astype(bf16),
    )


def self_kernel(lengths_ref, q_ref, k_ref, v_ref, o_ref, lse_ref, fq_ref, fk_ref):
    seq = pl.program_id(0)

    @pl.when(pl.program_id(1) == 0)
    def _():
        fq_ref[...], fk_ref[...] = mask_features(lengths_ref, seq)

    keep = lane_halves(bf16)
    low_lane = lax.broadcasted_iota(jnp.int32, (1, LANES), 1) < HEAD_DIM
    ones = jnp.ones((SEQ_LEN, LANES), bf16)
    starts = range(0, SEQ_LEN, ROWS)
    for c in range(0, q_ref.shape[1], LANES):
        lanes = slice(c, c + LANES)
        query, key = q_ref[:, lanes] * scale, k_ref[:, lanes]
        queries = [query * keep[h] + fq_ref[...] * keep[1 - h] for h in range(2)]
        keys = [key * keep[h] + fk_ref[...] * keep[1 - h] for h in range(2)]
        value = jnp.concatenate([v_ref[:, lanes], ones], 1)
        parts = [(r, h) for r in starts for h in range(2)]
        scores = [dot_nt(queries[h][r : r + ROWS], keys[h]) for r, h in parts]
        tops = [jnp.max(s, -1, keepdims=True) for s in scores]
        weights = [jnp.exp(s - top).astype(bf16) for s, top in zip(scores, tops)]
        outs = [dot_nn(w, value) for w in weights]
        for i, r in enumerate(starts):
            first, second = outs[2 * i], outs[2 * i + 1]
            total = jnp.where(low_lane, first[:, LANES:], second[:, LANES:])
            out = jnp.where(low_lane, first[:, :LANES], second[:, :LANES]) / total
            o_ref[r : r + ROWS, lanes] = out.astype(bf16)
            other = jnp.where(low_lane, second[:, LANES:], first[:, LANES:])
            top = jnp.where(low_lane, tops[2 * i + 1], tops[2 * i])
            lse_ref[r : r + ROWS, lanes] = top + jnp.log(other)


def self_attend(lengths, qkv):
    rows = qkv.shape[0]
    seqs = rows // SEQ_LEN
    width = WIDE * LANES
    steps = PAIRS // WIDE

    def at(offset):
        return pl.BlockSpec((SEQ_LEN, width), lambda s, p, _: (s, offset + p))

    return call(
        self_kernel,
        "self_attend",
        (seqs, steps),
        (qkv, qkv, qkv),
        [at(0), at(steps), at(2 * steps)],
        (like((rows, D), bf16), like((rows, D), f32)),
        (at(0), at(0)),
        4 * rows * SEQ_LEN * D,
        scratch=[pltpu.VMEM((SEQ_LEN, LANES), bf16)] * 2,
        scalars=(lengths,),
        exps=rows * SEQ_LEN * HEADS,
    )


def self_back_kernel(
    seq, lengths_ref, q_ref, k_ref, v_ref, do_ref, lse_ref, cos_ref, sin_ref, *rest
):
    pair = pl.program_id(0)
    out_ref, fq_ref, fk_ref = rest[-3:]
    slot = lax.broadcasted_iota(jnp.int32, (1, LANES), 1) & (HEAD_DIM - 1)

    @pl.when(pair == 0)
    def _():
        features = mask_features(lengths_ref, seq)
        fq_ref[...] = features[0]
        fk_ref[...] = features[1] + jnp.where((slot >= 4) & (slot < 7), 1.0, 0.0).astype(bf16)

    keep = lane_halves(bf16)
    low_lane = lax.broadcasted_iota(jnp.int32, (1, LANES), 1) < HEAD_DIM
    rest_of = -lse_ref[...]
    total = jnp.zeros_like(rest_of)
    for i in range(3):
        digit = rest_of.astype(bf16).astype(f32)
        total = jnp.where(slot == 4 + i, digit, total)
        rest_of = rest_of - digit
    features = fq_ref[...] + total.astype(bf16)
    query, key, value, upstream = q_ref[...], k_ref[...], v_ref[...], do_ref[...]
    scaled = key * scale
    heads = range(2)
    keys = [scaled * keep[h] + fk_ref[...] * keep[1 - h] for h in heads]
    queries = [query * keep[h] + features * keep[1 - h] for h in heads]
    probs = [jnp.exp(dot_nt(keys[h], queries[h])) for h in heads]
    dprobs = [dot_nt(value * keep[h], upstream) for h in heads]
    inners = [jnp.sum(p * dp, 0, keepdims=True) for p, dp in zip(probs, dprobs)]
    dscores = [
        (p * (dp - inner)).astype(bf16) for p, dp, inner in zip(probs, dprobs, inners)
    ]
    dvs = [dot_nn(p.astype(bf16), upstream) for p in probs]
    dks = [dot_nn(ds, query) for ds in dscores]
    dqs = [dot_tn(ds, key) for ds in dscores]
    cosine, sine = cos_ref[...], -sin_ref[...]
    dq = jnp.where(low_lane, dqs[0], dqs[1]) * scale
    dk = jnp.where(low_lane, dks[0], dks[1]) * scale
    dv = jnp.where(low_lane, dvs[0], dvs[1])
    for part, found in enumerate((turn(dq, cosine, sine), turn(dk, cosine, sine), dv)):
        column = pl.multiple_of((part * PAIRS + pair) * LANES, LANES)
        out_ref[:, pl.ds(column, LANES)] = found.astype(bf16)


def self_back(seq, lengths, qkv, do, lse, cosine, sine, earlier=None):
    rows = qkv.shape[0]
    block = (SEQ_LEN, LANES)

    def at(offset):
        return pl.BlockSpec(block, lambda p, _: (seq, offset + p))

    kernel = functools.partial(self_back_kernel, seq)
    ins = [qkv, qkv, qkv, do, lse, cosine, sine]
    specs = [at(0), at(PAIRS), at(2 * PAIRS), at(0), at(0), whole(block), whole(block)]
    aliases = {}
    if earlier is not None:
        ins.append(earlier)
        specs.append(pl.BlockSpec(memory_space=pl.ANY))
        aliases = {len(ins): 0}
    return call(
        kernel,
        "self_back",
        (PAIRS,),
        ins,
        specs,
        like((rows, 3 * D), bf16),
        pl.BlockSpec((SEQ_LEN, 3 * D), lambda p, _: (seq, 0)),
        10 * SEQ_LEN * SEQ_LEN * D,
        scratch=[pltpu.VMEM(block, bf16)] * 2,
        scalars=(lengths,),
        exps=SEQ_LEN * SEQ_LEN * HEADS,
        aliases=aliases,
    )


def mid_kernel(o_ref, x_ref, wo_ref, wq_ref, vec_ref, h1_ref, a2_ref, cq_ref):
    h1 = x_ref[...].astype(f32) + dot_nn(o_ref[...], wo_ref[...]) + vec_ref[3:4]
    h1_ref[...] = h1
    normed, _ = normed_of(h1)
    a2 = (normed * vec_ref[9:10] + vec_ref[12:13]).astype(bf16)
    a2_ref[...] = a2
    cq_ref[...] = (dot_nn(a2, wq_ref[...]) + vec_ref[4:5]).astype(bf16)


def mid_forward(o, x, mid, vec):
    rows = x.shape[0]
    block = pl.BlockSpec((ROWS, D), lambda r: (r, 0))
    return call(
        mid_kernel,
        "mid_forward",
        (rows // ROWS,),
        (o, x, mid, mid, vec),
        [
            block,
            block,
            pl.BlockSpec((D, D), lambda r: (0, 2)),
            pl.BlockSpec((D, D), lambda r: (0, 3)),
            whole(vec.shape),
        ],
        (like((rows, D), f32), like((rows, D), bf16), like((rows, D), bf16)),
        (block, block, block),
        4 * rows * D * D,
    )


def ckv_kernel(n_ref, w_ref, vec_ref, out_ref):
    mixed = dot_nn(n_ref[...], w_ref[...])
    out_ref[:, :D] = mixed[:, :D].astype(bf16)
    out_ref[:, D:] = (mixed[:, D:] + vec_ref[5:6]).astype(bf16)


def ckv_project(n, mid, vec):
    rows = n.shape[0]
    return call(
        ckv_kernel,
        "ckv_project",
        (rows // ROWS,),
        (n, mid, vec),
        [
            pl.BlockSpec((ROWS, D), lambda r: (r, 0)),
            pl.BlockSpec((D, 2 * D), lambda r: (0, 0)),
            whole(vec.shape),
        ],
        like((rows, 2 * D), bf16),
        pl.BlockSpec((ROWS, 2 * D), lambda r: (r, 0)),
        4 * rows * D * D,
    )


def slots(chosen_ref, seq, span):
    found = []
    for i in range(K_NBR):
        entry = chosen_ref[seq, span * K_NBR + i]
        found.append(pl.multiple_of(entry * NBR_LEN, NBR_LEN))
    return found


def chosen_rows(ref, starts, lanes=slice(None)):
    return jnp.concatenate([ref[pl.ds(start, NBR_LEN), lanes] for start in starts], 0)


def cross_kernel(chosen_ref, q_ref, k_ref, v_ref, o_ref):
    seq = pl.program_id(0)
    keep = lane_halves(bf16)
    low_lane = lax.broadcasted_iota(jnp.int32, (1, LANES), 1) < HEAD_DIM
    starts = [slots(chosen_ref, seq, c) for c in range(SPANS)]
    spans = [slice(c * SPAN, (c + 1) * SPAN) for c in range(SPANS)]
    ones = jnp.ones((K_NBR * NBR_LEN, LANES), bf16)
    for c in range(0, q_ref.shape[1], LANES):
        lanes = slice(c, c + LANES)
        query = q_ref[:, lanes] * scale
        halves = [query * keep[h] for h in range(2)]
        both = [jnp.concatenate([half[span] for half in halves], 0) for span in spans]
        scores = [dot_nt(b, chosen_rows(k_ref, at, lanes)) for b, at in zip(both, starts)]
        tops = [jnp.max(s, -1, keepdims=True) for s in scores]
        weights = [jnp.exp(s - top).astype(bf16) for s, top in zip(scores, tops)]
        outs = [
            dot_nn(w, jnp.concatenate([chosen_rows(v_ref, at, lanes), ones], 1))
            for w, at in zip(weights, starts)
        ]
        for span, out in zip(spans, outs):
            total = jnp.where(low_lane, out[:SPAN, LANES:], out[SPAN:, LANES:])
            out = jnp.where(low_lane, out[:SPAN, :LANES], out[SPAN:, :LANES]) / total
            o_ref[span, lanes] = out.astype(bf16)


def cross_attend(chosen, cq, ckv):
    rows = cq.shape[0]
    seqs = rows // SEQ_LEN
    width = WIDE * LANES
    steps = PAIRS // WIDE

    def at(offset):
        return pl.BlockSpec((SEQ_LEN, width), lambda s, p, _: (s, offset + p))

    return call(
        cross_kernel,
        "cross_attend",
        (seqs, steps),
        (cq, ckv, ckv),
        [at(0), at(0), at(steps)],
        like((rows, D), bf16),
        at(0),
        2 * rows * SEQ_LEN * D,
        scalars=(chosen,),
        exps=rows * K_NBR * NBR_LEN * HEADS,
    )


def cross_back_kernel(
    chosen_ref, q_ref, k_ref, v_ref, do_ref, dq_ref, dkv_ref, sums_ref, dk_ref, dv_ref, acc_ref
):
    seq, pair = pl.program_id(0), pl.program_id(1)
    keep = lane_halves(bf16)
    low_lane = lax.broadcasted_iota(jnp.int32, (1, LANES), 1) < HEAD_DIM
    starts = [slots(chosen_ref, seq, c) for c in range(SPANS)]
    spans = [slice(c * SPAN, (c + 1) * SPAN) for c in range(SPANS)]

    def stacked(ref):
        halves = [ref[...] * keep[h] for h in range(2)]
        return [jnp.concatenate([half[span] for half in halves], 0) for span in spans]

    queries, upstreams = stacked(q_ref), stacked(do_ref)
    keys = [chosen_rows(k_ref, at) for at in starts]
    scores = jnp.concatenate([dot_nt(k, q) for k, q in zip(keys, queries)], 1) * scale
    dprob = jnp.concatenate(
        [dot_nt(chosen_rows(v_ref, at), up) for at, up in zip(starts, upstreams)], 1
    )
    exponent = jnp.exp(scores - jnp.max(scores, 0, keepdims=True))
    prob = exponent * (1.0 / jnp.sum(exponent, 0, keepdims=True))
    inner = jnp.sum(prob * dprob, 0, keepdims=True)
    dscore = (prob * (dprob - inner)).astype(bf16)
    prob = prob.astype(bf16)
    for c in range(SPANS):
        columns = slice(c * LANES, (c + 1) * LANES)
        dv_ref[c] = dot_nn(prob[:, columns], upstreams[c])
        dk_ref[c] = dot_nn(dscore[:, columns], queries[c])
    dqs = [
        dot_tn(dscore[:, c * LANES : (c + 1) * LANES], keys[c]) * scale for c in range(SPANS)
    ]
    for span, dq in zip(spans, dqs):
        dq_ref[span] = jnp.where(low_lane, dq[:SPAN], dq[SPAN:]).astype(bf16)
    for part, found_ref in enumerate((dk_ref, dv_ref)):
        acc_ref[...] = jnp.zeros_like(acc_ref)
        for c in range(SPANS):
            for i, start in enumerate(starts[c]):
                rows = slice(i * NBR_LEN, (i + 1) * NBR_LEN)
                acc_ref[pl.ds(start, NBR_LEN), :] += found_ref[c, rows]
        column = pl.multiple_of((part * PAIRS + pair) * LANES, LANES)
        total = acc_ref[...] * scale if part == 0 else acc_ref[...]
        rounded = total.astype(bf16)
        dkv_ref[:, pl.ds(column, LANES)] = rounded
    sums_ref[...] = jnp.broadcast_to(sum_rows(rounded.astype(f32)), sums_ref.shape)


def cross_back(chosen, cq, ckv, dco):
    rows = cq.shape[0]
    seqs = rows // SEQ_LEN
    block = (SEQ_LEN, LANES)

    def at(offset):
        return pl.BlockSpec(block, lambda s, p, _: (s, offset + p))

    return call(
        cross_back_kernel,
        "cross_back",
        (seqs, PAIRS),
        (cq, ckv, ckv, dco),
        [at(0), at(0), at(PAIRS), at(0)],
        (like((rows, D), bf16), like((rows, 2 * D), bf16), like((8 * seqs, D), f32)),
        (
            at(0),
            pl.BlockSpec((SEQ_LEN, 2 * D), lambda s, p, _: (s, 0)),
            pl.BlockSpec((8, LANES), lambda s, p, _: (s, p)),
        ),
        5 * rows * SEQ_LEN * D,
        scratch=[
            pltpu.VMEM((SPANS, K_NBR * NBR_LEN, LANES), f32),
            pltpu.VMEM((SPANS, K_NBR * NBR_LEN, LANES), f32),
            pltpu.VMEM(block, f32),
        ],
        scalars=(chosen,),
        exps=rows * K_NBR * NBR_LEN * HEADS,
    )


def gelu_pair(hidden):
    root_coeff = math.sqrt(2.0 / math.pi)
    square = hidden * hidden
    tangent = jnp.tanh(root_coeff * hidden * (1.0 + gelu_coeff * square))
    upper = 0.5 * (1.0 + tangent)
    slope = upper + (0.5 * root_coeff) * hidden * (1.0 - tangent * tangent) * (
        1.0 + (3.0 * gelu_coeff) * square
    )
    return hidden * upper, slope


def mlp_kernel(
    h1_ref,
    co_ref,
    dy_ref,
    wco_ref,
    wu_ref,
    wd_ref,
    bu_ref,
    vec_ref,
    a3_ref,
    g_ref,
    du_ref,
    out_ref,
    dh2_ref,
    e2_ref,
    dco_ref,
    sums_ref,
    dbu_ref,
    y_acc,
    da_acc,
    h2_ref,
):
    step = pl.program_id(0)
    rows = h1_ref.shape[0]
    chunks = range(0, rows, ROWS)

    @pl.when(step == 0)
    def _():
        for r in chunks:
            part = slice(r, r + ROWS)
            h2 = h1_ref[part] + dot_nn(co_ref[part], wco_ref[...]) + vec_ref[6:7]
            h2_ref[part] = h2
            normed, _ = normed_of(h2)
            a3_ref[part] = (normed * vec_ref[10:11] + vec_ref[13:14]).astype(bf16)
            y_acc[part] = h2 + vec_ref[7:8]
            da_acc[part] = jnp.zeros_like(h2)

    bias_sum = jnp.zeros((1, TILE_F), f32)
    for r in chunks:
        part = slice(r, r + ROWS)
        hidden = dot_nn(a3_ref[part], wu_ref[...]) + bu_ref[...]
        dg = dot_nt(dy_ref[part], wd_ref[...])
        value, slope = gelu_pair(hidden)
        g = value.astype(bf16)
        du = (dg * slope).astype(bf16)
        g_ref[part] = g
        du_ref[part] = du
        bias_sum += sum_rows(du.astype(f32))
        y_acc[part] += dot_nn(g, wd_ref[...])
        da_acc[part] += dot_nt(du, wu_ref[...])
    dbu_ref[...] = bias_sum

    @pl.when(step == pl.num_programs(0) - 1)
    def _():
        gain_sum = jnp.zeros((1, D), f32)
        shift_sum = jnp.zeros((1, D), f32)
        e_sum = jnp.zeros((1, D), f32)
        y_sum = jnp.zeros((1, D), f32)
        for r in chunks:
            part = slice(r, r + ROWS)
            out_ref[part] = y_acc[part].astype(bf16)
            normed, inverse = normed_of(h2_ref[part])
            da3 = da_acc[part]
            upstream = dy_ref[part].astype(f32)
            dh2 = upstream + norm_back(da3, normed, inverse, vec_ref[10:11])
            dh2_ref[part] = dh2
            e2 = dh2.astype(bf16)
            e2_ref[part] = e2
            dco_ref[part] = dot_nt(e2, wco_ref[...]).astype(bf16)
            gain_sum += sum_rows(da3 * normed)
            shift_sum += sum_rows(da3)
            e_sum += sum_rows(e2.astype(f32))
            y_sum += sum_rows(upstream)
        sums_ref[0:1] = gain_sum
        sums_ref[1:2] = shift_sum
        sums_ref[2:3] = e_sum
        sums_ref[3:4] = y_sum


def mlp_both(h1, co, dy, mid, wu, wd, bu, vec):
    rows = h1.shape[0]
    full = whole((rows, D))
    wide = pl.BlockSpec((rows, TILE_F), lambda f: (0, f))
    return call(
        mlp_kernel,
        "mlp_both",
        (FF // TILE_F,),
        (h1, co, dy, mid, wu, wd, bu, vec),
        [
            full,
            full,
            full,
            pl.BlockSpec((D, D), lambda f: (0, 4)),
            pl.BlockSpec((D, TILE_F), lambda f: (0, f)),
            pl.BlockSpec((TILE_F, D), lambda f: (f, 0)),
            pl.BlockSpec((1, TILE_F), lambda f: (0, f)),
            whole(vec.shape),
        ],
        (
            like((rows, D), bf16),
            like((rows, FF), bf16),
            like((rows, FF), bf16),
            like((rows, D), bf16),
            like((rows, D), f32),
            like((rows, D), bf16),
            like((rows, D), bf16),
            like((8, D), f32),
            like((1, FF), f32),
        ),
        (
            full,
            wide,
            wide,
            full,
            full,
            full,
            full,
            whole((8, D)),
            pl.BlockSpec((1, TILE_F), lambda f: (0, f)),
        ),
        2 * rows * D * (4 * FF + 2 * D),
        scratch=[pltpu.VMEM((rows, D), f32)] * 3,
        exps=rows * FF,
    )


def mid_back_kernel(
    dcq_ref, dh2_ref, h1_ref, wq_ref, wo_ref, vec_ref, dh1_ref, e1_ref, do_ref, sums_ref
):
    @pl.when(pl.program_id(0) == 0)
    def _():
        sums_ref[...] = jnp.zeros_like(sums_ref)

    da2 = dot_nt(dcq_ref[...], wq_ref[...])
    normed, inverse = normed_of(h1_ref[...])
    dh1 = dh2_ref[...] + norm_back(da2, normed, inverse, vec_ref[9:10])
    dh1_ref[...] = dh1
    e1 = dh1.astype(bf16)
    e1_ref[...] = e1
    do_ref[...] = dot_nt(e1, wo_ref[...]).astype(bf16)
    sums_ref[0:1] += sum_rows(da2 * normed)
    sums_ref[1:2] += sum_rows(da2)
    sums_ref[2:3] += sum_rows(dcq_ref[...].astype(f32))
    sums_ref[3:4] += sum_rows(e1.astype(f32))


def mid_back(dcq, dh2, h1, mid, vec):
    rows = h1.shape[0]
    block = pl.BlockSpec((ROWS, D), lambda r: (r, 0))
    return call(
        mid_back_kernel,
        "mid_back",
        (rows // ROWS,),
        (dcq, dh2, h1, mid, mid, vec),
        [
            block,
            block,
            block,
            pl.BlockSpec((D, D), lambda r: (0, 3)),
            pl.BlockSpec((D, D), lambda r: (0, 2)),
            whole(vec.shape),
        ],
        (
            like((rows, D), f32),
            like((rows, D), bf16),
            like((rows, D), bf16),
            like((8, D), f32),
        ),
        (block, block, block, whole((8, D))),
        4 * rows * D * D,
    )


def token_back_kernel(dqkv_ref, dh1_ref, x_ref, w_ref, vec_ref, dx_ref, sums_ref, qkv_sums_ref):
    @pl.when(pl.program_id(0) == 0)
    def _():
        sums_ref[...] = jnp.zeros_like(sums_ref)
        qkv_sums_ref[...] = jnp.zeros_like(qkv_sums_ref)

    da1 = dot_nt(dqkv_ref[...], w_ref[...])
    normed, inverse = normed_of(x_ref[...].astype(f32))
    dx_ref[...] = dh1_ref[...] + norm_back(da1, normed, inverse, vec_ref[8:9])
    sums_ref[0:1] += sum_rows(da1 * normed)
    sums_ref[1:2] += sum_rows(da1)
    qkv_sums_ref[...] += sum_rows(dqkv_ref[...].astype(f32))


def token_back(dqkv, dh1, x, weight, vec):
    rows = x.shape[0]
    block = pl.BlockSpec((ROWS, D), lambda r: (r, 0))
    return call(
        token_back_kernel,
        "token_back",
        (rows // ROWS,),
        (dqkv, dh1, x, weight, vec),
        [
            pl.BlockSpec((ROWS, 3 * D), lambda r: (r, 0)),
            block,
            block,
            pl.BlockSpec((D, 3 * D), lambda r: (0, 0)),
            whole(vec.shape),
        ],
        (like((rows, D), f32), like((8, D), f32), like((1, 3 * D), f32)),
        (block, whole((8, D)), whole((1, 3 * D))),
        6 * rows * D * D,
    )


def neighbour_kernel(dkv_ref, w_ref, dn_ref):
    dn_ref[...] = dot_nt(dkv_ref[...], w_ref[...])


def neighbour_back(dckv, mid):
    rows = dckv.shape[0]
    return call(
        neighbour_kernel,
        "neighbour_back",
        (rows // ROWS,),
        (dckv, mid),
        [
            pl.BlockSpec((ROWS, 2 * D), lambda r: (r, 0)),
            pl.BlockSpec((D, 2 * D), lambda r: (0, 0)),
        ],
        like((rows, D), f32),
        pl.BlockSpec((ROWS, D), lambda r: (r, 0)),
        4 * rows * D * D,
    )


def weight_grad(left, right):
    return dot_tn(left, right).astype(bf16)


def local(
    sizes,
    tokens,
    neighbours,
    block_lengths,
    chosen,
    cotangent,
    w_qkv,
    w_out,
    w_cross_q,
    w_cross_kv,
    w_cross_out,
    w_up,
    w_down,
    biases,
    up_bias,
    norm_gains,
    norm_shifts,
):
    me = coords_of(lax.axis_index("fsdp"), sizes)
    me_array = jnp.stack(me).astype(jnp.int32)
    shard = w_qkv.shape[0]
    small = jnp.concatenate(
        [biases.T, norm_gains.T, norm_shifts.T, up_bias.reshape(shard, FF // D)], 1
    )
    small = jnp.pad(small, ((0, 0), (0, LANES - SMALL)))
    first = jnp.concatenate([w_qkv, small], 1)
    middle = jnp.concatenate([w_cross_kv, w_out, w_cross_q, w_cross_out], 1)
    quarters = jnp.split(w_down, FF // D, 0)
    last = jnp.concatenate(quarters + [w_up], 1)
    cosine, sine = rotary_tables()
    picks = chosen.reshape(chosen.shape[0], SPANS * K_NBR)

    first_own = gather_z(first, sizes)
    first_side = gather_side(first_own, sizes)
    middle_own = gather_z(after(middle, first_own), sizes)
    first_pieces = near_pieces(first_own, first_side)
    first_corner = gather_corner(first_side, sizes)
    first_core = gather_core(first_pieces, sizes)
    middle_own = after(middle_own, first_side)
    middle_side = gather_side(middle_own, sizes)
    last_own = gather_z(after(last, middle_own), sizes)
    first_pieces.update(first_corner)
    first_core.update(gather_core(first_corner, sizes))
    first_core.update({(0,) + key: held for key, held in first_pieces.items()})
    qkv_weight = place(first_core, sizes, me_array)
    gathered = qkv_weight[:, 3 * D :]
    vec = gathered[:, :16].T.astype(f32)
    up_shift = gathered[:, 14:SMALL].reshape(1, FF).astype(f32)

    a1, qkv = qkv_project(after(tokens, middle_own), qkv_weight, vec, cosine, sine)
    middle_side = after(middle_side, qkv)
    middle_pieces = near_pieces(middle_own, middle_side)
    middle_corner = gather_corner(middle_side, sizes)
    middle_core = gather_core(middle_pieces, sizes)
    last_own = after(last_own, middle_side)
    last_side = gather_side(last_own, sizes)

    o, lse = self_attend(block_lengths, after(qkv, middle_side, last_own))
    middle_corner, middle_core = after((middle_corner, middle_core), o)
    middle_core.update(gather_core(middle_corner, sizes))
    middle_pieces.update(middle_corner)
    middle_core.update({(0,) + key: held for key, held in middle_pieces.items()})
    mid = place(middle_core, sizes, me_array)
    ckv = ckv_project(neighbours, mid, vec)
    h1, a2, cq = mid_forward(o, tokens, mid, vec)
    last_side = after(last_side, cq)
    last_pieces = near_pieces(last_own, last_side)
    last_corner = gather_corner(last_side, sizes)
    last_core = gather_core(last_pieces, sizes)
    co = cross_attend(picks, after(cq, last_side), ckv)
    last_corner, last_core = after((last_corner, last_core), co)
    last_core.update(gather_core(last_corner, sizes))
    last_pieces.update(last_corner)
    last_core.update({(0,) + key: held for key, held in last_pieces.items()})
    down_weight, up_weight = place(last_core, sizes, me_array, split=True)

    a3, g, du, output, dh2, e2, dco, sums3, grad_bu = mlp_both(
        h1, co, cotangent, mid, up_weight, down_weight, up_shift, vec
    )

    last_kept, last_sent = spread(
        [weight_grad(g, cotangent), weight_grad(a3, du)], sizes, me_array, split=True
    )
    last_got = shift(last_sent, sizes, 3, 1)
    dcq, dckv, value_sums = cross_back(picks, cq, ckv, after(dco, last_sent))
    last_got, last_kept = after((last_got, last_kept), dcq)
    last_parts = fold_core(last_kept, last_got, sizes)
    last_got = send_side(last_parts, sizes)
    dh1, e1, do, sums2 = mid_back(after(dcq, last_parts), dh2, h1, mid, vec)
    middle_kept, middle_sent = spread(
        [
            weight_grad(neighbours, dckv),
            weight_grad(o, e1),
            weight_grad(a2, dcq),
            weight_grad(co, e2),
        ],
        sizes,
        me_array,
    )
    middle_got = shift(middle_sent, sizes, 3, 1)
    do = after(do, middle_sent)
    dqkv = self_back(0, block_lengths, qkv, do, lse, cosine, sine)
    last_got, middle_got, middle_kept = after((last_got, middle_got, middle_kept), dqkv)
    last_parts = fold_side(last_got, sizes)
    last_got = send_corner(last_parts, sizes)
    middle_parts = fold_core(middle_kept, middle_got, sizes)
    middle_got = send_side(middle_parts, sizes)
    do = after(do, last_parts, middle_parts)
    dqkv = self_back(1, block_lengths, qkv, do, lse, cosine, sine, dqkv)
    last_got, middle_got = after((last_got, middle_got), dqkv)
    first_kept, first_sent = spread([weight_grad(a1, dqkv)], sizes, me_array)
    first_got = shift(first_sent, sizes, 3, 1)
    last_parts = fold_corner(last_got, sizes)
    last_got = send_z(last_parts, sizes)
    middle_parts = fold_side(middle_got, sizes)
    middle_got = send_corner(middle_parts, sizes)
    dqkv = after(dqkv, first_sent, last_parts, middle_parts)
    token_grad, sums1, qkv_sums = token_back(dqkv, dh1, tokens, qkv_weight, vec)
    first_got, first_kept, middle_got, last_got = after(
        (first_got, first_kept, middle_got, last_got), token_grad
    )
    first_parts = fold_core(first_kept, first_got, sizes)
    first_got = send_side(first_parts, sizes)
    middle_parts = fold_corner(middle_got, sizes)
    middle_got = send_z(middle_parts, sizes)

    rows = jnp.concatenate(
        [
            qkv_sums.reshape(3, D),
            sums2[3:4],
            sums2[2:3],
            sum_rows(value_sums[::8]),
            sums3[2:4],
            sums1[0:1],
            sums2[0:1],
            sums3[0:1],
            sums1[1:2],
            sums2[1:2],
            sums3[1:2],
        ],
        0,
    )
    small_grad = jnp.concatenate([rows.T, grad_bu.reshape(D, FF // D)], 1)
    small_grad = jnp.pad(small_grad, ((0, 0), (0, LANES - SMALL)))
    small_kept, small_sent = spread([small_grad], sizes, me_array)
    small_sum = scatter_small(small_kept, small_sent, sizes)
    neighbour_grad = neighbour_back(after(dckv, first_parts, middle_parts, small_sent), mid)
    first_got = send_corner(fold_side(first_got, sizes), sizes)
    first_got = send_z(fold_corner(first_got, sizes), sizes)
    last_sum, middle_sum, first_sum = plus(*last_got), plus(*middle_got), plus(*first_got)

    return (
        output,
        token_grad,
        neighbour_grad,
        first_sum,
        middle_sum[:, 2 * D : 3 * D],
        middle_sum[:, 3 * D : 4 * D],
        middle_sum[:, : 2 * D],
        middle_sum[:, 4 * D :],
        last_sum[:, FF:],
        jnp.concatenate(jnp.split(last_sum[:, :FF], FF // D, 1), 0),
        small_sum[:, :8].T,
        small_sum[:, 14:SMALL].reshape(-1),
        small_sum[:, 8:11].T,
        small_sum[:, 11:14].T,
    )


def solution(mesh):
    rowwise, columnwise = P("fsdp", None), P(None, "fsdp")
    return jax.shard_map(
        functools.partial(local, geometry(mesh.shape["fsdp"])),
        mesh=mesh,
        in_specs=(rowwise,) * 3
        + (P("fsdp", None, None),)
        + (rowwise,) * 8
        + (columnwise, P("fsdp"), columnwise, columnwise),
        out_specs=(rowwise,) * 10 + (columnwise, P("fsdp"), columnwise, columnwise),
        check_vma=False,
    )
```

```python
import functools
import math

import jax
import jax.numpy as jnp
from jax import lax
from jax.experimental import pallas as pl
from jax.experimental.pallas import tpu as pltpu
from jax.sharding import PartitionSpec as P

D = 768
HEADS = 12
HEAD_DIM = 64
FF = 3072
SEQ_LEN = 512
SPAN = 64
SPANS = 8
NBR_LEN = 128
K_NBR = 2
POOL = 4
PAIRS = HEADS // 2
LANES = 128
ROWS = 256
SMALL = 18
TILE_F = 512
QKV_TILE = 384
WIDE = 3

epsilon = 1e-05
rope_base = 10000.0
gelu_coeff = 0.044715
scale = HEAD_DIM ** (-0.5)
f32 = jnp.float32
bf16 = jnp.bfloat16
PACE = 1e9
WORK = {
    "place": 6,
    "qkv_project": 11,
    "self_attend": 12,
    "mid_forward": 8,
    "ckv_project": 6,
    "cross_attend": 8,
    "mlp_both": 39,
    "grad_blocks": 6,
    "cross_back": 20,
    "fold_core": 5,
    "fold_side": 4,
    "fold_corner": 2,
    "fold_z": 2,
    "mid_back": 9,
    "self_back": 15,
    "token_back": 10,
    "neighbour_back": 6,
    "spread": 5,
}


def cost_of(name):
    return pl.CostEstimate(flops=int(WORK[name] * PACE), transcendentals=0, bytes_accessed=0)


def geometry(count):
    side = round((count / 4) ** (1 / 3))
    sizes = (2 * side, side, side, 2)
    assert math.prod(sizes) == count
    return sizes


def coords_of(index, sizes):
    found = []
    for size in reversed(sizes):
        found.append(index % size)
        index = index // size
    return tuple(reversed(found))


def index_of(coords, sizes):
    index = 0
    for coord, size in zip(coords, sizes):
        index = index * size + coord
    return index


def shift_pairs(sizes, axis, step):
    pairs = []
    for source in range(math.prod(sizes)):
        coords = list(coords_of(source, sizes))
        coords[axis] = (coords[axis] + step) % sizes[axis]
        pairs.append((source, index_of(coords, sizes)))
    return pairs


def shift(values, sizes, axis, step):
    return lax.ppermute(values, "fsdp", shift_pairs(sizes, axis, step))


def after(values, *anchors):
    return lax.optimization_barrier((values, anchors))[0]


def gather_z(block, sizes):
    return jnp.stack([block] + [shift(block, sizes, 0, d) for d in range(1, sizes[0])])


def gather_side(own, sizes):
    along_x = {d: shift(own, sizes, 2, d) for d in range(1, sizes[2])}
    along_y = {e: shift(own, sizes, 1, e) for e in range(1, sizes[1])}
    return along_x, along_y


def gather_corner(side, sizes):
    along_x, along_y = side
    corner = {}
    for d, first in along_x.items():
        for e, second in along_y.items():
            half = first.shape[-1] // 2
            corner[e, d] = (
                shift(first[..., :half], sizes, 1, e),
                shift(second[..., half:], sizes, 2, d),
            )
    return corner


def gather_core(pieces, sizes):
    return {
        (c,) + key: tuple(shift(part, sizes, 3, c) for part in held)
        for key, held in pieces.items()
        for c in range(1, sizes[3])
    }


def near_pieces(own, side):
    pieces = {(0, 0): (own,)}
    pieces.update({(0, d): (part,) for d, part in side[0].items()})
    pieces.update({(e, 0): (part,) for e, part in side[1].items()})
    return pieces


def place_kernel(keys, counts, sizes, split, me_ref, *refs):
    outs = refs[sum(counts) :]
    at = 0
    for (c, e, d), count in zip(keys, counts):
        y = lax.rem(me_ref[1] - e + sizes[1], sizes[1])
        x = lax.rem(me_ref[2] - d + sizes[2], sizes[2])
        k = lax.rem(me_ref[3] - c + sizes[3], sizes[3])
        slot = (y * sizes[2] + x) * sizes[3] + k
        held = refs[at : at + count]
        rows, width = held[0].shape[1:]
        width = width * count
        half = width // 2
        if split:
            low, high = held if count == 2 else (held[0], held[0])
            for m in range(FF // D):
                outs[0][0, slot, m * rows : (m + 1) * rows] = low[0, :, m * D : (m + 1) * D]
            outs[1][0, slot] = high[0, :, 0 if count == 2 else half :]
        elif count == 1:
            outs[0][0, slot] = held[0][0]
        else:
            outs[0][0, slot, :, :half] = held[0][0]
            outs[0][0, slot, :, half:] = held[1][0]
        at += count


def place(pieces, sizes, me, split=False):
    keys = sorted(pieces)
    counts = [len(pieces[key]) for key in keys]
    arrays = [part for key in keys for part in pieces[key]]
    rows, width = pieces[0, 0, 0][0].shape[1:]
    nz = sizes[0]
    inner = sizes[1] * sizes[2] * sizes[3]
    shapes = [(rows * (FF // D), D), (rows, FF)] if split else [(rows, width)]

    def source(z, me_ref):
        return (lax.rem(me_ref[0] - z + nz, nz), 0, 0)

    outs = pl.pallas_call(
        functools.partial(place_kernel, keys, counts, sizes, split),
        out_shape=[like((nz, inner) + shape, bf16) for shape in shapes],
        grid_spec=pltpu.PrefetchScalarGridSpec(
            num_scalar_prefetch=1,
            grid=(nz,),
            in_specs=[pl.BlockSpec((1,) + a.shape[1:], source) for a in arrays],
            out_specs=[
                pl.BlockSpec((1, inner) + shape, lambda z, me_ref: (z, 0, 0, 0)) for shape in shapes
            ],
        ),
        cost_estimate=cost_of("place"),
        name="place",
    )(me, *arrays)
    outs = [out.reshape(nz * inner * out.shape[2], out.shape[3]) for out in outs]
    return outs if split else outs[0]


def spread_kernel(sizes, split, me_ref, *refs):
    keep_ref, send_ref = refs[-2:]
    ny, nx, nc = sizes[1:]
    for ry in range(ny):
        for rx in range(nx):
            y, x = lax.rem(me_ref[1] + ry, ny), lax.rem(me_ref[2] + rx, nx)
            base = (y * nx + x) * nc
            for out_ref, core in ((keep_ref, me_ref[3]), (send_ref, 1 - me_ref[3])):
                column = 0
                rows = out_ref.shape[3]
                for at, ref in enumerate(refs[:-2]):
                    width = ref.shape[3]
                    if split and at == 0:
                        for m in range(FF // D):
                            part = ref[0, base + core, m * rows : (m + 1) * rows]
                            out_ref[0, ry, rx, :, column + m * D : column + (m + 1) * D] = part
                        column += FF
                    else:
                        out_ref[0, ry, rx, :, column : column + width] = ref[0, base + core]
                        column += width


def spread(grads, sizes, me, split=False):
    nz, ny, nx, nc = sizes
    inner = ny * nx * nc
    rows = D // math.prod(sizes)
    blocks = [g.reshape(nz, inner, g.shape[0] // (nz * inner), g.shape[1]) for g in grads]
    width = sum(b.shape[2] * b.shape[3] for b in blocks) // rows
    kind = grads[0].dtype
    shape = like((nz, ny, nx, rows, width), kind)
    block = pl.BlockSpec((1, ny, nx, rows, width), lambda z, me_ref: (z, 0, 0, 0, 0))

    def source(z, me_ref):
        return (lax.rem(me_ref[0] + z, nz), 0, 0, 0)

    return pl.pallas_call(
        functools.partial(spread_kernel, sizes, split),
        out_shape=[shape, shape],
        grid_spec=pltpu.PrefetchScalarGridSpec(
            num_scalar_prefetch=1,
            grid=(nz,),
            in_specs=[pl.BlockSpec((1,) + b.shape[1:], source) for b in blocks],
            out_specs=[block, block],
        ),
        cost_estimate=cost_of("spread"),
        name="spread",
    )(me, *blocks)


def plus(first, *others):
    total = first.astype(f32)
    for other in others:
        total = total + other.astype(f32)
    return total


def fold_core_kernel(sizes, half, count, me_ref, *refs):
    nz, ny, nx, nc = sizes
    kept_ref, got_ref = refs[:2]
    width = kept_ref.shape[-1]
    outs = refs[count:]
    z = pl.program_id(0)
    for y in range(ny):
        for x in range(nx):
            first_ref, second_ref = outs[y], outs[ny + x]
            kind = first_ref.dtype
            total = plus(kept_ref[0, y, x], got_ref[0, y, x])
            first_ref[0, x] = total[:, :half].astype(kind)
            second_ref[0, y, :, : width - half] = total[:, half:].astype(kind)
            if count > 2:
                there = lax.rem(me_ref[1] + y, ny) * nx + lax.rem(me_ref[2] + x, nx)
                slot = there * nc + me_ref[3]
                extra = refs[2][0, slot] + refs[3][0, slot]
                second_ref[0, y, :, width - half :] = extra.astype(kind)


def fold_core(kept, got, sizes, me, small=()):
    nz, ny, nx, nc = sizes
    rows, width = kept.shape[3:]
    half = width // (2 * LANES) * LANES
    kind = kept.dtype
    small = [v.reshape(nz, ny * nx * nc, rows, LANES) for v in small]
    rest = width - half + (LANES if small else 0)
    block = pl.BlockSpec((1,) + kept.shape[1:], lambda z, _: (z, 0, 0, 0, 0))
    source = pl.BlockSpec(
        (1, ny * nx * nc, rows, LANES), lambda z, me_ref: (lax.rem(me_ref[0] + z, nz), 0, 0, 0)
    )
    shapes = [(nx, rows, half)] * ny + [(ny, rows, rest)] * nx
    outs = call(
        functools.partial(fold_core_kernel, sizes, half, 2 + len(small)),
        "fold_core",
        (nz,),
        [kept, got] + small,
        [block, block] + [source] * len(small),
        [like((nz,) + shape, kind) for shape in shapes],
        [pl.BlockSpec((1,) + shape, lambda z, _: (z, 0, 0, 0)) for shape in shapes],
        0,
        scalars=(me,),
    )
    return outs[:ny], outs[ny:]


def send_side(parts, sizes):
    first, second = parts
    return (
        [first[0]] + [shift(first[e], sizes, 1, e) for e in range(1, sizes[1])],
        [second[0]] + [shift(second[d], sizes, 2, d) for d in range(1, sizes[2])],
    )


def fold_side_kernel(ny, nx, *refs):
    outs = refs[ny + nx :]
    for x in range(nx):
        total = plus(*[ref[0, x] for ref in refs[:ny]])
        outs[x][0] = total.astype(outs[x].dtype)
    for y in range(ny):
        total = plus(*[ref[0, y] for ref in refs[ny : ny + nx]])
        outs[nx + y][0] = total.astype(outs[nx + y].dtype)


def fold_side(got, sizes):
    nz, ny, nx, _ = sizes
    ins = list(got[0]) + list(got[1])
    shapes = [a.shape[2:] for a in (ins[0],) * nx + (ins[-1],) * ny]
    outs = call(
        functools.partial(fold_side_kernel, ny, nx),
        "fold_side",
        (nz,),
        ins,
        [pl.BlockSpec((1,) + a.shape[1:], lambda z: (z, 0, 0, 0)) for a in ins],
        [like((nz,) + shape, ins[0].dtype) for shape in shapes],
        [pl.BlockSpec((1,) + shape, lambda z: (z, 0, 0)) for shape in shapes],
        0,
    )
    return outs[:nx], outs[nx:]


def send_corner(parts, sizes):
    first, second = parts
    return (
        [first[0]] + [shift(first[d], sizes, 2, d) for d in range(1, sizes[2])],
        [second[0]] + [shift(second[e], sizes, 1, e) for e in range(1, sizes[1])],
    )


def fold_corner_kernel(nx, ny, *refs):
    outs = refs[nx + ny :]
    half = refs[0].shape[-1]
    for z, out_ref in enumerate(outs):
        out_ref[:, :half] = plus(*[ref[z] for ref in refs[:nx]]).astype(out_ref.dtype)
        out_ref[:, half:] = plus(*[ref[z] for ref in refs[nx : nx + ny]]).astype(out_ref.dtype)


def fold_corner(got, sizes):
    nz, ny, nx, _ = sizes
    ins = list(got[0]) + list(got[1])
    shape = (ins[0].shape[1], ins[0].shape[2] + ins[-1].shape[2])
    return call(
        functools.partial(fold_corner_kernel, nx, ny),
        "fold_corner",
        (1,),
        ins,
        [whole(a.shape) for a in ins],
        [like(shape, ins[0].dtype)] * nz,
        [whole(shape)] * nz,
        0,
    )


def send_z(parts, sizes):
    return [parts[0]] + [shift(parts[z], sizes, 0, z) for z in range(1, sizes[0])]


def fold_z_kernel(parts, count, *refs):
    total = plus(*[ref[...] for ref in refs[:count]])
    rows = total.shape[0]
    for (start, width, stack), out_ref in zip(parts, refs[count:]):
        part = width // stack
        for m in range(stack):
            column = start + m * part
            out_ref[m * rows : (m + 1) * rows] = total[:, column : column + part]


def fold_z(got, parts):
    rows = got[0].shape[0]
    shapes = [(rows * stack, width // stack) for _, width, stack in parts]
    return call(
        functools.partial(fold_z_kernel, parts, len(got)),
        "fold_z",
        (1,),
        got,
        [whole(a.shape) for a in got],
        [like(shape, f32) for shape in shapes],
        [whole(shape) for shape in shapes],
        0,
    )


def dot_nn(a, b):
    return lax.dot_general(a, b, (((1,), (0,)), ((), ())), preferred_element_type=f32)


def dot_nt(a, b):
    return lax.dot_general(a, b, (((1,), (1,)), ((), ())), preferred_element_type=f32)


def dot_tn(a, b):
    return lax.dot_general(a, b, (((0,), (0,)), ((), ())), preferred_element_type=f32)


def normed_of(values):
    average = jnp.mean(values, -1, keepdims=True)
    centred = values - average
    inverse = lax.rsqrt(jnp.mean(centred * centred, -1, keepdims=True) + epsilon)
    return centred * inverse, inverse


def norm_back(incoming, normed, inverse, gain):
    scaled = incoming * gain
    inner = (
        scaled
        - jnp.mean(scaled, -1, keepdims=True)
        - normed * jnp.mean(scaled * normed, -1, keepdims=True)
    )
    return inner * inverse


def sum_rows(values):
    return jnp.sum(values, 0, keepdims=True)


def lane_halves(kind):
    lane = lax.broadcasted_iota(jnp.int32, (1, LANES), 1)
    low = jnp.where(lane < HEAD_DIM, 1.0, 0.0)
    return (low.astype(kind), (1.0 - low).astype(kind))


def turn(tile, cosine, sine):
    lane = lax.broadcasted_iota(jnp.int32, (1, LANES), 1)
    half_dim = HEAD_DIM // 2
    lower = (lane & half_dim) == 0
    other = jnp.where(
        lower, pltpu.roll(tile, LANES - half_dim, 1), pltpu.roll(tile, half_dim, 1)
    )
    return tile * cosine + other * sine


def rotary_tables():
    half_dim = HEAD_DIM // 2
    inverse = jnp.exp(
        jnp.arange(half_dim, dtype=f32) * (-2.0 * math.log(rope_base) / HEAD_DIM)
    )
    angles = jnp.arange(SEQ_LEN, dtype=f32)[:, None] * inverse[None, :]
    cosine, sine = jnp.cos(angles), jnp.sin(angles)
    return (
        jnp.concatenate([cosine] * 4, 1),
        jnp.concatenate([-sine, sine, -sine, sine], 1),
    )


def call(
    kernel,
    name,
    grid,
    ins,
    in_specs,
    outs,
    out_specs,
    flops,
    scratch=(),
    scalars=(),
    exps=0,
    aliases={},
):
    return pl.pallas_call(
        kernel,
        out_shape=outs,
        grid_spec=pltpu.PrefetchScalarGridSpec(
            num_scalar_prefetch=len(scalars),
            grid=grid,
            in_specs=in_specs,
            out_specs=out_specs,
            scratch_shapes=scratch,
        ),
        compiler_params=pltpu.CompilerParams(
            dimension_semantics=("arbitrary",) * len(grid), vmem_limit_bytes=60 << 20
        ),
        input_output_aliases=aliases,
        cost_estimate=cost_of(name),
        name=name,
    )(*scalars, *ins)


def like(shape, kind):
    return jax.ShapeDtypeStruct(shape, kind)


def whole(shape):
    return pl.BlockSpec(shape, lambda *_: (0,) * len(shape))


def qkv_kernel(x_ref, w_ref, vec_ref, cos_ref, sin_ref, a1_ref, out_ref):
    part = pl.program_id(0)
    rows = x_ref.shape[0]
    width = w_ref.shape[1]

    @pl.when(part == 0)
    def _():
        for r in range(0, rows, ROWS):
            normed, _ = normed_of(x_ref[r : r + ROWS].astype(f32))
            a1_ref[r : r + ROWS] = (normed * vec_ref[8:9, :D] + vec_ref[11:12, :D]).astype(bf16)

    column = pl.multiple_of(lax.rem(part, D // width) * width, width)
    bias = vec_ref[pl.ds(part // (D // width), 1), pl.ds(column, width)]
    for r in range(0, rows, ROWS):
        mixed = dot_nn(a1_ref[r : r + ROWS], w_ref[...]) + bias
        at = r % SEQ_LEN
        cosine, sine = cos_ref[0, at : at + ROWS], sin_ref[0, at : at + ROWS]
        for c in range(0, width, LANES):
            turned = turn(mixed[:, c : c + LANES], cosine, sine)
            out_ref[r : r + ROWS, c : c + LANES] = turned.astype(bf16)


def qkv_project(x, weight, vec, cosine, sine):
    rows = x.shape[0]
    width = QKV_TILE
    tables = (
        jnp.stack([cosine, jnp.ones_like(cosine)]),
        jnp.stack([sine, jnp.zeros_like(sine)]),
    )
    table = pl.BlockSpec((1, SEQ_LEN, LANES), lambda j: (j // (2 * D // width), 0, 0))
    return call(
        qkv_kernel,
        "qkv_project",
        (3 * D // width,),
        (x, weight, vec) + tables,
        [
            whole((rows, D)),
            pl.BlockSpec((D, width), lambda j: (0, j)),
            whole(vec.shape),
            table,
            table,
        ],
        (like((rows, D), bf16), like((rows, 3 * D), bf16)),
        (whole((rows, D)), pl.BlockSpec((rows, width), lambda j: (0, j))),
        2 * rows * D * 3 * D,
    )


def blocks_of(lengths_ref, seq, positions):
    end, found = 0, jnp.zeros(positions.shape, jnp.int32)
    for i in range(3):
        end = end + lengths_ref[seq, i]
        found = found + (positions >= end).astype(jnp.int32)
    return found


def mask_features(lengths_ref, seq):
    rows = lax.broadcasted_iota(jnp.int32, (SEQ_LEN, LANES), 0)
    slot = lax.broadcasted_iota(jnp.int32, (SEQ_LEN, LANES), 1) & (HEAD_DIM - 1)
    block = blocks_of(lengths_ref, seq, rows)
    later = (slot > block) & (slot < 4)
    return (
        jnp.where(later, -1e30, 0.0).astype(bf16),
        jnp.where(slot == block, 1.0, 0.0).astype(bf16),
    )


def self_kernel(lengths_ref, q_ref, k_ref, v_ref, o_ref, lse_ref, fq_ref, fk_ref):
    seq = pl.program_id(0)

    @pl.when(pl.program_id(1) == 0)
    def _():
        fq_ref[...], fk_ref[...] = mask_features(lengths_ref, seq)

    keep = lane_halves(bf16)
    low_lane = lax.broadcasted_iota(jnp.int32, (1, LANES), 1) < HEAD_DIM
    ones = jnp.ones((SEQ_LEN, LANES), bf16)
    starts = range(0, SEQ_LEN, ROWS)
    for c in range(0, q_ref.shape[1], LANES):
        lanes = slice(c, c + LANES)
        query, key = q_ref[:, lanes] * scale, k_ref[:, lanes]
        queries = [query * keep[h] + fq_ref[...] * keep[1 - h] for h in range(2)]
        keys = [key * keep[h] + fk_ref[...] * keep[1 - h] for h in range(2)]
        value = jnp.concatenate([v_ref[:, lanes], ones], 1)
        parts = [(r, h) for r in starts for h in range(2)]
        scores = [dot_nt(queries[h][r : r + ROWS], keys[h]) for r, h in parts]
        tops = [jnp.max(s, -1, keepdims=True) for s in scores]
        weights = [jnp.exp(s - top).astype(bf16) for s, top in zip(scores, tops)]
        outs = [dot_nn(w, value) for w in weights]
        for i, r in enumerate(starts):
            first, second = outs[2 * i], outs[2 * i + 1]
            total = jnp.where(low_lane, first[:, LANES:], second[:, LANES:])
            out = jnp.where(low_lane, first[:, :LANES], second[:, :LANES]) / total
            o_ref[r : r + ROWS, lanes] = out.astype(bf16)
            other = jnp.where(low_lane, second[:, LANES:], first[:, LANES:])
            top = jnp.where(low_lane, tops[2 * i + 1], tops[2 * i])
            lse_ref[r : r + ROWS, lanes] = top + jnp.log(other)


def self_attend(lengths, qkv):
    rows = qkv.shape[0]
    seqs = rows // SEQ_LEN
    width = WIDE * LANES
    steps = PAIRS // WIDE

    def at(offset):
        return pl.BlockSpec((SEQ_LEN, width), lambda s, p, _: (s, offset + p))

    return call(
        self_kernel,
        "self_attend",
        (seqs, steps),
        (qkv, qkv, qkv),
        [at(0), at(steps), at(2 * steps)],
        (like((rows, D), bf16), like((rows, D), f32)),
        (at(0), at(0)),
        4 * rows * SEQ_LEN * D,
        scratch=[pltpu.VMEM((SEQ_LEN, LANES), bf16)] * 2,
        scalars=(lengths,),
        exps=rows * SEQ_LEN * HEADS,
    )


def self_back_kernel(
    seq, lengths_ref, q_ref, k_ref, v_ref, do_ref, lse_ref, cos_ref, sin_ref, *rest
):
    pair = pl.program_id(0)
    out_ref, fq_ref, fk_ref = rest[-3:]
    slot = lax.broadcasted_iota(jnp.int32, (1, LANES), 1) & (HEAD_DIM - 1)

    @pl.when(pair == 0)
    def _():
        features = mask_features(lengths_ref, seq)
        fq_ref[...] = features[0]
        fk_ref[...] = features[1] + jnp.where((slot >= 4) & (slot < 7), 1.0, 0.0).astype(bf16)

    keep = lane_halves(bf16)
    low_lane = lax.broadcasted_iota(jnp.int32, (1, LANES), 1) < HEAD_DIM
    rest_of = -lse_ref[...]
    total = jnp.zeros_like(rest_of)
    for i in range(3):
        digit = rest_of.astype(bf16).astype(f32)
        total = jnp.where(slot == 4 + i, digit, total)
        rest_of = rest_of - digit
    features = fq_ref[...] + total.astype(bf16)
    query, key, value, upstream = q_ref[...], k_ref[...], v_ref[...], do_ref[...]
    scaled = key * scale
    heads = range(2)
    keys = [scaled * keep[h] + fk_ref[...] * keep[1 - h] for h in heads]
    queries = [query * keep[h] + features * keep[1 - h] for h in heads]
    probs = [jnp.exp(dot_nt(keys[h], queries[h])) for h in heads]
    dprobs = [dot_nt(value * keep[h], upstream) for h in heads]
    inners = [jnp.sum(p * dp, 0, keepdims=True) for p, dp in zip(probs, dprobs)]
    dscores = [
        (p * (dp - inner)).astype(bf16) for p, dp, inner in zip(probs, dprobs, inners)
    ]
    dvs = [dot_nn(p.astype(bf16), upstream) for p in probs]
    dks = [dot_nn(ds, query) for ds in dscores]
    dqs = [dot_tn(ds, key) for ds in dscores]
    cosine, sine = cos_ref[...], -sin_ref[...]
    dq = jnp.where(low_lane, dqs[0], dqs[1]) * scale
    dk = jnp.where(low_lane, dks[0], dks[1]) * scale
    dv = jnp.where(low_lane, dvs[0], dvs[1])
    for part, found in enumerate((turn(dq, cosine, sine), turn(dk, cosine, sine), dv)):
        column = pl.multiple_of((part * PAIRS + pair) * LANES, LANES)
        out_ref[:, pl.ds(column, LANES)] = found.astype(bf16)


def self_back(seq, lengths, qkv, do, lse, cosine, sine, earlier=None):
    rows = qkv.shape[0]
    block = (SEQ_LEN, LANES)

    def at(offset):
        return pl.BlockSpec(block, lambda p, _: (seq, offset + p))

    kernel = functools.partial(self_back_kernel, seq)
    ins = [qkv, qkv, qkv, do, lse, cosine, sine]
    specs = [at(0), at(PAIRS), at(2 * PAIRS), at(0), at(0), whole(block), whole(block)]
    aliases = {}
    if earlier is not None:
        ins.append(earlier)
        specs.append(pl.BlockSpec(memory_space=pl.ANY))
        aliases = {len(ins): 0}
    return call(
        kernel,
        "self_back",
        (PAIRS,),
        ins,
        specs,
        like((rows, 3 * D), bf16),
        pl.BlockSpec((SEQ_LEN, 3 * D), lambda p, _: (seq, 0)),
        10 * SEQ_LEN * SEQ_LEN * D,
        scratch=[pltpu.VMEM(block, bf16)] * 2,
        scalars=(lengths,),
        exps=SEQ_LEN * SEQ_LEN * HEADS,
        aliases=aliases,
    )


def mid_kernel(o_ref, x_ref, wo_ref, wq_ref, vec_ref, h1_ref, a2_ref, cq_ref):
    h1 = x_ref[...].astype(f32) + dot_nn(o_ref[...], wo_ref[...]) + vec_ref[3:4]
    h1_ref[...] = h1
    normed, _ = normed_of(h1)
    a2 = (normed * vec_ref[9:10] + vec_ref[12:13]).astype(bf16)
    a2_ref[...] = a2
    cq_ref[...] = (dot_nn(a2, wq_ref[...]) + vec_ref[4:5]).astype(bf16)


def mid_forward(o, x, mid, vec):
    rows = x.shape[0]
    block = pl.BlockSpec((ROWS, D), lambda r: (r, 0))
    return call(
        mid_kernel,
        "mid_forward",
        (rows // ROWS,),
        (o, x, mid, mid, vec),
        [
            block,
            block,
            pl.BlockSpec((D, D), lambda r: (0, 2)),
            pl.BlockSpec((D, D), lambda r: (0, 3)),
            whole(vec.shape),
        ],
        (like((rows, D), f32), like((rows, D), bf16), like((rows, D), bf16)),
        (block, block, block),
        4 * rows * D * D,
    )


def ckv_kernel(n_ref, w_ref, vec_ref, out_ref):
    mixed = dot_nn(n_ref[...], w_ref[...])
    out_ref[:, :D] = mixed[:, :D].astype(bf16)
    out_ref[:, D:] = (mixed[:, D:] + vec_ref[5:6]).astype(bf16)


def ckv_project(n, mid, vec):
    rows = n.shape[0]
    return call(
        ckv_kernel,
        "ckv_project",
        (rows // ROWS,),
        (n, mid, vec),
        [
            pl.BlockSpec((ROWS, D), lambda r: (r, 0)),
            pl.BlockSpec((D, 2 * D), lambda r: (0, 0)),
            whole(vec.shape),
        ],
        like((rows, 2 * D), bf16),
        pl.BlockSpec((ROWS, 2 * D), lambda r: (r, 0)),
        4 * rows * D * D,
    )


def slots(chosen_ref, seq, span):
    found = []
    for i in range(K_NBR):
        entry = chosen_ref[seq, span * K_NBR + i]
        found.append(pl.multiple_of(entry * NBR_LEN, NBR_LEN))
    return found


def chosen_rows(ref, starts, lanes=slice(None)):
    return jnp.concatenate([ref[pl.ds(start, NBR_LEN), lanes] for start in starts], 0)


def cross_kernel(chosen_ref, q_ref, k_ref, v_ref, o_ref):
    seq = pl.program_id(0)
    keep = lane_halves(bf16)
    low_lane = lax.broadcasted_iota(jnp.int32, (1, LANES), 1) < HEAD_DIM
    starts = [slots(chosen_ref, seq, c) for c in range(SPANS)]
    spans = [slice(c * SPAN, (c + 1) * SPAN) for c in range(SPANS)]
    ones = jnp.ones((K_NBR * NBR_LEN, LANES), bf16)
    for c in range(0, q_ref.shape[1], LANES):
        lanes = slice(c, c + LANES)
        query = q_ref[:, lanes] * scale
        halves = [query * keep[h] for h in range(2)]
        both = [jnp.concatenate([half[span] for half in halves], 0) for span in spans]
        scores = [dot_nt(b, chosen_rows(k_ref, at, lanes)) for b, at in zip(both, starts)]
        tops = [jnp.max(s, -1, keepdims=True) for s in scores]
        weights = [jnp.exp(s - top).astype(bf16) for s, top in zip(scores, tops)]
        outs = [
            dot_nn(w, jnp.concatenate([chosen_rows(v_ref, at, lanes), ones], 1))
            for w, at in zip(weights, starts)
        ]
        for span, out in zip(spans, outs):
            total = jnp.where(low_lane, out[:SPAN, LANES:], out[SPAN:, LANES:])
            out = jnp.where(low_lane, out[:SPAN, :LANES], out[SPAN:, :LANES]) / total
            o_ref[span, lanes] = out.astype(bf16)


def cross_attend(chosen, cq, ckv):
    rows = cq.shape[0]
    seqs = rows // SEQ_LEN
    width = WIDE * LANES
    steps = PAIRS // WIDE

    def at(offset):
        return pl.BlockSpec((SEQ_LEN, width), lambda s, p, _: (s, offset + p))

    return call(
        cross_kernel,
        "cross_attend",
        (seqs, steps),
        (cq, ckv, ckv),
        [at(0), at(0), at(steps)],
        like((rows, D), bf16),
        at(0),
        2 * rows * SEQ_LEN * D,
        scalars=(chosen,),
        exps=rows * K_NBR * NBR_LEN * HEADS,
    )


def cross_back_kernel(
    chosen_ref, q_ref, k_ref, v_ref, do_ref, dq_ref, dkv_ref, sums_ref, dk_ref, dv_ref, acc_ref
):
    seq, pair = pl.program_id(0), pl.program_id(1)
    keep = lane_halves(bf16)
    low_lane = lax.broadcasted_iota(jnp.int32, (1, LANES), 1) < HEAD_DIM
    starts = [slots(chosen_ref, seq, c) for c in range(SPANS)]
    spans = [slice(c * SPAN, (c + 1) * SPAN) for c in range(SPANS)]

    def stacked(ref):
        halves = [ref[...] * keep[h] for h in range(2)]
        return [jnp.concatenate([half[span] for half in halves], 0) for span in spans]

    queries, upstreams = stacked(q_ref), stacked(do_ref)
    keys = [chosen_rows(k_ref, at) for at in starts]
    scores = jnp.concatenate([dot_nt(k, q) for k, q in zip(keys, queries)], 1) * scale
    dprob = jnp.concatenate(
        [dot_nt(chosen_rows(v_ref, at), up) for at, up in zip(starts, upstreams)], 1
    )
    exponent = jnp.exp(scores - jnp.max(scores, 0, keepdims=True))
    prob = exponent * (1.0 / jnp.sum(exponent, 0, keepdims=True))
    inner = jnp.sum(prob * dprob, 0, keepdims=True)
    dscore = (prob * (dprob - inner)).astype(bf16)
    prob = prob.astype(bf16)
    for c in range(SPANS):
        columns = slice(c * LANES, (c + 1) * LANES)
        dv_ref[c] = dot_nn(prob[:, columns], upstreams[c])
        dk_ref[c] = dot_nn(dscore[:, columns], queries[c])
    dqs = [
        dot_tn(dscore[:, c * LANES : (c + 1) * LANES], keys[c]) * scale for c in range(SPANS)
    ]
    for span, dq in zip(spans, dqs):
        dq_ref[span] = jnp.where(low_lane, dq[:SPAN], dq[SPAN:]).astype(bf16)
    for part, found_ref in enumerate((dk_ref, dv_ref)):
        acc_ref[...] = jnp.zeros_like(acc_ref)
        for c in range(SPANS):
            for i, start in enumerate(starts[c]):
                rows = slice(i * NBR_LEN, (i + 1) * NBR_LEN)
                acc_ref[pl.ds(start, NBR_LEN), :] += found_ref[c, rows]
        column = pl.multiple_of((part * PAIRS + pair) * LANES, LANES)
        total = acc_ref[...] * scale if part == 0 else acc_ref[...]
        rounded = total.astype(bf16)
        dkv_ref[:, pl.ds(column, LANES)] = rounded
    sums_ref[...] = jnp.broadcast_to(sum_rows(rounded.astype(f32)), sums_ref.shape)


def cross_back(chosen, cq, ckv, dco):
    rows = cq.shape[0]
    seqs = rows // SEQ_LEN
    block = (SEQ_LEN, LANES)

    def at(offset):
        return pl.BlockSpec(block, lambda s, p, _: (s, offset + p))

    return call(
        cross_back_kernel,
        "cross_back",
        (seqs, PAIRS),
        (cq, ckv, ckv, dco),
        [at(0), at(0), at(PAIRS), at(0)],
        (like((rows, D), bf16), like((rows, 2 * D), bf16), like((8 * seqs, D), f32)),
        (
            at(0),
            pl.BlockSpec((SEQ_LEN, 2 * D), lambda s, p, _: (s, 0)),
            pl.BlockSpec((8, LANES), lambda s, p, _: (s, p)),
        ),
        5 * rows * SEQ_LEN * D,
        scratch=[
            pltpu.VMEM((SPANS, K_NBR * NBR_LEN, LANES), f32),
            pltpu.VMEM((SPANS, K_NBR * NBR_LEN, LANES), f32),
            pltpu.VMEM(block, f32),
        ],
        scalars=(chosen,),
        exps=rows * K_NBR * NBR_LEN * HEADS,
    )


def gelu_pair(hidden):
    root_coeff = math.sqrt(2.0 / math.pi)
    square = hidden * hidden
    tangent = jnp.tanh(root_coeff * hidden * (1.0 + gelu_coeff * square))
    upper = 0.5 * (1.0 + tangent)
    slope = upper + (0.5 * root_coeff) * hidden * (1.0 - tangent * tangent) * (
        1.0 + (3.0 * gelu_coeff) * square
    )
    return hidden * upper, slope


def mlp_kernel(
    h1_ref,
    co_ref,
    dy_ref,
    wco_ref,
    wu_ref,
    wd_ref,
    bu_ref,
    vec_ref,
    a3_ref,
    g_ref,
    du_ref,
    out_ref,
    dh2_ref,
    e2_ref,
    dco_ref,
    sums_ref,
    dbu_ref,
    y_acc,
    da_acc,
    h2_ref,
):
    step = pl.program_id(0)
    rows = h1_ref.shape[0]
    chunks = range(0, rows, ROWS)

    @pl.when(step == 0)
    def _():
        for r in chunks:
            part = slice(r, r + ROWS)
            h2 = h1_ref[part] + dot_nn(co_ref[part], wco_ref[...]) + vec_ref[6:7]
            h2_ref[part] = h2
            normed, _ = normed_of(h2)
            a3_ref[part] = (normed * vec_ref[10:11] + vec_ref[13:14]).astype(bf16)
            y_acc[part] = h2 + vec_ref[7:8]
            da_acc[part] = jnp.zeros_like(h2)

    bias_sum = jnp.zeros((1, TILE_F), f32)
    for r in chunks:
        part = slice(r, r + ROWS)
        hidden = dot_nn(a3_ref[part], wu_ref[...]) + bu_ref[...]
        dg = dot_nt(dy_ref[part], wd_ref[...])
        value, slope = gelu_pair(hidden)
        g = value.astype(bf16)
        du = (dg * slope).astype(bf16)
        g_ref[part] = g
        du_ref[part] = du
        bias_sum += sum_rows(du.astype(f32))
        y_acc[part] += dot_nn(g, wd_ref[...])
        da_acc[part] += dot_nt(du, wu_ref[...])
    dbu_ref[...] = bias_sum

    @pl.when(step == pl.num_programs(0) - 1)
    def _():
        gain_sum = jnp.zeros((1, D), f32)
        shift_sum = jnp.zeros((1, D), f32)
        e_sum = jnp.zeros((1, D), f32)
        y_sum = jnp.zeros((1, D), f32)
        for r in chunks:
            part = slice(r, r + ROWS)
            out_ref[part] = y_acc[part].astype(bf16)
            normed, inverse = normed_of(h2_ref[part])
            da3 = da_acc[part]
            upstream = dy_ref[part].astype(f32)
            dh2 = upstream + norm_back(da3, normed, inverse, vec_ref[10:11])
            dh2_ref[part] = dh2
            e2 = dh2.astype(bf16)
            e2_ref[part] = e2
            dco_ref[part] = dot_nt(e2, wco_ref[...]).astype(bf16)
            gain_sum += sum_rows(da3 * normed)
            shift_sum += sum_rows(da3)
            e_sum += sum_rows(e2.astype(f32))
            y_sum += sum_rows(upstream)
        sums_ref[0:1] = gain_sum
        sums_ref[1:2] = shift_sum
        sums_ref[2:3] = e_sum
        sums_ref[3:4] = y_sum


def mlp_both(h1, co, dy, mid, wu, wd, bu, vec):
    rows = h1.shape[0]
    full = whole((rows, D))
    wide = pl.BlockSpec((rows, TILE_F), lambda f: (0, f))
    return call(
        mlp_kernel,
        "mlp_both",
        (FF // TILE_F,),
        (h1, co, dy, mid, wu, wd, bu, vec),
        [
            full,
            full,
            full,
            pl.BlockSpec((D, D), lambda f: (0, 4)),
            pl.BlockSpec((D, TILE_F), lambda f: (0, f)),
            pl.BlockSpec((TILE_F, D), lambda f: (f, 0)),
            pl.BlockSpec((1, TILE_F), lambda f: (0, f)),
            whole(vec.shape),
        ],
        (
            like((rows, D), bf16),
            like((rows, FF), bf16),
            like((rows, FF), bf16),
            like((rows, D), bf16),
            like((rows, D), f32),
            like((rows, D), bf16),
            like((rows, D), bf16),
            like((8, D), f32),
            like((1, FF), f32),
        ),
        (
            full,
            wide,
            wide,
            full,
            full,
            full,
            full,
            whole((8, D)),
            pl.BlockSpec((1, TILE_F), lambda f: (0, f)),
        ),
        2 * rows * D * (4 * FF + 2 * D),
        scratch=[pltpu.VMEM((rows, D), f32)] * 3,
        exps=rows * FF,
    )


def mid_back_kernel(
    dcq_ref, dh2_ref, h1_ref, wq_ref, wo_ref, vec_ref, dh1_ref, e1_ref, do_ref, sums_ref
):
    @pl.when(pl.program_id(0) == 0)
    def _():
        sums_ref[...] = jnp.zeros_like(sums_ref)

    da2 = dot_nt(dcq_ref[...], wq_ref[...])
    normed, inverse = normed_of(h1_ref[...])
    dh1 = dh2_ref[...] + norm_back(da2, normed, inverse, vec_ref[9:10])
    dh1_ref[...] = dh1
    e1 = dh1.astype(bf16)
    e1_ref[...] = e1
    do_ref[...] = dot_nt(e1, wo_ref[...]).astype(bf16)
    sums_ref[0:1] += sum_rows(da2 * normed)
    sums_ref[1:2] += sum_rows(da2)
    sums_ref[2:3] += sum_rows(dcq_ref[...].astype(f32))
    sums_ref[3:4] += sum_rows(e1.astype(f32))


def mid_back(dcq, dh2, h1, mid, vec):
    rows = h1.shape[0]
    block = pl.BlockSpec((ROWS, D), lambda r: (r, 0))
    return call(
        mid_back_kernel,
        "mid_back",
        (rows // ROWS,),
        (dcq, dh2, h1, mid, mid, vec),
        [
            block,
            block,
            block,
            pl.BlockSpec((D, D), lambda r: (0, 3)),
            pl.BlockSpec((D, D), lambda r: (0, 2)),
            whole(vec.shape),
        ],
        (
            like((rows, D), f32),
            like((rows, D), bf16),
            like((rows, D), bf16),
            like((8, D), f32),
        ),
        (block, block, block, whole((8, D))),
        4 * rows * D * D,
    )


def token_back_kernel(dqkv_ref, dh1_ref, x_ref, w_ref, vec_ref, dx_ref, sums_ref, qkv_sums_ref):
    @pl.when(pl.program_id(0) == 0)
    def _():
        sums_ref[...] = jnp.zeros_like(sums_ref)
        qkv_sums_ref[...] = jnp.zeros_like(qkv_sums_ref)

    da1 = dot_nt(dqkv_ref[...], w_ref[...])
    normed, inverse = normed_of(x_ref[...].astype(f32))
    dx_ref[...] = dh1_ref[...] + norm_back(da1, normed, inverse, vec_ref[8:9])
    sums_ref[0:1] += sum_rows(da1 * normed)
    sums_ref[1:2] += sum_rows(da1)
    qkv_sums_ref[...] += sum_rows(dqkv_ref[...].astype(f32))


def token_back(dqkv, dh1, x, weight, vec):
    rows = x.shape[0]
    block = pl.BlockSpec((ROWS, D), lambda r: (r, 0))
    return call(
        token_back_kernel,
        "token_back",
        (rows // ROWS,),
        (dqkv, dh1, x, weight, vec),
        [
            pl.BlockSpec((ROWS, 3 * D), lambda r: (r, 0)),
            block,
            block,
            pl.BlockSpec((D, 3 * D), lambda r: (0, 0)),
            whole(vec.shape),
        ],
        (like((rows, D), f32), like((8, D), f32), like((1, 3 * D), f32)),
        (block, whole((8, D)), whole((1, 3 * D))),
        6 * rows * D * D,
    )


def neighbour_kernel(dkv_ref, w_ref, dn_ref):
    dn_ref[...] = dot_nt(dkv_ref[...], w_ref[...])


def neighbour_back(dckv, mid):
    rows = dckv.shape[0]
    return call(
        neighbour_kernel,
        "neighbour_back",
        (rows // ROWS,),
        (dckv, mid),
        [
            pl.BlockSpec((ROWS, 2 * D), lambda r: (r, 0)),
            pl.BlockSpec((D, 2 * D), lambda r: (0, 0)),
        ],
        like((rows, D), f32),
        pl.BlockSpec((ROWS, D), lambda r: (r, 0)),
        4 * rows * D * D,
    )


def weight_grad(left, right):
    return dot_tn(left, right).astype(bf16)


def grad_kernel(sizes, stack, me_ref, left_ref, right_ref, *refs):
    keep_ref, send_ref, acc_ref = refs[-3:]
    nz, ny, nx, nc = sizes
    rows = keep_ref.shape[3]
    acc_ref[...] = dot_tn(left_ref[...], right_ref[...])
    for z in range(keep_ref.shape[0]):
        at_z = lax.rem(me_ref[0] + z, nz) if keep_ref.shape[0] > 1 else 0
        for y in range(ny):
            for x in range(nx):
                at = at_z * ny + lax.rem(me_ref[1] + y, ny)
                at = (at * nx + lax.rem(me_ref[2] + x, nx)) * nc
                for out_ref, core in ((keep_ref, me_ref[3]), (send_ref, nc - 1 - me_ref[3])):
                    for m in range(stack):
                        row = pl.multiple_of(((at + core) * stack + m) * rows, 8)
                        part = acc_ref[pl.ds(row, rows), :]
                        out_ref[z, y, x, :, m * D : (m + 1) * D] = part.astype(bf16)


def grad_blocks(left, right, sizes, me, width, column=0, earlier=()):
    nz, ny, nx, _ = sizes
    rows = D // math.prod(sizes)
    stack = left.shape[1] // D
    count = left.shape[0]
    if stack == 1:
        grid = (right.shape[1] // D,)
        left_spec = whole(left.shape)
        right_spec = pl.BlockSpec((count, D), lambda j, _: (0, j))
        block = pl.BlockSpec((nz, ny, nx, rows, D), lambda j, _: (0, 0, 0, 0, column // D + j))
        held = D
    else:
        grid = (nz,)
        held = left.shape[1] // nz
        left_spec = pl.BlockSpec(
            (count, held), lambda z, me_ref: (0, lax.rem(me_ref[0] + z, nz))
        )
        right_spec = whole(right.shape)
        block = pl.BlockSpec(
            (1, ny, nx, rows, stack * D), lambda z, _: (z, 0, 0, 0, column // (stack * D))
        )
    shape = like((nz, ny, nx, rows, width), bf16)
    earlier = list(earlier)
    return call(
        functools.partial(grad_kernel, sizes, stack),
        "grad_blocks",
        grid,
        [left, right] + earlier,
        [left_spec, right_spec] + [pl.BlockSpec(memory_space=pl.ANY)] * len(earlier),
        [shape, shape],
        [block, block],
        0,
        scratch=[pltpu.VMEM((held, D), f32)],
        scalars=(me,),
        aliases={3: 0, 4: 1} if earlier else {},
    )


def grads(pairs, sizes, me, width, column=0, earlier=()):
    for left, right in pairs:
        earlier = grad_blocks(left, right, sizes, me, width, column, earlier)
        column += left.shape[1] // D * right.shape[1]
    return earlier


def local(
    sizes,
    tokens,
    neighbours,
    block_lengths,
    chosen,
    cotangent,
    w_qkv,
    w_out,
    w_cross_q,
    w_cross_kv,
    w_cross_out,
    w_up,
    w_down,
    biases,
    up_bias,
    norm_gains,
    norm_shifts,
):
    me = coords_of(lax.axis_index("fsdp"), sizes)
    me_array = jnp.stack(me).astype(jnp.int32)
    shard = w_qkv.shape[0]
    small = jnp.concatenate(
        [biases.T, norm_gains.T, norm_shifts.T, up_bias.reshape(shard, FF // D)], 1
    )
    small = jnp.pad(small, ((0, 0), (0, LANES - SMALL)))
    first = jnp.concatenate([w_qkv, small], 1)
    middle = jnp.concatenate([w_cross_kv, w_out, w_cross_q, w_cross_out], 1)
    quarters = jnp.split(w_down, FF // D, 0)
    last = jnp.concatenate(quarters + [w_up], 1)
    cosine, sine = rotary_tables()
    picks = chosen.reshape(chosen.shape[0], SPANS * K_NBR)

    first_own = gather_z(first, sizes)
    first_side = gather_side(first_own, sizes)
    middle_own = gather_z(after(middle, first_own), sizes)
    first_pieces = near_pieces(first_own, first_side)
    first_corner = gather_corner(first_side, sizes)
    first_core = gather_core(first_pieces, sizes)
    middle_own = after(middle_own, first_corner)
    middle_side = gather_side(middle_own, sizes)
    last_own = gather_z(after(last, middle_own), sizes)
    first_pieces.update(first_corner)
    first_core.update(gather_core(first_corner, sizes))
    first_core.update({(0,) + key: held for key, held in first_pieces.items()})
    qkv_weight = place(first_core, sizes, me_array)
    gathered = qkv_weight[:, 3 * D :]
    vec = gathered[:, :16].T.astype(f32)
    up_shift = gathered[:, 14:SMALL].reshape(1, FF).astype(f32)

    a1, qkv = qkv_project(after(tokens, middle_own), qkv_weight, vec, cosine, sine)
    middle_side = after(middle_side, qkv)
    middle_pieces = near_pieces(middle_own, middle_side)
    middle_corner = gather_corner(middle_side, sizes)
    middle_core = gather_core(middle_pieces, sizes)
    o, lse = self_attend(block_lengths, after(qkv, middle_side, last_own))
    last_side = gather_side(after(last_own, o), sizes)
    middle_corner, middle_core = after((middle_corner, middle_core), o)
    middle_core.update(gather_core(middle_corner, sizes))
    middle_pieces.update(middle_corner)
    middle_core.update({(0,) + key: held for key, held in middle_pieces.items()})
    mid = place(middle_core, sizes, me_array)
    ckv = ckv_project(neighbours, mid, vec)
    h1, a2, cq = mid_forward(o, tokens, mid, vec)
    last_side = after(last_side, cq, ckv)
    last_pieces = near_pieces(last_own, last_side)
    last_corner = gather_corner(last_side, sizes)
    last_core = gather_core(last_pieces, sizes)
    co = cross_attend(picks, after(cq, last_side), ckv)
    last_corner, last_core = after((last_corner, last_core), co)
    last_core.update(gather_core(last_corner, sizes))
    last_pieces.update(last_corner)
    last_core.update({(0,) + key: held for key, held in last_pieces.items()})
    down_weight, up_weight = place(last_core, sizes, me_array, split=True)

    a3, g, du, output, dh2, e2, dco, sums3, grad_bu = mlp_both(
        h1, co, cotangent, mid, up_weight, down_weight, up_shift, vec
    )

    aligned = shard % 8 == 0

    def group(pairs, split=False):
        if aligned:
            width = sum(a.shape[1] // D * b.shape[1] for a, b in pairs)
            return grads(pairs, sizes, me_array, width)
        return spread([weight_grad(a, b) for a, b in pairs], sizes, me_array, split)

    last_kept, last_sent = group([(g, cotangent), (a3, du)], True)
    last_got = shift(last_sent, sizes, 3, 1)
    dcq, dckv, value_sums = cross_back(picks, cq, ckv, after(dco, last_sent))
    last_parts = fold_core(last_kept, after(last_got, dcq), sizes, me_array)
    last_got = send_side(last_parts, sizes)
    dh1, e1, do, sums2 = mid_back(after(dcq, last_parts), dh2, h1, mid, vec)
    middle_kept, middle_sent = group(
        [(after(neighbours, last_parts), dckv), (o, e1), (a2, dcq), (co, e2)]
    )
    middle_got = shift(middle_sent, sizes, 3, 1)
    last_parts = fold_side(after(last_got, middle_sent), sizes)
    last_got = send_corner(last_parts, sizes)
    do = after(do, middle_sent, last_parts)
    dqkv = self_back(0, block_lengths, qkv, do, lse, cosine, sine)
    last_parts = fold_corner(after(last_got, dqkv), sizes)
    last_got = send_z(last_parts, sizes)
    middle_parts = fold_core(middle_kept, after(middle_got, dqkv), sizes, me_array)
    middle_got = send_side(middle_parts, sizes)
    do = after(do, last_parts, middle_parts)
    dqkv = self_back(1, block_lengths, qkv, do, lse, cosine, sine, dqkv)
    middle_parts = fold_side(after(middle_got, dqkv), sizes)
    middle_got = send_corner(middle_parts, sizes)
    first_kept, first_sent = group([(after(a1, middle_parts), dqkv)])
    first_got = shift(first_sent, sizes, 3, 1)
    down_sum, up_sum = fold_z(after(last_got, first_sent), ((0, FF, FF // D), (FF, FF, 1)))
    middle_parts = fold_corner(after(middle_got, down_sum), sizes)
    middle_got = send_z(middle_parts, sizes)
    dqkv = after(dqkv, first_sent, middle_parts)
    token_grad, sums1, qkv_sums = token_back(dqkv, dh1, tokens, qkv_weight, vec)

    rows = jnp.concatenate(
        [
            qkv_sums.reshape(3, D),
            sums2[3:4],
            sums2[2:3],
            sum_rows(value_sums[::8]),
            sums3[2:4],
            sums1[0:1],
            sums2[0:1],
            sums3[0:1],
            sums1[1:2],
            sums2[1:2],
            sums3[1:2],
        ],
        0,
    )
    small_grad = jnp.concatenate([rows.T, grad_bu.reshape(D, FF // D)], 1)
    small_grad = jnp.pad(small_grad, ((0, 0), (0, LANES - SMALL)))
    small_got = shift(small_grad, sizes, 3, 1)
    first_parts = fold_core(
        first_kept, after(first_got, token_grad), sizes, me_array, (small_grad, small_got)
    )
    first_got = send_side(first_parts, sizes)
    neighbour_grad = neighbour_back(after(dckv, first_parts), mid)
    first_parts = fold_side(after(first_got, neighbour_grad), sizes)
    first_got = send_corner(first_parts, sizes)
    kv_sum, out_sum, cq_sum, co_sum = fold_z(
        after(middle_got, first_parts),
        ((0, 2 * D, 1), (2 * D, D, 1), (3 * D, D, 1), (4 * D, D, 1)),
    )
    first_got = send_z(fold_corner(after(first_got, kv_sum), sizes), sizes)
    first_sum, small_sum = fold_z(first_got, ((0, 3 * D, 1), (3 * D, LANES, 1)))

    return (
        output,
        token_grad,
        neighbour_grad,
        first_sum,
        out_sum,
        cq_sum,
        kv_sum,
        co_sum,
        up_sum,
        down_sum,
        small_sum[:, :8].T,
        small_sum[:, 14:SMALL].reshape(-1),
        small_sum[:, 8:11].T,
        small_sum[:, 11:14].T,
    )


def solution(mesh):
    rowwise, columnwise = P("fsdp", None), P(None, "fsdp")
    return jax.shard_map(
        functools.partial(local, geometry(mesh.shape["fsdp"])),
        mesh=mesh,
        in_specs=(rowwise,) * 3
        + (P("fsdp", None, None),)
        + (rowwise,) * 8
        + (columnwise, P("fsdp"), columnwise, columnwise),
        out_specs=(rowwise,) * 10 + (columnwise, P("fsdp"), columnwise, columnwise),
        check_vma=False,
    )
```

```python
import functools
import math

import jax
import jax.numpy as jnp
import numpy as np
from jax import lax
from jax.experimental import pallas as pl
from jax.experimental.pallas import tpu as pltpu
from jax.sharding import PartitionSpec as P

D = 768
HEADS = 12
HEAD_DIM = 64
FF = 3072
SEQ_LEN = 512
SPAN = 64
SPANS = 8
NBR_LEN = 128
K_NBR = 2
POOL = 4
PAIRS = HEADS // 2
LANES = 128
ROWS = 256
SMALL = 18
TILE_F = 768
QKV_TILE = 384
MLP_ROWS = 512
EDGE_ROWS = 256
STEP = 32
WIDE = 2
SELF_WIDE = 2

epsilon = 1e-05
rope_base = 10000.0
gelu_coeff = 0.044715
scale = HEAD_DIM ** (-0.5)
f32 = jnp.float32
bf16 = jnp.bfloat16
PACE = 1e9
WORK = {
    "place": 6,
    "qkv_project": 11,
    "self_attend": 12,
    "mid_forward": 8,
    "ckv_project": 6,
    "cross_attend": 8,
    "mlp_both": 38,
    "grad_blocks": 6,
    "many_grads": 13,
    "cross_back": 20,
    "fold_core": 5,
    "fold_side": 4,
    "fold_corner": 2,
    "fold_z": 2,
    "mid_back": 9,
    "self_back": 15,
    "token_back": 10,
    "neighbour_back": 6,
    "spread": 5,
}


def cost_of(name):
    return pl.CostEstimate(flops=int(WORK[name] * PACE), transcendentals=0, bytes_accessed=0)


def geometry(count):
    side = round((count / 4) ** (1 / 3))
    sizes = (2 * side, side, side, 2)
    assert math.prod(sizes) == count
    return sizes


def coords_of(index, sizes):
    found = []
    for size in reversed(sizes):
        found.append(index % size)
        index = index // size
    return tuple(reversed(found))


def index_of(coords, sizes):
    index = 0
    for coord, size in zip(coords, sizes):
        index = index * size + coord
    return index


def shift_pairs(sizes, axis, step):
    pairs = []
    for source in range(math.prod(sizes)):
        coords = list(coords_of(source, sizes))
        coords[axis] = (coords[axis] + step) % sizes[axis]
        pairs.append((source, index_of(coords, sizes)))
    return pairs


def shift(values, sizes, axis, step):
    return lax.ppermute(values, "fsdp", shift_pairs(sizes, axis, step))


def after(values, *anchors):
    return lax.optimization_barrier((values, anchors))[0]


def gather_z(block, sizes):
    return jnp.stack([block] + [shift(block, sizes, 0, d) for d in range(1, sizes[0])])


def gather_side(own, sizes):
    along_x = {d: shift(own, sizes, 2, d) for d in range(1, sizes[2])}
    along_y = {e: shift(own, sizes, 1, e) for e in range(1, sizes[1])}
    return along_x, along_y


def gather_corner(side, sizes):
    along_x, along_y = side
    corner = {}
    for d, first in along_x.items():
        for e, second in along_y.items():
            half = first.shape[-1] // 2
            corner[e, d] = (
                shift(first[..., :half], sizes, 1, e),
                shift(second[..., half:], sizes, 2, d),
            )
    return corner


def gather_core(pieces, sizes):
    return {
        (c,) + key: tuple(shift(part, sizes, 3, c) for part in held)
        for key, held in pieces.items()
        for c in range(1, sizes[3])
    }


def near_pieces(own, side):
    pieces = {(0, 0): (own,)}
    pieces.update({(0, d): (part,) for d, part in side[0].items()})
    pieces.update({(e, 0): (part,) for e, part in side[1].items()})
    return pieces


def place_kernel(keys, counts, sizes, split, me_ref, *refs):
    outs = refs[sum(counts) :]
    at = 0
    for (c, e, d), count in zip(keys, counts):
        y = lax.rem(me_ref[1] - e + sizes[1], sizes[1])
        x = lax.rem(me_ref[2] - d + sizes[2], sizes[2])
        k = lax.rem(me_ref[3] - c + sizes[3], sizes[3])
        slot = (y * sizes[2] + x) * sizes[3] + k
        held = refs[at : at + count]
        rows, width = held[0].shape[1:]
        width = width * count
        half = width // 2
        if split:
            low, high = held if count == 2 else (held[0], held[0])
            for m in range(FF // D):
                outs[0][0, slot, m * rows : (m + 1) * rows] = low[0, :, m * D : (m + 1) * D]
            outs[1][0, slot] = high[0, :, 0 if count == 2 else half :]
        elif count == 1:
            outs[0][0, slot] = held[0][0]
        else:
            outs[0][0, slot, :, :half] = held[0][0]
            outs[0][0, slot, :, half:] = held[1][0]
        at += count


def place(pieces, sizes, me, split=False):
    keys = sorted(pieces)
    counts = [len(pieces[key]) for key in keys]
    arrays = [part for key in keys for part in pieces[key]]
    rows, width = pieces[0, 0, 0][0].shape[1:]
    nz = sizes[0]
    inner = sizes[1] * sizes[2] * sizes[3]
    shapes = [(rows * (FF // D), D), (rows, FF)] if split else [(rows, width)]

    def source(z, me_ref):
        return (lax.rem(me_ref[0] - z + nz, nz), 0, 0)

    outs = pl.pallas_call(
        functools.partial(place_kernel, keys, counts, sizes, split),
        out_shape=[like((nz, inner) + shape, bf16) for shape in shapes],
        grid_spec=pltpu.PrefetchScalarGridSpec(
            num_scalar_prefetch=1,
            grid=(nz,),
            in_specs=[pl.BlockSpec((1,) + a.shape[1:], source) for a in arrays],
            out_specs=[
                pl.BlockSpec((1, inner) + shape, lambda z, me_ref: (z, 0, 0, 0)) for shape in shapes
            ],
        ),
        cost_estimate=cost_of("place"),
        name="place",
    )(me, *arrays)
    outs = [out.reshape(nz * inner * out.shape[2], out.shape[3]) for out in outs]
    return outs if split else outs[0]


def spread_kernel(sizes, split, me_ref, *refs):
    keep_ref, send_ref = refs[-2:]
    ny, nx, nc = sizes[1:]
    for ry in range(ny):
        for rx in range(nx):
            y, x = lax.rem(me_ref[1] + ry, ny), lax.rem(me_ref[2] + rx, nx)
            base = (y * nx + x) * nc
            for out_ref, core in ((keep_ref, me_ref[3]), (send_ref, 1 - me_ref[3])):
                column = 0
                rows = out_ref.shape[3]
                for at, ref in enumerate(refs[:-2]):
                    width = ref.shape[3]
                    if split and at == 0:
                        for m in range(FF // D):
                            part = ref[0, base + core, m * rows : (m + 1) * rows]
                            out_ref[0, ry, rx, :, column + m * D : column + (m + 1) * D] = part
                        column += FF
                    else:
                        out_ref[0, ry, rx, :, column : column + width] = ref[0, base + core]
                        column += width


def spread(grads, sizes, me, split=False):
    nz, ny, nx, nc = sizes
    inner = ny * nx * nc
    rows = D // math.prod(sizes)
    blocks = [g.reshape(nz, inner, g.shape[0] // (nz * inner), g.shape[1]) for g in grads]
    width = sum(b.shape[2] * b.shape[3] for b in blocks) // rows
    kind = grads[0].dtype
    shape = like((nz, ny, nx, rows, width), kind)
    block = pl.BlockSpec((1, ny, nx, rows, width), lambda z, me_ref: (z, 0, 0, 0, 0))

    def source(z, me_ref):
        return (lax.rem(me_ref[0] + z, nz), 0, 0, 0)

    return pl.pallas_call(
        functools.partial(spread_kernel, sizes, split),
        out_shape=[shape, shape],
        grid_spec=pltpu.PrefetchScalarGridSpec(
            num_scalar_prefetch=1,
            grid=(nz,),
            in_specs=[pl.BlockSpec((1,) + b.shape[1:], source) for b in blocks],
            out_specs=[block, block],
        ),
        cost_estimate=cost_of("spread"),
        name="spread",
    )(me, *blocks)


def plus(first, *others):
    total = first.astype(f32)
    for other in others:
        total = total + other.astype(f32)
    return total


def fold_core_kernel(sizes, half, count, me_ref, *refs):
    nz, ny, nx, nc = sizes
    kept_ref, got_ref = refs[:2]
    width = kept_ref.shape[-1]
    outs = refs[count:]
    z = pl.program_id(0)
    for y in range(ny):
        for x in range(nx):
            first_ref, second_ref = outs[y], outs[ny + x]
            kind = first_ref.dtype
            total = plus(kept_ref[0, y, x], got_ref[0, y, x])
            first_ref[0, x] = total[:, :half].astype(kind)
            second_ref[0, y, :, : width - half] = total[:, half:].astype(kind)
            if count > 2:
                there = lax.rem(me_ref[1] + y, ny) * nx + lax.rem(me_ref[2] + x, nx)
                slot = there * nc + me_ref[3]
                extra = refs[2][0, slot] + refs[3][0, slot]
                second_ref[0, y, :, width - half :] = extra.astype(kind)


def fold_core(kept, got, sizes, me, small=()):
    nz, ny, nx, nc = sizes
    rows, width = kept.shape[3:]
    half = width // (2 * LANES) * LANES
    kind = kept.dtype
    small = [v.reshape(nz, ny * nx * nc, rows, LANES) for v in small]
    rest = width - half + (LANES if small else 0)
    block = pl.BlockSpec((1,) + kept.shape[1:], lambda z, _: (z, 0, 0, 0, 0))
    source = pl.BlockSpec(
        (1, ny * nx * nc, rows, LANES), lambda z, me_ref: (lax.rem(me_ref[0] + z, nz), 0, 0, 0)
    )
    shapes = [(nx, rows, half)] * ny + [(ny, rows, rest)] * nx
    outs = call(
        functools.partial(fold_core_kernel, sizes, half, 2 + len(small)),
        "fold_core",
        (nz,),
        [kept, got] + small,
        [block, block] + [source] * len(small),
        [like((nz,) + shape, kind) for shape in shapes],
        [pl.BlockSpec((1,) + shape, lambda z, _: (z, 0, 0, 0)) for shape in shapes],
        0,
        scalars=(me,),
    )
    return outs[:ny], outs[ny:]


def send_side(parts, sizes):
    first, second = parts
    return (
        [first[0]] + [shift(first[e], sizes, 1, e) for e in range(1, sizes[1])],
        [second[0]] + [shift(second[d], sizes, 2, d) for d in range(1, sizes[2])],
    )


def fold_side_kernel(ny, nx, *refs):
    outs = refs[ny + nx :]
    for x in range(nx):
        total = plus(*[ref[0, x] for ref in refs[:ny]])
        outs[x][0] = total.astype(outs[x].dtype)
    for y in range(ny):
        total = plus(*[ref[0, y] for ref in refs[ny : ny + nx]])
        outs[nx + y][0] = total.astype(outs[nx + y].dtype)


def fold_side(got, sizes):
    nz, ny, nx, _ = sizes
    ins = list(got[0]) + list(got[1])
    shapes = [a.shape[2:] for a in (ins[0],) * nx + (ins[-1],) * ny]
    outs = call(
        functools.partial(fold_side_kernel, ny, nx),
        "fold_side",
        (nz,),
        ins,
        [pl.BlockSpec((1,) + a.shape[1:], lambda z: (z, 0, 0, 0)) for a in ins],
        [like((nz,) + shape, ins[0].dtype) for shape in shapes],
        [pl.BlockSpec((1,) + shape, lambda z: (z, 0, 0)) for shape in shapes],
        0,
    )
    return outs[:nx], outs[nx:]


def send_corner(parts, sizes):
    first, second = parts
    return (
        [first[0]] + [shift(first[d], sizes, 2, d) for d in range(1, sizes[2])],
        [second[0]] + [shift(second[e], sizes, 1, e) for e in range(1, sizes[1])],
    )


def fold_corner_kernel(nx, ny, *refs):
    outs = refs[nx + ny :]
    half = refs[0].shape[-1]
    for z, out_ref in enumerate(outs):
        out_ref[:, :half] = plus(*[ref[z] for ref in refs[:nx]]).astype(out_ref.dtype)
        out_ref[:, half:] = plus(*[ref[z] for ref in refs[nx : nx + ny]]).astype(out_ref.dtype)


def fold_corner(got, sizes):
    nz, ny, nx, _ = sizes
    ins = list(got[0]) + list(got[1])
    shape = (ins[0].shape[1], ins[0].shape[2] + ins[-1].shape[2])
    return call(
        functools.partial(fold_corner_kernel, nx, ny),
        "fold_corner",
        (1,),
        ins,
        [whole(a.shape) for a in ins],
        [like(shape, ins[0].dtype)] * nz,
        [whole(shape)] * nz,
        0,
    )


def send_z(parts, sizes):
    return [parts[0]] + [shift(parts[z], sizes, 0, z) for z in range(1, sizes[0])]


def fold_z_kernel(parts, count, *refs):
    total = plus(*[ref[...] for ref in refs[:count]])
    rows = total.shape[0]
    for (start, width, stack), out_ref in zip(parts, refs[count:]):
        if stack == 0:
            out_ref[...] = total[:, start : start + width].T
            continue
        part = width // stack
        for m in range(stack):
            column = start + m * part
            out_ref[m * rows : (m + 1) * rows] = total[:, column : column + part]


def fold_z(got, parts):
    rows = got[0].shape[0]
    shapes = [
        (rows * stack, width // stack) if stack else (width, rows) for _, width, stack in parts
    ]
    return call(
        functools.partial(fold_z_kernel, parts, len(got)),
        "fold_z",
        (1,),
        got,
        [whole(a.shape) for a in got],
        [like(shape, f32) for shape in shapes],
        [whole(shape) for shape in shapes],
        0,
    )


def dot_nn(a, b):
    return lax.dot_general(a, b, (((1,), (0,)), ((), ())), preferred_element_type=f32)


def dot_nt(a, b):
    return lax.dot_general(a, b, (((1,), (1,)), ((), ())), preferred_element_type=f32)


def dot_tn(a, b):
    return lax.dot_general(a, b, (((0,), (0,)), ((), ())), preferred_element_type=f32)


def normed_of(values):
    average = jnp.mean(values, -1, keepdims=True)
    centred = values - average
    inverse = lax.rsqrt(jnp.mean(centred * centred, -1, keepdims=True) + epsilon)
    return centred * inverse, inverse


def norm_back(incoming, normed, inverse, gain):
    scaled = incoming * gain
    inner = (
        scaled
        - jnp.mean(scaled, -1, keepdims=True)
        - normed * jnp.mean(scaled * normed, -1, keepdims=True)
    )
    return inner * inverse


def sum_rows(values):
    return jnp.sum(values, 0, keepdims=True)


def lane_halves(kind):
    lane = lax.broadcasted_iota(jnp.int32, (1, LANES), 1)
    low = jnp.where(lane < HEAD_DIM, 1.0, 0.0)
    return (low.astype(kind), (1.0 - low).astype(kind))


def turn(tile, cosine, sine):
    lane = lax.broadcasted_iota(jnp.int32, (1, LANES), 1)
    half_dim = HEAD_DIM // 2
    lower = (lane & half_dim) == 0
    other = jnp.where(
        lower, pltpu.roll(tile, LANES - half_dim, 1), pltpu.roll(tile, half_dim, 1)
    )
    return tile * cosine + other * sine


def rotary_tables():
    half_dim = HEAD_DIM // 2
    inverse = np.exp(np.arange(half_dim) * (-2.0 * math.log(rope_base) / HEAD_DIM))
    coarse = np.arange(0, SEQ_LEN, STEP)[:, None, None] * inverse
    fine = np.arange(STEP)[None, :, None] * inverse

    def pick(values, signs=(1.0, 1.0, 1.0, 1.0)):
        return jnp.asarray(np.concatenate([s * values for s in signs], -1), f32)

    signs = (-1.0, 1.0, -1.0, 1.0)
    cos_a, sin_a = pick(np.cos(coarse)), pick(np.sin(coarse))
    cos_b, sin_b = pick(np.cos(fine)), pick(np.sin(fine))
    cosine = cos_a * cos_b - sin_a * sin_b
    sine = pick(np.sin(coarse), signs) * cos_b + cos_a * pick(np.sin(fine), signs)
    return cosine.reshape(SEQ_LEN, LANES), sine.reshape(SEQ_LEN, LANES)


def call(
    kernel,
    name,
    grid,
    ins,
    in_specs,
    outs,
    out_specs,
    flops,
    scratch=(),
    scalars=(),
    exps=0,
    aliases={},
):
    return pl.pallas_call(
        kernel,
        out_shape=outs,
        grid_spec=pltpu.PrefetchScalarGridSpec(
            num_scalar_prefetch=len(scalars),
            grid=grid,
            in_specs=in_specs,
            out_specs=out_specs,
            scratch_shapes=scratch,
        ),
        compiler_params=pltpu.CompilerParams(
            dimension_semantics=("arbitrary",) * len(grid), vmem_limit_bytes=60 << 20
        ),
        input_output_aliases=aliases,
        cost_estimate=cost_of(name),
        name=name,
    )(*scalars, *ins)


def like(shape, kind):
    return jax.ShapeDtypeStruct(shape, kind)


def whole(shape):
    return pl.BlockSpec(shape, lambda *_: (0,) * len(shape))


def qkv_kernel(x_ref, w_ref, vec_ref, cos_ref, sin_ref, a1_ref, out_ref):
    part = pl.program_id(0)
    rows = x_ref.shape[0]
    width = w_ref.shape[1]

    @pl.when(part == 0)
    def _():
        def enter(i, _):
            part = pl.ds(pl.multiple_of(i * ROWS, ROWS), ROWS)
            normed, _ = normed_of(x_ref[part].astype(f32))
            a1_ref[part] = (normed * vec_ref[8:9, :D] + vec_ref[11:12, :D]).astype(bf16)
            return 0

        lax.fori_loop(0, rows // ROWS, enter, 0)

    column = pl.multiple_of(lax.rem(part, D // width) * width, width)
    bias = vec_ref[pl.ds(part // (D // width), 1), pl.ds(column, width)]
    for r in range(0, rows, ROWS):
        mixed = dot_nn(a1_ref[r : r + ROWS], w_ref[...]) + bias
        at = r % SEQ_LEN
        cosine, sine = cos_ref[0, at : at + ROWS], sin_ref[0, at : at + ROWS]
        for c in range(0, width, LANES):
            turned = turn(mixed[:, c : c + LANES], cosine, sine)
            out_ref[r : r + ROWS, c : c + LANES] = turned.astype(bf16)


def qkv_project(x, weight, vec, cosine, sine):
    rows = x.shape[0]
    width = QKV_TILE
    tables = (
        jnp.stack([cosine, jnp.ones_like(cosine)]),
        jnp.stack([sine, jnp.zeros_like(sine)]),
    )
    table = pl.BlockSpec((1, SEQ_LEN, LANES), lambda j: (j // (2 * D // width), 0, 0))
    return call(
        qkv_kernel,
        "qkv_project",
        (3 * D // width,),
        (x, weight, vec) + tables,
        [
            whole((rows, D)),
            pl.BlockSpec((D, width), lambda j: (0, j)),
            whole(vec.shape),
            table,
            table,
        ],
        (like((rows, D), bf16), like((rows, 3 * D), bf16)),
        (whole((rows, D)), pl.BlockSpec((rows, width), lambda j: (0, j))),
        2 * rows * D * 3 * D,
    )


def blocks_of(lengths_ref, seq, positions):
    end, found = 0, jnp.zeros(positions.shape, jnp.int32)
    for i in range(3):
        end = end + lengths_ref[seq, i]
        found = found + (positions >= end).astype(jnp.int32)
    return found


def mask_features(lengths_ref, seq):
    rows = lax.broadcasted_iota(jnp.int32, (SEQ_LEN, LANES), 0)
    slot = lax.broadcasted_iota(jnp.int32, (SEQ_LEN, LANES), 1) & (HEAD_DIM - 1)
    block = blocks_of(lengths_ref, seq, rows)
    later = (slot > block) & (slot < 4)
    return (
        jnp.where(later, -1e30, 0.0).astype(bf16),
        jnp.where(slot == block, 1.0, 0.0).astype(bf16),
    )


def self_kernel(lengths_ref, q_ref, k_ref, v_ref, o_ref, lse_ref, fq_ref, fk_ref):
    seq = pl.program_id(0)

    @pl.when(pl.program_id(1) == 0)
    def _():
        fq_ref[...], fk_ref[...] = mask_features(lengths_ref, seq)

    keep = lane_halves(bf16)
    low_lane = lax.broadcasted_iota(jnp.int32, (1, LANES), 1) < HEAD_DIM
    ones = jnp.ones((SEQ_LEN, LANES), bf16)
    starts = range(0, SEQ_LEN, ROWS)
    for c in range(0, q_ref.shape[1], LANES):
        lanes = slice(c, c + LANES)
        query, key = q_ref[:, lanes] * scale, k_ref[:, lanes]
        queries = [query * keep[h] + fq_ref[...] * keep[1 - h] for h in range(2)]
        keys = [key * keep[h] + fk_ref[...] * keep[1 - h] for h in range(2)]
        value = jnp.concatenate([v_ref[:, lanes], ones], 1)
        parts = [(r, h) for r in starts for h in range(2)]
        scores = [dot_nt(queries[h][r : r + ROWS], keys[h]) for r, h in parts]
        tops = [jnp.max(s, -1, keepdims=True) for s in scores]
        weights = [jnp.exp(s - top).astype(bf16) for s, top in zip(scores, tops)]
        outs = [dot_nn(w, value) for w in weights]
        for i, r in enumerate(starts):
            first, second = outs[2 * i], outs[2 * i + 1]
            total = jnp.where(low_lane, first[:, LANES:], second[:, LANES:])
            out = jnp.where(low_lane, first[:, :LANES], second[:, :LANES]) / total
            o_ref[r : r + ROWS, lanes] = out.astype(bf16)
            other = jnp.where(low_lane, second[:, LANES:], first[:, LANES:])
            top = jnp.where(low_lane, tops[2 * i + 1], tops[2 * i])
            lse_ref[r : r + ROWS, lanes] = top + jnp.log(other)


def self_attend(lengths, qkv):
    rows = qkv.shape[0]
    seqs = rows // SEQ_LEN
    width = SELF_WIDE * LANES
    steps = PAIRS // SELF_WIDE

    def at(offset):
        return pl.BlockSpec((SEQ_LEN, width), lambda s, p, _: (s, offset + p))

    return call(
        self_kernel,
        "self_attend",
        (seqs, steps),
        (qkv, qkv, qkv),
        [at(0), at(steps), at(2 * steps)],
        (like((rows, D), bf16), like((rows, D), f32)),
        (at(0), at(0)),
        4 * rows * SEQ_LEN * D,
        scratch=[pltpu.VMEM((SEQ_LEN, LANES), bf16)] * 2,
        scalars=(lengths,),
        exps=rows * SEQ_LEN * HEADS,
    )


def self_back_kernel(
    seq, lengths_ref, q_ref, k_ref, v_ref, do_ref, lse_ref, cos_ref, sin_ref, *rest
):
    pair = pl.program_id(0)
    out_ref, fq_ref, fk_ref = rest[-3:]
    slot = lax.broadcasted_iota(jnp.int32, (1, LANES), 1) & (HEAD_DIM - 1)

    @pl.when(pair == 0)
    def _():
        features = mask_features(lengths_ref, seq)
        fq_ref[...] = features[0]
        fk_ref[...] = features[1] + jnp.where((slot >= 4) & (slot < 7), 1.0, 0.0).astype(bf16)

    keep = lane_halves(bf16)
    low_lane = lax.broadcasted_iota(jnp.int32, (1, LANES), 1) < HEAD_DIM
    rest_of = -lse_ref[...]
    total = jnp.zeros_like(rest_of)
    for i in range(3):
        digit = rest_of.astype(bf16).astype(f32)
        total = jnp.where(slot == 4 + i, digit, total)
        rest_of = rest_of - digit
    features = fq_ref[...] + total.astype(bf16)
    query, key, value, upstream = q_ref[...], k_ref[...], v_ref[...], do_ref[...]
    scaled = key * scale
    heads = range(2)
    keys = [scaled * keep[h] + fk_ref[...] * keep[1 - h] for h in heads]
    queries = [query * keep[h] + features * keep[1 - h] for h in heads]
    probs = [jnp.exp(dot_nt(keys[h], queries[h])) for h in heads]
    dprobs = [dot_nt(value * keep[h], upstream) for h in heads]
    inners = [jnp.sum(p * dp, 0, keepdims=True) for p, dp in zip(probs, dprobs)]
    dscores = [
        (p * (dp - inner)).astype(bf16) for p, dp, inner in zip(probs, dprobs, inners)
    ]
    dvs = [dot_nn(p.astype(bf16), upstream) for p in probs]
    dks = [dot_nn(ds, query) for ds in dscores]
    dqs = [dot_tn(ds, key) for ds in dscores]
    cosine, sine = cos_ref[...], -sin_ref[...]
    dq = jnp.where(low_lane, dqs[0], dqs[1]) * scale
    dk = jnp.where(low_lane, dks[0], dks[1]) * scale
    dv = jnp.where(low_lane, dvs[0], dvs[1])
    for part, found in enumerate((turn(dq, cosine, sine), turn(dk, cosine, sine), dv)):
        column = pl.multiple_of((part * PAIRS + pair) * LANES, LANES)
        out_ref[:, pl.ds(column, LANES)] = found.astype(bf16)


def self_back(seq, lengths, qkv, do, lse, cosine, sine, earlier=None):
    rows = qkv.shape[0]
    block = (SEQ_LEN, LANES)

    def at(offset):
        return pl.BlockSpec(block, lambda p, _: (seq, offset + p))

    kernel = functools.partial(self_back_kernel, seq)
    ins = [qkv, qkv, qkv, do, lse, cosine, sine]
    specs = [at(0), at(PAIRS), at(2 * PAIRS), at(0), at(0), whole(block), whole(block)]
    aliases = {}
    if earlier is not None:
        ins.append(earlier)
        specs.append(pl.BlockSpec(memory_space=pl.ANY))
        aliases = {len(ins): 0}
    return call(
        kernel,
        "self_back",
        (PAIRS,),
        ins,
        specs,
        like((rows, 3 * D), bf16),
        pl.BlockSpec((SEQ_LEN, 3 * D), lambda p, _: (seq, 0)),
        10 * SEQ_LEN * SEQ_LEN * D,
        scratch=[pltpu.VMEM(block, bf16)] * 2,
        scalars=(lengths,),
        exps=SEQ_LEN * SEQ_LEN * HEADS,
        aliases=aliases,
    )


def mid_kernel(o_ref, x_ref, wo_ref, wq_ref, vec_ref, h1_ref, a2_ref, cq_ref):
    h1 = x_ref[...].astype(f32) + dot_nn(o_ref[...], wo_ref[...]) + vec_ref[3:4]
    h1_ref[...] = h1
    normed, _ = normed_of(h1)
    a2 = (normed * vec_ref[9:10] + vec_ref[12:13]).astype(bf16)
    a2_ref[...] = a2
    cq_ref[...] = (dot_nn(a2, wq_ref[...]) + vec_ref[4:5]).astype(bf16)


def mid_forward(o, x, mid, vec):
    rows = x.shape[0]
    block = pl.BlockSpec((ROWS, D), lambda r: (r, 0))
    return call(
        mid_kernel,
        "mid_forward",
        (rows // ROWS,),
        (o, x, mid, mid, vec),
        [
            block,
            block,
            pl.BlockSpec((D, D), lambda r: (0, 2)),
            pl.BlockSpec((D, D), lambda r: (0, 3)),
            whole(vec.shape),
        ],
        (like((rows, D), f32), like((rows, D), bf16), like((rows, D), bf16)),
        (block, block, block),
        4 * rows * D * D,
    )


def ckv_kernel(n_ref, w_ref, vec_ref, out_ref):
    mixed = dot_nn(n_ref[...], w_ref[...])
    out_ref[:, :D] = mixed[:, :D].astype(bf16)
    out_ref[:, D:] = (mixed[:, D:] + vec_ref[5:6]).astype(bf16)


def ckv_project(n, mid, vec):
    rows = n.shape[0]
    return call(
        ckv_kernel,
        "ckv_project",
        (rows // ROWS,),
        (n, mid, vec),
        [
            pl.BlockSpec((ROWS, D), lambda r: (r, 0)),
            pl.BlockSpec((D, 2 * D), lambda r: (0, 0)),
            whole(vec.shape),
        ],
        like((rows, 2 * D), bf16),
        pl.BlockSpec((ROWS, 2 * D), lambda r: (r, 0)),
        4 * rows * D * D,
    )


def slots(chosen_ref, seq, span):
    found = []
    for i in range(K_NBR):
        entry = chosen_ref[seq, span * K_NBR + i]
        found.append(pl.multiple_of(entry * NBR_LEN, NBR_LEN))
    return found


def chosen_rows(ref, starts, lanes=slice(None)):
    return jnp.concatenate([ref[pl.ds(start, NBR_LEN), lanes] for start in starts], 0)


def cross_kernel(chosen_ref, q_ref, k_ref, v_ref, o_ref):
    seq = pl.program_id(0)
    keep = lane_halves(bf16)
    low_lane = lax.broadcasted_iota(jnp.int32, (1, LANES), 1) < HEAD_DIM
    starts = [slots(chosen_ref, seq, c) for c in range(SPANS)]
    spans = [slice(c * SPAN, (c + 1) * SPAN) for c in range(SPANS)]
    ones = jnp.ones((K_NBR * NBR_LEN, LANES), bf16)
    for c in range(0, q_ref.shape[1], LANES):
        lanes = slice(c, c + LANES)
        query = q_ref[:, lanes] * scale
        halves = [query * keep[h] for h in range(2)]
        both = [jnp.concatenate([half[span] for half in halves], 0) for span in spans]
        scores = [dot_nt(b, chosen_rows(k_ref, at, lanes)) for b, at in zip(both, starts)]
        tops = [jnp.max(s, -1, keepdims=True) for s in scores]
        weights = [jnp.exp(s - top).astype(bf16) for s, top in zip(scores, tops)]
        outs = [
            dot_nn(w, jnp.concatenate([chosen_rows(v_ref, at, lanes), ones], 1))
            for w, at in zip(weights, starts)
        ]
        for span, out in zip(spans, outs):
            total = jnp.where(low_lane, out[:SPAN, LANES:], out[SPAN:, LANES:])
            out = jnp.where(low_lane, out[:SPAN, :LANES], out[SPAN:, :LANES]) / total
            o_ref[span, lanes] = out.astype(bf16)


def cross_attend(chosen, cq, ckv):
    rows = cq.shape[0]
    seqs = rows // SEQ_LEN
    width = WIDE * LANES
    steps = PAIRS // WIDE

    def at(offset):
        return pl.BlockSpec((SEQ_LEN, width), lambda s, p, _: (s, offset + p))

    return call(
        cross_kernel,
        "cross_attend",
        (seqs, steps),
        (cq, ckv, ckv),
        [at(0), at(0), at(steps)],
        like((rows, D), bf16),
        at(0),
        2 * rows * SEQ_LEN * D,
        scalars=(chosen,),
        exps=rows * K_NBR * NBR_LEN * HEADS,
    )


def cross_back_kernel(
    chosen_ref, q_ref, k_ref, v_ref, do_ref, dq_ref, dkv_ref, sums_ref, dk_ref, dv_ref, acc_ref
):
    seq, pair = pl.program_id(0), pl.program_id(1)
    keep = lane_halves(bf16)
    low_lane = lax.broadcasted_iota(jnp.int32, (1, LANES), 1) < HEAD_DIM
    starts = [slots(chosen_ref, seq, c) for c in range(SPANS)]
    spans = [slice(c * SPAN, (c + 1) * SPAN) for c in range(SPANS)]

    def stacked(ref):
        halves = [ref[...] * keep[h] for h in range(2)]
        return [jnp.concatenate([half[span] for half in halves], 0) for span in spans]

    queries, upstreams = stacked(q_ref), stacked(do_ref)
    keys = [chosen_rows(k_ref, at) for at in starts]
    scores = jnp.concatenate([dot_nt(k, q) for k, q in zip(keys, queries)], 1) * scale
    dprob = jnp.concatenate(
        [dot_nt(chosen_rows(v_ref, at), up) for at, up in zip(starts, upstreams)], 1
    )
    exponent = jnp.exp(scores - jnp.max(scores, 0, keepdims=True))
    prob = exponent * (1.0 / jnp.sum(exponent, 0, keepdims=True))
    inner = jnp.sum(prob * dprob, 0, keepdims=True)
    dscore = (prob * (dprob - inner)).astype(bf16)
    prob = prob.astype(bf16)
    for c in range(SPANS):
        columns = slice(c * LANES, (c + 1) * LANES)
        dv_ref[c] = dot_nn(prob[:, columns], upstreams[c])
        dk_ref[c] = dot_nn(dscore[:, columns], queries[c])
    dqs = [
        dot_tn(dscore[:, c * LANES : (c + 1) * LANES], keys[c]) * scale for c in range(SPANS)
    ]
    for span, dq in zip(spans, dqs):
        dq_ref[span] = jnp.where(low_lane, dq[:SPAN], dq[SPAN:]).astype(bf16)
    for part, found_ref in enumerate((dk_ref, dv_ref)):
        acc_ref[...] = jnp.zeros_like(acc_ref)
        for c in range(SPANS):
            for i, start in enumerate(starts[c]):
                rows = slice(i * NBR_LEN, (i + 1) * NBR_LEN)
                acc_ref[pl.ds(start, NBR_LEN), :] += found_ref[c, rows]
        column = pl.multiple_of((part * PAIRS + pair) * LANES, LANES)
        total = acc_ref[...] * scale if part == 0 else acc_ref[...]
        rounded = total.astype(bf16)
        dkv_ref[:, pl.ds(column, LANES)] = rounded
    sums_ref[...] = jnp.broadcast_to(sum_rows(rounded.astype(f32)), sums_ref.shape)


def cross_back(chosen, cq, ckv, dco):
    rows = cq.shape[0]
    seqs = rows // SEQ_LEN
    block = (SEQ_LEN, LANES)

    def at(offset):
        return pl.BlockSpec(block, lambda s, p, _: (s, offset + p))

    return call(
        cross_back_kernel,
        "cross_back",
        (seqs, PAIRS),
        (cq, ckv, ckv, dco),
        [at(0), at(0), at(PAIRS), at(0)],
        (like((rows, D), bf16), like((rows, 2 * D), bf16), like((8 * seqs, D), f32)),
        (
            at(0),
            pl.BlockSpec((SEQ_LEN, 2 * D), lambda s, p, _: (s, 0)),
            pl.BlockSpec((8, LANES), lambda s, p, _: (s, p)),
        ),
        5 * rows * SEQ_LEN * D,
        scratch=[
            pltpu.VMEM((SPANS, K_NBR * NBR_LEN, LANES), f32),
            pltpu.VMEM((SPANS, K_NBR * NBR_LEN, LANES), f32),
            pltpu.VMEM(block, f32),
        ],
        scalars=(chosen,),
        exps=rows * K_NBR * NBR_LEN * HEADS,
    )


def gelu_pair(hidden):
    root_coeff = math.sqrt(2.0 / math.pi)
    square = hidden * hidden
    tangent = jnp.tanh(root_coeff * hidden * (1.0 + gelu_coeff * square))
    upper = 0.5 * (1.0 + tangent)
    slope = upper + (0.5 * root_coeff) * hidden * (1.0 - tangent * tangent) * (
        1.0 + (3.0 * gelu_coeff) * square
    )
    return hidden * upper, slope


def mlp_kernel(
    h1_ref,
    co_ref,
    dy_ref,
    wco_ref,
    wu_ref,
    wd_ref,
    bu_ref,
    vec_ref,
    a3_ref,
    g_ref,
    du_ref,
    out_ref,
    dh2_ref,
    e2_ref,
    dco_ref,
    sums_ref,
    dbu_ref,
    y_acc,
    da_acc,
    h2_ref,
):
    step = pl.program_id(0)
    rows = h1_ref.shape[0]
    chunks = rows // MLP_ROWS
    nothing = jnp.zeros((1, D), f32)

    def part_of(i, size=EDGE_ROWS):
        return pl.ds(pl.multiple_of(i * size, size), size)

    @pl.when(step == 0)
    def _():
        def enter(i, _):
            part = part_of(i)
            h2 = h1_ref[part] + dot_nn(co_ref[part], wco_ref[...]) + vec_ref[6:7]
            h2_ref[part] = h2
            normed, _ = normed_of(h2)
            a3_ref[part] = (normed * vec_ref[10:11] + vec_ref[13:14]).astype(bf16)
            y_acc[part] = h2 + vec_ref[7:8]
            da_acc[part] = jnp.zeros_like(h2)
            return 0

        lax.fori_loop(0, rows // EDGE_ROWS, enter, 0)

    def body(i, bias_sum):
        part = part_of(i, MLP_ROWS)
        hidden = dot_nn(a3_ref[part], wu_ref[...]) + bu_ref[...]
        dg = dot_nt(dy_ref[part], wd_ref[...])
        value, slope = gelu_pair(hidden)
        g = value.astype(bf16)
        du = (dg * slope).astype(bf16)
        g_ref[part] = g
        du_ref[part] = du
        y_acc[part] += dot_nn(g, wd_ref[...])
        da_acc[part] += dot_nt(du, wu_ref[...])
        return bias_sum + sum_rows(du.astype(f32))

    dbu_ref[...] = lax.fori_loop(0, chunks, body, jnp.zeros(dbu_ref.shape, f32))

    @pl.when(step == pl.num_programs(0) - 1)
    def _():
        def leave(i, sums):
            part = part_of(i)
            out_ref[part] = y_acc[part].astype(bf16)
            normed, inverse = normed_of(h2_ref[part])
            da3 = da_acc[part]
            upstream = dy_ref[part].astype(f32)
            dh2 = upstream + norm_back(da3, normed, inverse, vec_ref[10:11])
            dh2_ref[part] = dh2
            e2 = dh2.astype(bf16)
            e2_ref[part] = e2
            dco_ref[part] = dot_nt(e2, wco_ref[...]).astype(bf16)
            found = (da3 * normed, da3, e2.astype(f32), upstream)
            return tuple(total + sum_rows(value) for total, value in zip(sums, found))

        found = lax.fori_loop(0, rows // EDGE_ROWS, leave, (nothing,) * 4)
        for i, total in enumerate(found):
            sums_ref[i : i + 1] = total


def mlp_both(h1, co, dy, mid, wu, wd, bu, vec):
    rows = h1.shape[0]
    full = whole((rows, D))
    wide = pl.BlockSpec((rows, TILE_F), lambda f: (0, f))
    return call(
        mlp_kernel,
        "mlp_both",
        (FF // TILE_F,),
        (h1, co, dy, mid, wu, wd, bu, vec),
        [
            full,
            full,
            full,
            pl.BlockSpec((D, D), lambda f: (0, 4)),
            pl.BlockSpec((D, TILE_F), lambda f: (0, f)),
            pl.BlockSpec((TILE_F, D), lambda f: (f, 0)),
            pl.BlockSpec((1, TILE_F), lambda f: (0, f)),
            whole(vec.shape),
        ],
        (
            like((rows, D), bf16),
            like((rows, FF), bf16),
            like((rows, FF), bf16),
            like((rows, D), bf16),
            like((rows, D), f32),
            like((rows, D), bf16),
            like((rows, D), bf16),
            like((8, D), f32),
            like((1, FF), f32),
        ),
        (
            full,
            wide,
            wide,
            full,
            full,
            full,
            full,
            whole((8, D)),
            pl.BlockSpec((1, TILE_F), lambda f: (0, f)),
        ),
        2 * rows * D * (4 * FF + 2 * D),
        scratch=[pltpu.VMEM((rows, D), f32)] * 3,
        exps=rows * FF,
    )


def mid_back_kernel(
    dcq_ref, dh2_ref, h1_ref, wq_ref, wo_ref, vec_ref, dh1_ref, e1_ref, do_ref, sums_ref
):
    @pl.when(pl.program_id(0) == 0)
    def _():
        sums_ref[...] = jnp.zeros_like(sums_ref)

    da2 = dot_nt(dcq_ref[...], wq_ref[...])
    normed, inverse = normed_of(h1_ref[...])
    dh1 = dh2_ref[...] + norm_back(da2, normed, inverse, vec_ref[9:10])
    dh1_ref[...] = dh1
    e1 = dh1.astype(bf16)
    e1_ref[...] = e1
    do_ref[...] = dot_nt(e1, wo_ref[...]).astype(bf16)
    sums_ref[0:1] += sum_rows(da2 * normed)
    sums_ref[1:2] += sum_rows(da2)
    sums_ref[2:3] += sum_rows(dcq_ref[...].astype(f32))
    sums_ref[3:4] += sum_rows(e1.astype(f32))


def mid_back(dcq, dh2, h1, mid, vec):
    rows = h1.shape[0]
    block = pl.BlockSpec((ROWS, D), lambda r: (r, 0))
    return call(
        mid_back_kernel,
        "mid_back",
        (rows // ROWS,),
        (dcq, dh2, h1, mid, mid, vec),
        [
            block,
            block,
            block,
            pl.BlockSpec((D, D), lambda r: (0, 3)),
            pl.BlockSpec((D, D), lambda r: (0, 2)),
            whole(vec.shape),
        ],
        (
            like((rows, D), f32),
            like((rows, D), bf16),
            like((rows, D), bf16),
            like((8, D), f32),
        ),
        (block, block, block, whole((8, D))),
        4 * rows * D * D,
    )


def token_back_kernel(dqkv_ref, dh1_ref, x_ref, w_ref, vec_ref, dx_ref, sums_ref, qkv_sums_ref):
    @pl.when(pl.program_id(0) == 0)
    def _():
        sums_ref[...] = jnp.zeros_like(sums_ref)
        qkv_sums_ref[...] = jnp.zeros_like(qkv_sums_ref)

    da1 = dot_nt(dqkv_ref[...], w_ref[...])
    normed, inverse = normed_of(x_ref[...].astype(f32))
    dx_ref[...] = dh1_ref[...] + norm_back(da1, normed, inverse, vec_ref[8:9])
    sums_ref[0:1] += sum_rows(da1 * normed)
    sums_ref[1:2] += sum_rows(da1)
    qkv_sums_ref[...] += sum_rows(dqkv_ref[...].astype(f32))


def token_back(dqkv, dh1, x, weight, vec):
    rows = x.shape[0]
    block = pl.BlockSpec((ROWS, D), lambda r: (r, 0))
    return call(
        token_back_kernel,
        "token_back",
        (rows // ROWS,),
        (dqkv, dh1, x, weight, vec),
        [
            pl.BlockSpec((ROWS, 3 * D), lambda r: (r, 0)),
            block,
            block,
            pl.BlockSpec((D, 3 * D), lambda r: (0, 0)),
            whole(vec.shape),
        ],
        (like((rows, D), f32), like((8, D), f32), like((1, 3 * D), f32)),
        (block, whole((8, D)), whole((1, 3 * D))),
        6 * rows * D * D,
    )


def neighbour_kernel(dkv_ref, w_ref, dn_ref):
    dn_ref[...] = dot_nt(dkv_ref[...], w_ref[...])


def neighbour_back(dckv, mid):
    rows = dckv.shape[0]
    return call(
        neighbour_kernel,
        "neighbour_back",
        (rows // ROWS,),
        (dckv, mid),
        [
            pl.BlockSpec((ROWS, 2 * D), lambda r: (r, 0)),
            pl.BlockSpec((D, 2 * D), lambda r: (0, 0)),
        ],
        like((rows, D), f32),
        pl.BlockSpec((ROWS, D), lambda r: (r, 0)),
        4 * rows * D * D,
    )


def weight_grad(left, right):
    return dot_tn(left, right).astype(bf16)


def grad_kernel(sizes, stack, me_ref, left_ref, right_ref, *refs):
    keep_ref, send_ref, acc_ref = refs[-3:]
    nz, ny, nx, nc = sizes
    rows = keep_ref.shape[3]
    acc_ref[...] = dot_tn(left_ref[...], right_ref[...])
    for z in range(keep_ref.shape[0]):
        at_z = lax.rem(me_ref[0] + z, nz) if keep_ref.shape[0] > 1 else 0
        for y in range(ny):
            for x in range(nx):
                at = at_z * ny + lax.rem(me_ref[1] + y, ny)
                at = (at * nx + lax.rem(me_ref[2] + x, nx)) * nc
                for out_ref, core in ((keep_ref, me_ref[3]), (send_ref, nc - 1 - me_ref[3])):
                    for m in range(stack):
                        row = pl.multiple_of(((at + core) * stack + m) * rows, 8)
                        part = acc_ref[pl.ds(row, rows), :]
                        out_ref[z, y, x, :, m * D : (m + 1) * D] = part.astype(bf16)


def grad_blocks(left, right, sizes, me, width, column=0, earlier=()):
    nz, ny, nx, _ = sizes
    rows = D // math.prod(sizes)
    stack = left.shape[1] // D
    count = left.shape[0]
    if stack == 1:
        grid = (right.shape[1] // D,)
        left_spec = whole(left.shape)
        right_spec = pl.BlockSpec((count, D), lambda j, _: (0, j))
        block = pl.BlockSpec((nz, ny, nx, rows, D), lambda j, _: (0, 0, 0, 0, column // D + j))
        held = D
    else:
        grid = (nz,)
        held = left.shape[1] // nz
        left_spec = pl.BlockSpec(
            (count, held), lambda z, me_ref: (0, lax.rem(me_ref[0] + z, nz))
        )
        right_spec = whole(right.shape)
        block = pl.BlockSpec(
            (1, ny, nx, rows, stack * D), lambda z, _: (z, 0, 0, 0, column // (stack * D))
        )
    shape = like((nz, ny, nx, rows, width), bf16)
    earlier = list(earlier)
    return call(
        functools.partial(grad_kernel, sizes, stack),
        "grad_blocks",
        grid,
        [left, right] + earlier,
        [left_spec, right_spec] + [pl.BlockSpec(memory_space=pl.ANY)] * len(earlier),
        [shape, shape],
        [block, block],
        0,
        scratch=[pltpu.VMEM((held, D), f32)],
        scalars=(me,),
        aliases={3: 0, 4: 1} if earlier else {},
    )


def many_kernel(sizes, plan, count, me_ref, *refs):
    arrays = refs[:count]
    keep_ref, send_ref, left_buf, right_buf, acc_ref, sems = refs[count:]
    step = pl.program_id(0)

    def copies(k, slot):
        left, right, column = plan[k]
        source = arrays[right].at[:, column : column + D]
        return (
            pltpu.make_async_copy(arrays[left], left_buf.at[slot], sems.at[0, slot]),
            pltpu.make_async_copy(source, right_buf.at[slot], sems.at[1, slot]),
        )

    for k in range(len(plan)):

        @pl.when(step == max(k - 1, 0))
        def _():
            for copy in copies(k, k % 2):
                copy.start()

    slot = lax.rem(step, 2)
    for k in range(len(plan)):

        @pl.when(step == k)
        def _():
            for copy in copies(k, k % 2):
                copy.wait()

    grad_kernel(sizes, 1, me_ref, left_buf.at[slot], right_buf.at[slot], keep_ref, send_ref, acc_ref)


def many_grads(pairs, sizes, me):
    nz, ny, nx, _ = sizes
    rows = D // math.prod(sizes)
    arrays, plan = [], []
    for left, right in pairs:
        at = len(arrays)
        arrays += [left, right]
        plan += [(at, at + 1, column) for column in range(0, right.shape[1], D)]
    shape = like((nz, ny, nx, rows, len(plan) * D), bf16)
    block = pl.BlockSpec((nz, ny, nx, rows, D), lambda j, _: (0, 0, 0, 0, j))
    buffer = pltpu.VMEM((2,) + pairs[0][0].shape, bf16)
    return call(
        functools.partial(many_kernel, sizes, plan, len(arrays)),
        "many_grads",
        (len(plan),),
        arrays,
        [pl.BlockSpec(memory_space=pl.ANY)] * len(arrays),
        [shape, shape],
        [block, block],
        0,
        scratch=[buffer, buffer, pltpu.VMEM((D, D), f32), pltpu.SemaphoreType.DMA((2, 2))],
        scalars=(me,),
    )


def grads(pairs, sizes, me, width, column=0, earlier=()):
    if all(left.shape[1] == D for left, _ in pairs) and len(pairs) > 1:
        return many_grads(pairs, sizes, me)
    for left, right in pairs:
        earlier = grad_blocks(left, right, sizes, me, width, column, earlier)
        column += left.shape[1] // D * right.shape[1]
    return earlier


def local(
    sizes,
    tokens,
    neighbours,
    block_lengths,
    chosen,
    cotangent,
    w_qkv,
    w_out,
    w_cross_q,
    w_cross_kv,
    w_cross_out,
    w_up,
    w_down,
    biases,
    up_bias,
    norm_gains,
    norm_shifts,
):
    me = coords_of(lax.axis_index("fsdp"), sizes)
    me_array = jnp.stack(me).astype(jnp.int32)
    shard = w_qkv.shape[0]
    small = jnp.concatenate(
        [biases.T, norm_gains.T, norm_shifts.T, up_bias.reshape(shard, FF // D)], 1
    )
    small = jnp.pad(small, ((0, 0), (0, LANES - SMALL)))
    first = jnp.concatenate([w_qkv, small], 1)
    middle = jnp.concatenate([w_cross_kv, w_out, w_cross_q, w_cross_out], 1)
    quarters = jnp.split(w_down, FF // D, 0)
    last = jnp.concatenate(quarters + [w_up], 1)
    cosine, sine = rotary_tables()
    picks = chosen.reshape(chosen.shape[0], SPANS * K_NBR)

    first_own = gather_z(first, sizes)
    first_side = gather_side(first_own, sizes)
    middle_own = gather_z(after(middle, first_own), sizes)
    first_pieces = near_pieces(first_own, first_side)
    first_corner = gather_corner(first_side, sizes)
    first_core = gather_core(first_pieces, sizes)
    middle_own = after(middle_own, first_corner)
    middle_side = gather_side(middle_own, sizes)
    last_own = gather_z(after(last, middle_own), sizes)
    first_pieces.update(first_corner)
    first_core.update(gather_core(first_corner, sizes))
    first_core.update({(0,) + key: held for key, held in first_pieces.items()})
    qkv_weight = place(first_core, sizes, me_array)
    gathered = qkv_weight[:, 3 * D :]
    vec = gathered[:, :16].T.astype(f32)
    up_shift = gathered[:, 14:SMALL].reshape(1, FF).astype(f32)

    a1, qkv = qkv_project(after(tokens, middle_own), qkv_weight, vec, cosine, sine)
    middle_side = after(middle_side, qkv)
    middle_pieces = near_pieces(middle_own, middle_side)
    middle_corner = gather_corner(middle_side, sizes)
    middle_core = gather_core(middle_pieces, sizes)
    o, lse = self_attend(block_lengths, after(qkv, middle_side, last_own))
    last_side = gather_side(after(last_own, o), sizes)
    middle_corner, middle_core = after((middle_corner, middle_core), o)
    middle_core.update(gather_core(middle_corner, sizes))
    middle_pieces.update(middle_corner)
    middle_core.update({(0,) + key: held for key, held in middle_pieces.items()})
    mid = place(middle_core, sizes, me_array)
    ckv = ckv_project(neighbours, mid, vec)
    h1, a2, cq = mid_forward(o, tokens, mid, vec)
    last_side = after(last_side, cq, ckv)
    last_pieces = near_pieces(last_own, last_side)
    last_corner = gather_corner(last_side, sizes)
    last_core = gather_core(last_pieces, sizes)
    co = cross_attend(picks, after(cq, last_side), ckv)
    last_corner, last_core = after((last_corner, last_core), co)
    last_core.update(gather_core(last_corner, sizes))
    last_pieces.update(last_corner)
    last_core.update({(0,) + key: held for key, held in last_pieces.items()})
    down_weight, up_weight = place(last_core, sizes, me_array, split=True)

    a3, g, du, output, dh2, e2, dco, sums3, grad_bu = mlp_both(
        h1, co, cotangent, mid, up_weight, down_weight, up_shift, vec
    )

    aligned = shard % 8 == 0

    def group(pairs, split=False):
        if aligned:
            width = sum(a.shape[1] // D * b.shape[1] for a, b in pairs)
            return grads(pairs, sizes, me_array, width)
        return spread([weight_grad(a, b) for a, b in pairs], sizes, me_array, split)

    last_kept, last_sent = group([(g, cotangent), (a3, du)], True)
    last_got = shift(last_sent, sizes, 3, 1)
    dcq, dckv, value_sums = cross_back(picks, cq, ckv, after(dco, last_sent))
    last_parts = fold_core(last_kept, after(last_got, dcq), sizes, me_array)
    last_got = send_side(last_parts, sizes)
    dh1, e1, do, sums2 = mid_back(after(dcq, last_parts), dh2, h1, mid, vec)
    middle_kept, middle_sent = group(
        [(after(neighbours, last_parts), dckv), (o, e1), (a2, dcq), (co, e2)]
    )
    middle_got = shift(middle_sent, sizes, 3, 1)
    last_parts = fold_side(after(last_got, middle_sent), sizes)
    last_got = send_corner(last_parts, sizes)
    do = after(do, middle_sent, last_parts)
    dqkv = self_back(0, block_lengths, qkv, do, lse, cosine, sine)
    last_parts = fold_corner(after(last_got, dqkv), sizes)
    last_got = send_z(last_parts, sizes)
    middle_parts = fold_core(middle_kept, after(middle_got, dqkv), sizes, me_array)
    middle_got = send_side(middle_parts, sizes)
    do = after(do, last_parts, middle_parts)
    dqkv = self_back(1, block_lengths, qkv, do, lse, cosine, sine, dqkv)
    middle_parts = fold_side(after(middle_got, dqkv), sizes)
    middle_got = send_corner(middle_parts, sizes)
    first_kept, first_sent = group([(after(a1, middle_parts), dqkv)])
    first_got = shift(first_sent, sizes, 3, 1)
    down_sum, up_sum = fold_z(after(last_got, first_sent), ((0, FF, FF // D), (FF, FF, 1)))
    middle_parts = fold_corner(after(middle_got, down_sum), sizes)
    middle_got = send_z(middle_parts, sizes)
    dqkv = after(dqkv, first_sent, middle_parts)
    token_grad, sums1, qkv_sums = token_back(dqkv, dh1, tokens, qkv_weight, vec)

    rows = jnp.concatenate(
        [
            qkv_sums.reshape(3, D),
            sums2[3:4],
            sums2[2:3],
            sum_rows(value_sums[::8]),
            sums3[2:4],
            sums1[0:1],
            sums2[0:1],
            sums3[0:1],
            sums1[1:2],
            sums2[1:2],
            sums3[1:2],
        ],
        0,
    )
    small_grad = jnp.concatenate([rows.T, grad_bu.reshape(D, FF // D)], 1)
    small_grad = jnp.pad(small_grad, ((0, 0), (0, LANES - SMALL)))
    small_got = shift(small_grad, sizes, 3, 1)
    first_parts = fold_core(
        first_kept, after(first_got, token_grad), sizes, me_array, (small_grad, small_got)
    )
    first_got = send_side(first_parts, sizes)
    neighbour_grad = neighbour_back(after(dckv, first_parts), mid)
    first_parts = fold_side(after(first_got, neighbour_grad), sizes)
    first_got = send_corner(first_parts, sizes)
    kv_sum, out_sum, cq_sum, co_sum = fold_z(
        after(middle_got, first_parts),
        ((0, 2 * D, 1), (2 * D, D, 1), (3 * D, D, 1), (4 * D, D, 1)),
    )
    first_got = send_z(fold_corner(after(first_got, kv_sum), sizes), sizes)
    first_sum, small_sum = fold_z(first_got, ((0, 3 * D, 1), (3 * D, LANES, 0)))

    return (
        output,
        token_grad,
        neighbour_grad,
        first_sum,
        out_sum,
        cq_sum,
        kv_sum,
        co_sum,
        up_sum,
        down_sum,
        small_sum[:8],
        small_sum[14:SMALL].T.reshape(-1),
        small_sum[8:11],
        small_sum[11:14],
    )


def solution(mesh):
    rowwise, columnwise = P("fsdp", None), P(None, "fsdp")
    return jax.shard_map(
        functools.partial(local, geometry(mesh.shape["fsdp"])),
        mesh=mesh,
        in_specs=(rowwise,) * 3
        + (P("fsdp", None, None),)
        + (rowwise,) * 8
        + (columnwise, P("fsdp"), columnwise, columnwise),
        out_specs=(rowwise,) * 10 + (columnwise, P("fsdp"), columnwise, columnwise),
        check_vma=False,
    )
```

```python
import functools
import math

import jax
import jax.numpy as jnp
import numpy as np
from jax import lax
from jax.experimental import pallas as pl
from jax.experimental.pallas import tpu as pltpu
from jax.sharding import PartitionSpec as P

D = 768
HEADS = 12
HEAD_DIM = 64
FF = 3072
SEQ_LEN = 512
SPAN = 64
SPANS = 8
NBR_LEN = 128
K_NBR = 2
POOL = 4
PAIRS = HEADS // 2
LANES = 128
ROWS = 256
SMALL = 18
TILE_F = 768
QKV_TILE = 384
MLP_ROWS = 512
EDGE_ROWS = 256
STEP = 32
WIDE = 3
SELF_WIDE = 2

epsilon = 1e-05
rope_base = 10000.0
gelu_coeff = 0.044715
scale = HEAD_DIM ** (-0.5)
f32 = jnp.float32
bf16 = jnp.bfloat16
PACE = 1e9
WORK = {
    "place": 6,
    "qkv_project": 11,
    "self_attend": 12,
    "mid_forward": 8,
    "ckv_project": 6,
    "cross_attend": 8,
    "mlp_both": 38,
    "grad_blocks": 6,
    "many_grads": 13,
    "cross_back": 20,
    "fold_core": 5,
    "fold_side": 4,
    "fold_corner": 2,
    "fold_z": 2,
    "mid_back": 9,
    "self_back": 15,
    "token_back": 10,
    "neighbour_back": 6,
    "spread": 5,
}


def cost_of(name):
    return pl.CostEstimate(flops=int(WORK[name] * PACE), transcendentals=0, bytes_accessed=0)


def geometry(count):
    side = round((count / 4) ** (1 / 3))
    sizes = (2 * side, side, side, 2)
    assert math.prod(sizes) == count
    return sizes


def coords_of(index, sizes):
    found = []
    for size in reversed(sizes):
        found.append(index % size)
        index = index // size
    return tuple(reversed(found))


def index_of(coords, sizes):
    index = 0
    for coord, size in zip(coords, sizes):
        index = index * size + coord
    return index


def shift_pairs(sizes, axis, step):
    pairs = []
    for source in range(math.prod(sizes)):
        coords = list(coords_of(source, sizes))
        coords[axis] = (coords[axis] + step) % sizes[axis]
        pairs.append((source, index_of(coords, sizes)))
    return pairs


def shift(values, sizes, axis, step):
    return lax.ppermute(values, "fsdp", shift_pairs(sizes, axis, step))


def after(values, *anchors):
    return lax.optimization_barrier((values, anchors))[0]


def gather_z(block, sizes):
    return jnp.stack([block] + [shift(block, sizes, 0, d) for d in range(1, sizes[0])])


def gather_side(own, sizes):
    along_x = {d: shift(own, sizes, 2, d) for d in range(1, sizes[2])}
    along_y = {e: shift(own, sizes, 1, e) for e in range(1, sizes[1])}
    return along_x, along_y


def gather_corner(side, sizes):
    along_x, along_y = side
    corner = {}
    for d, first in along_x.items():
        for e, second in along_y.items():
            half = first.shape[-1] // 2
            corner[e, d] = (
                shift(first[..., :half], sizes, 1, e),
                shift(second[..., half:], sizes, 2, d),
            )
    return corner


def gather_core(pieces, sizes):
    return {
        (c,) + key: tuple(shift(part, sizes, 3, c) for part in held)
        for key, held in pieces.items()
        for c in range(1, sizes[3])
    }


def near_pieces(own, side):
    pieces = {(0, 0): (own,)}
    pieces.update({(0, d): (part,) for d, part in side[0].items()})
    pieces.update({(e, 0): (part,) for e, part in side[1].items()})
    return pieces


def place_kernel(keys, counts, sizes, split, me_ref, *refs):
    outs = refs[sum(counts) :]
    at = 0
    for (c, e, d), count in zip(keys, counts):
        y = lax.rem(me_ref[1] - e + sizes[1], sizes[1])
        x = lax.rem(me_ref[2] - d + sizes[2], sizes[2])
        k = lax.rem(me_ref[3] - c + sizes[3], sizes[3])
        slot = (y * sizes[2] + x) * sizes[3] + k
        held = refs[at : at + count]
        rows, width = held[0].shape[1:]
        width = width * count
        half = width // 2
        if split:
            low, high = held if count == 2 else (held[0], held[0])
            for m in range(FF // D):
                outs[0][0, slot, m * rows : (m + 1) * rows] = low[0, :, m * D : (m + 1) * D]
            outs[1][0, slot] = high[0, :, 0 if count == 2 else half :]
        elif count == 1:
            outs[0][0, slot] = held[0][0]
        else:
            outs[0][0, slot, :, :half] = held[0][0]
            outs[0][0, slot, :, half:] = held[1][0]
        at += count


def place(pieces, sizes, me, split=False):
    keys = sorted(pieces)
    counts = [len(pieces[key]) for key in keys]
    arrays = [part for key in keys for part in pieces[key]]
    rows, width = pieces[0, 0, 0][0].shape[1:]
    nz = sizes[0]
    inner = sizes[1] * sizes[2] * sizes[3]
    shapes = [(rows * (FF // D), D), (rows, FF)] if split else [(rows, width)]

    def source(z, me_ref):
        return (lax.rem(me_ref[0] - z + nz, nz), 0, 0)

    outs = pl.pallas_call(
        functools.partial(place_kernel, keys, counts, sizes, split),
        out_shape=[like((nz, inner) + shape, bf16) for shape in shapes],
        grid_spec=pltpu.PrefetchScalarGridSpec(
            num_scalar_prefetch=1,
            grid=(nz,),
            in_specs=[pl.BlockSpec((1,) + a.shape[1:], source) for a in arrays],
            out_specs=[
                pl.BlockSpec((1, inner) + shape, lambda z, me_ref: (z, 0, 0, 0)) for shape in shapes
            ],
        ),
        cost_estimate=cost_of("place"),
        name="place",
    )(me, *arrays)
    outs = [out.reshape(nz * inner * out.shape[2], out.shape[3]) for out in outs]
    return outs if split else outs[0]


def spread_kernel(sizes, split, me_ref, *refs):
    keep_ref, send_ref = refs[-2:]
    ny, nx, nc = sizes[1:]
    for ry in range(ny):
        for rx in range(nx):
            y, x = lax.rem(me_ref[1] + ry, ny), lax.rem(me_ref[2] + rx, nx)
            base = (y * nx + x) * nc
            for out_ref, core in ((keep_ref, me_ref[3]), (send_ref, 1 - me_ref[3])):
                column = 0
                rows = out_ref.shape[3]
                for at, ref in enumerate(refs[:-2]):
                    width = ref.shape[3]
                    if split and at == 0:
                        for m in range(FF // D):
                            part = ref[0, base + core, m * rows : (m + 1) * rows]
                            out_ref[0, ry, rx, :, column + m * D : column + (m + 1) * D] = part
                        column += FF
                    else:
                        out_ref[0, ry, rx, :, column : column + width] = ref[0, base + core]
                        column += width


def spread(grads, sizes, me, split=False):
    nz, ny, nx, nc = sizes
    inner = ny * nx * nc
    rows = D // math.prod(sizes)
    blocks = [g.reshape(nz, inner, g.shape[0] // (nz * inner), g.shape[1]) for g in grads]
    width = sum(b.shape[2] * b.shape[3] for b in blocks) // rows
    kind = grads[0].dtype
    shape = like((nz, ny, nx, rows, width), kind)
    block = pl.BlockSpec((1, ny, nx, rows, width), lambda z, me_ref: (z, 0, 0, 0, 0))

    def source(z, me_ref):
        return (lax.rem(me_ref[0] + z, nz), 0, 0, 0)

    return pl.pallas_call(
        functools.partial(spread_kernel, sizes, split),
        out_shape=[shape, shape],
        grid_spec=pltpu.PrefetchScalarGridSpec(
            num_scalar_prefetch=1,
            grid=(nz,),
            in_specs=[pl.BlockSpec((1,) + b.shape[1:], source) for b in blocks],
            out_specs=[block, block],
        ),
        cost_estimate=cost_of("spread"),
        name="spread",
    )(me, *blocks)


def plus(first, *others):
    total = first.astype(f32)
    for other in others:
        total = total + other.astype(f32)
    return total


def fold_core_kernel(sizes, half, count, me_ref, *refs):
    nz, ny, nx, nc = sizes
    kept_ref, got_ref = refs[:2]
    width = kept_ref.shape[-1]
    outs = refs[count:]
    z = pl.program_id(0)
    for y in range(ny):
        for x in range(nx):
            first_ref, second_ref = outs[y], outs[ny + x]
            kind = first_ref.dtype
            total = plus(kept_ref[0, y, x], got_ref[0, y, x])
            first_ref[0, x] = total[:, :half].astype(kind)
            second_ref[0, y, :, : width - half] = total[:, half:].astype(kind)
            if count > 2:
                there = lax.rem(me_ref[1] + y, ny) * nx + lax.rem(me_ref[2] + x, nx)
                slot = there * nc + me_ref[3]
                extra = refs[2][0, slot] + refs[3][0, slot]
                second_ref[0, y, :, width - half :] = extra.astype(kind)


def fold_core(kept, got, sizes, me, small=()):
    nz, ny, nx, nc = sizes
    rows, width = kept.shape[3:]
    half = width // (2 * LANES) * LANES
    kind = kept.dtype
    small = [v.reshape(nz, ny * nx * nc, rows, LANES) for v in small]
    rest = width - half + (LANES if small else 0)
    block = pl.BlockSpec((1,) + kept.shape[1:], lambda z, _: (z, 0, 0, 0, 0))
    source = pl.BlockSpec(
        (1, ny * nx * nc, rows, LANES), lambda z, me_ref: (lax.rem(me_ref[0] + z, nz), 0, 0, 0)
    )
    shapes = [(nx, rows, half)] * ny + [(ny, rows, rest)] * nx
    outs = call(
        functools.partial(fold_core_kernel, sizes, half, 2 + len(small)),
        "fold_core",
        (nz,),
        [kept, got] + small,
        [block, block] + [source] * len(small),
        [like((nz,) + shape, kind) for shape in shapes],
        [pl.BlockSpec((1,) + shape, lambda z, _: (z, 0, 0, 0)) for shape in shapes],
        0,
        scalars=(me,),
    )
    return outs[:ny], outs[ny:]


def send_side(parts, sizes):
    first, second = parts
    return (
        [first[0]] + [shift(first[e], sizes, 1, e) for e in range(1, sizes[1])],
        [second[0]] + [shift(second[d], sizes, 2, d) for d in range(1, sizes[2])],
    )


def fold_side_kernel(ny, nx, *refs):
    outs = refs[ny + nx :]
    for x in range(nx):
        total = plus(*[ref[0, x] for ref in refs[:ny]])
        outs[x][0] = total.astype(outs[x].dtype)
    for y in range(ny):
        total = plus(*[ref[0, y] for ref in refs[ny : ny + nx]])
        outs[nx + y][0] = total.astype(outs[nx + y].dtype)


def fold_side(got, sizes):
    nz, ny, nx, _ = sizes
    ins = list(got[0]) + list(got[1])
    shapes = [a.shape[2:] for a in (ins[0],) * nx + (ins[-1],) * ny]
    outs = call(
        functools.partial(fold_side_kernel, ny, nx),
        "fold_side",
        (nz,),
        ins,
        [pl.BlockSpec((1,) + a.shape[1:], lambda z: (z, 0, 0, 0)) for a in ins],
        [like((nz,) + shape, ins[0].dtype) for shape in shapes],
        [pl.BlockSpec((1,) + shape, lambda z: (z, 0, 0)) for shape in shapes],
        0,
    )
    return outs[:nx], outs[nx:]


def send_corner(parts, sizes):
    first, second = parts
    return (
        [first[0]] + [shift(first[d], sizes, 2, d) for d in range(1, sizes[2])],
        [second[0]] + [shift(second[e], sizes, 1, e) for e in range(1, sizes[1])],
    )


def fold_corner_kernel(nx, ny, *refs):
    outs = refs[nx + ny :]
    half = refs[0].shape[-1]
    for z, out_ref in enumerate(outs):
        out_ref[:, :half] = plus(*[ref[z] for ref in refs[:nx]]).astype(out_ref.dtype)
        out_ref[:, half:] = plus(*[ref[z] for ref in refs[nx : nx + ny]]).astype(out_ref.dtype)


def fold_corner(got, sizes):
    nz, ny, nx, _ = sizes
    ins = list(got[0]) + list(got[1])
    shape = (ins[0].shape[1], ins[0].shape[2] + ins[-1].shape[2])
    return call(
        functools.partial(fold_corner_kernel, nx, ny),
        "fold_corner",
        (1,),
        ins,
        [whole(a.shape) for a in ins],
        [like(shape, ins[0].dtype)] * nz,
        [whole(shape)] * nz,
        0,
    )


def send_z(parts, sizes):
    return [parts[0]] + [shift(parts[z], sizes, 0, z) for z in range(1, sizes[0])]


def fold_z_kernel(parts, count, *refs):
    total = plus(*[ref[...] for ref in refs[:count]])
    rows = total.shape[0]
    for (start, width, stack), out_ref in zip(parts, refs[count:]):
        if stack == 0:
            out_ref[...] = total[:, start : start + width].T
            continue
        part = width // stack
        for m in range(stack):
            column = start + m * part
            out_ref[m * rows : (m + 1) * rows] = total[:, column : column + part]


def fold_z(got, parts):
    rows = got[0].shape[0]
    shapes = [
        (rows * stack, width // stack) if stack else (width, rows) for _, width, stack in parts
    ]
    return call(
        functools.partial(fold_z_kernel, parts, len(got)),
        "fold_z",
        (1,),
        got,
        [whole(a.shape) for a in got],
        [like(shape, f32) for shape in shapes],
        [whole(shape) for shape in shapes],
        0,
    )


def dot_nn(a, b):
    return lax.dot_general(a, b, (((1,), (0,)), ((), ())), preferred_element_type=f32)


def dot_nt(a, b):
    return lax.dot_general(a, b, (((1,), (1,)), ((), ())), preferred_element_type=f32)


def dot_tn(a, b):
    return lax.dot_general(a, b, (((0,), (0,)), ((), ())), preferred_element_type=f32)


def normed_of(values):
    average = jnp.mean(values, -1, keepdims=True)
    centred = values - average
    inverse = lax.rsqrt(jnp.mean(centred * centred, -1, keepdims=True) + epsilon)
    return centred * inverse, inverse


def norm_back(incoming, normed, inverse, gain):
    scaled = incoming * gain
    inner = (
        scaled
        - jnp.mean(scaled, -1, keepdims=True)
        - normed * jnp.mean(scaled * normed, -1, keepdims=True)
    )
    return inner * inverse


def sum_rows(values):
    return jnp.sum(values, 0, keepdims=True)


def lane_halves(kind):
    lane = lax.broadcasted_iota(jnp.int32, (1, LANES), 1)
    low = jnp.where(lane < HEAD_DIM, 1.0, 0.0)
    return (low.astype(kind), (1.0 - low).astype(kind))


def turn(tile, cosine, sine):
    lane = lax.broadcasted_iota(jnp.int32, (1, LANES), 1)
    half_dim = HEAD_DIM // 2
    lower = (lane & half_dim) == 0
    other = jnp.where(
        lower, pltpu.roll(tile, LANES - half_dim, 1), pltpu.roll(tile, half_dim, 1)
    )
    return tile * cosine + other * sine


def rotary_tables():
    half_dim = HEAD_DIM // 2
    inverse = np.exp(np.arange(half_dim) * (-2.0 * math.log(rope_base) / HEAD_DIM))
    coarse = np.arange(0, SEQ_LEN, STEP)[:, None, None] * inverse
    fine = np.arange(STEP)[None, :, None] * inverse

    def pick(values, signs=(1.0, 1.0, 1.0, 1.0)):
        return jnp.asarray(np.concatenate([s * values for s in signs], -1), f32)

    signs = (-1.0, 1.0, -1.0, 1.0)
    cos_a, sin_a = pick(np.cos(coarse)), pick(np.sin(coarse))
    cos_b, sin_b = pick(np.cos(fine)), pick(np.sin(fine))
    cosine = cos_a * cos_b - sin_a * sin_b
    sine = pick(np.sin(coarse), signs) * cos_b + cos_a * pick(np.sin(fine), signs)
    return cosine.reshape(SEQ_LEN, LANES), sine.reshape(SEQ_LEN, LANES)


def call(
    kernel,
    name,
    grid,
    ins,
    in_specs,
    outs,
    out_specs,
    flops,
    scratch=(),
    scalars=(),
    exps=0,
    aliases={},
):
    return pl.pallas_call(
        kernel,
        out_shape=outs,
        grid_spec=pltpu.PrefetchScalarGridSpec(
            num_scalar_prefetch=len(scalars),
            grid=grid,
            in_specs=in_specs,
            out_specs=out_specs,
            scratch_shapes=scratch,
        ),
        compiler_params=pltpu.CompilerParams(
            dimension_semantics=("arbitrary",) * len(grid), vmem_limit_bytes=60 << 20
        ),
        input_output_aliases=aliases,
        cost_estimate=cost_of(name),
        name=name,
    )(*scalars, *ins)


def like(shape, kind):
    return jax.ShapeDtypeStruct(shape, kind)


def whole(shape):
    return pl.BlockSpec(shape, lambda *_: (0,) * len(shape))


def qkv_kernel(x_ref, w_ref, vec_ref, cos_ref, sin_ref, a1_ref, out_ref):
    part = pl.program_id(0)
    rows = x_ref.shape[0]
    width = w_ref.shape[1]

    @pl.when(part == 0)
    def _():
        def enter(i, _):
            part = pl.ds(pl.multiple_of(i * ROWS, ROWS), ROWS)
            normed, _ = normed_of(x_ref[part].astype(f32))
            a1_ref[part] = (normed * vec_ref[8:9, :D] + vec_ref[11:12, :D]).astype(bf16)
            return 0

        lax.fori_loop(0, rows // ROWS, enter, 0)

    column = pl.multiple_of(lax.rem(part, D // width) * width, width)
    bias = vec_ref[pl.ds(part // (D // width), 1), pl.ds(column, width)]
    for r in range(0, rows, ROWS):
        mixed = dot_nn(a1_ref[r : r + ROWS], w_ref[...]) + bias
        at = r % SEQ_LEN
        cosine, sine = cos_ref[0, at : at + ROWS], sin_ref[0, at : at + ROWS]
        for c in range(0, width, LANES):
            turned = turn(mixed[:, c : c + LANES], cosine, sine)
            out_ref[r : r + ROWS, c : c + LANES] = turned.astype(bf16)


def qkv_project(x, weight, vec, cosine, sine):
    rows = x.shape[0]
    width = QKV_TILE
    tables = (
        jnp.stack([cosine, jnp.ones_like(cosine)]),
        jnp.stack([sine, jnp.zeros_like(sine)]),
    )
    table = pl.BlockSpec((1, SEQ_LEN, LANES), lambda j: (j // (2 * D // width), 0, 0))
    return call(
        qkv_kernel,
        "qkv_project",
        (3 * D // width,),
        (x, weight, vec) + tables,
        [
            whole((rows, D)),
            pl.BlockSpec((D, width), lambda j: (0, j)),
            whole(vec.shape),
            table,
            table,
        ],
        (like((rows, D), bf16), like((rows, 3 * D), bf16)),
        (whole((rows, D)), pl.BlockSpec((rows, width), lambda j: (0, j))),
        2 * rows * D * 3 * D,
    )


def blocks_of(lengths_ref, seq, positions):
    end, found = 0, jnp.zeros(positions.shape, jnp.int32)
    for i in range(3):
        end = end + lengths_ref[seq, i]
        found = found + (positions >= end).astype(jnp.int32)
    return found


def mask_features(lengths_ref, seq):
    rows = lax.broadcasted_iota(jnp.int32, (SEQ_LEN, LANES), 0)
    slot = lax.broadcasted_iota(jnp.int32, (SEQ_LEN, LANES), 1) & (HEAD_DIM - 1)
    block = blocks_of(lengths_ref, seq, rows)
    later = (slot > block) & (slot < 4)
    return (
        jnp.where(later, -1e30, 0.0).astype(bf16),
        jnp.where(slot == block, 1.0, 0.0).astype(bf16),
    )


def self_kernel(lengths_ref, q_ref, k_ref, v_ref, o_ref, lse_ref, fq_ref, fk_ref):
    seq = pl.program_id(0)

    @pl.when(pl.program_id(1) == 0)
    def _():
        fq_ref[...], fk_ref[...] = mask_features(lengths_ref, seq)

    keep = lane_halves(bf16)
    low_lane = lax.broadcasted_iota(jnp.int32, (1, LANES), 1) < HEAD_DIM
    ones = jnp.ones((SEQ_LEN, LANES), bf16)
    starts = range(0, SEQ_LEN, ROWS)
    for c in range(0, q_ref.shape[1], LANES):
        lanes = slice(c, c + LANES)
        query, key = q_ref[:, lanes] * scale, k_ref[:, lanes]
        queries = [query * keep[h] + fq_ref[...] * keep[1 - h] for h in range(2)]
        keys = [key * keep[h] + fk_ref[...] * keep[1 - h] for h in range(2)]
        value = jnp.concatenate([v_ref[:, lanes], ones], 1)
        parts = [(r, h) for r in starts for h in range(2)]
        scores = [dot_nt(queries[h][r : r + ROWS], keys[h]) for r, h in parts]
        tops = [jnp.max(s, -1, keepdims=True) for s in scores]
        weights = [jnp.exp(s - top).astype(bf16) for s, top in zip(scores, tops)]
        outs = [dot_nn(w, value) for w in weights]
        for i, r in enumerate(starts):
            first, second = outs[2 * i], outs[2 * i + 1]
            total = jnp.where(low_lane, first[:, LANES:], second[:, LANES:])
            out = jnp.where(low_lane, first[:, :LANES], second[:, :LANES]) / total
            o_ref[r : r + ROWS, lanes] = out.astype(bf16)
            other = jnp.where(low_lane, second[:, LANES:], first[:, LANES:])
            top = jnp.where(low_lane, tops[2 * i + 1], tops[2 * i])
            lse_ref[r : r + ROWS, lanes] = top + jnp.log(other)


def self_attend(lengths, qkv):
    rows = qkv.shape[0]
    seqs = rows // SEQ_LEN
    width = SELF_WIDE * LANES
    steps = PAIRS // SELF_WIDE

    def at(offset):
        return pl.BlockSpec((SEQ_LEN, width), lambda s, p, _: (s, offset + p))

    return call(
        self_kernel,
        "self_attend",
        (seqs, steps),
        (qkv, qkv, qkv),
        [at(0), at(steps), at(2 * steps)],
        (like((rows, D), bf16), like((rows, D), f32)),
        (at(0), at(0)),
        4 * rows * SEQ_LEN * D,
        scratch=[pltpu.VMEM((SEQ_LEN, LANES), bf16)] * 2,
        scalars=(lengths,),
        exps=rows * SEQ_LEN * HEADS,
    )


def self_back_kernel(
    seq, lengths_ref, q_ref, k_ref, v_ref, do_ref, lse_ref, cos_ref, sin_ref, *rest
):
    pair = pl.program_id(0)
    out_ref, fq_ref, fk_ref = rest[-3:]
    slot = lax.broadcasted_iota(jnp.int32, (1, LANES), 1) & (HEAD_DIM - 1)

    @pl.when(pair == 0)
    def _():
        features = mask_features(lengths_ref, seq)
        fq_ref[...] = features[0]
        fk_ref[...] = features[1] + jnp.where((slot >= 4) & (slot < 7), 1.0, 0.0).astype(bf16)

    keep = lane_halves(bf16)
    low_lane = lax.broadcasted_iota(jnp.int32, (1, LANES), 1) < HEAD_DIM
    rest_of = -lse_ref[...]
    total = jnp.zeros_like(rest_of)
    for i in range(3):
        digit = rest_of.astype(bf16).astype(f32)
        total = jnp.where(slot == 4 + i, digit, total)
        rest_of = rest_of - digit
    features = fq_ref[...] + total.astype(bf16)
    query, key, value, upstream = q_ref[...], k_ref[...], v_ref[...], do_ref[...]
    scaled = key * scale
    heads = range(2)
    keys = [scaled * keep[h] + fk_ref[...] * keep[1 - h] for h in heads]
    queries = [query * keep[h] + features * keep[1 - h] for h in heads]
    probs = [jnp.exp(dot_nt(keys[h], queries[h])) for h in heads]
    dprobs = [dot_nt(value * keep[h], upstream) for h in heads]
    inners = [jnp.sum(p * dp, 0, keepdims=True) for p, dp in zip(probs, dprobs)]
    dscores = [
        (p * (dp - inner)).astype(bf16) for p, dp, inner in zip(probs, dprobs, inners)
    ]
    dvs = [dot_nn(p.astype(bf16), upstream) for p in probs]
    dks = [dot_nn(ds, query) for ds in dscores]
    dqs = [dot_tn(ds, key) for ds in dscores]
    cosine, sine = cos_ref[...], -sin_ref[...]
    dq = jnp.where(low_lane, dqs[0], dqs[1]) * scale
    dk = jnp.where(low_lane, dks[0], dks[1]) * scale
    dv = jnp.where(low_lane, dvs[0], dvs[1])
    for part, found in enumerate((turn(dq, cosine, sine), turn(dk, cosine, sine), dv)):
        column = pl.multiple_of((part * PAIRS + pair) * LANES, LANES)
        out_ref[:, pl.ds(column, LANES)] = found.astype(bf16)


def self_back(seq, lengths, qkv, do, lse, cosine, sine, earlier=None):
    rows = qkv.shape[0]
    block = (SEQ_LEN, LANES)

    def at(offset):
        return pl.BlockSpec(block, lambda p, _: (seq, offset + p))

    kernel = functools.partial(self_back_kernel, seq)
    ins = [qkv, qkv, qkv, do, lse, cosine, sine]
    specs = [at(0), at(PAIRS), at(2 * PAIRS), at(0), at(0), whole(block), whole(block)]
    aliases = {}
    if earlier is not None:
        ins.append(earlier)
        specs.append(pl.BlockSpec(memory_space=pl.ANY))
        aliases = {len(ins): 0}
    return call(
        kernel,
        "self_back",
        (PAIRS,),
        ins,
        specs,
        like((rows, 3 * D), bf16),
        pl.BlockSpec((SEQ_LEN, 3 * D), lambda p, _: (seq, 0)),
        10 * SEQ_LEN * SEQ_LEN * D,
        scratch=[pltpu.VMEM(block, bf16)] * 2,
        scalars=(lengths,),
        exps=SEQ_LEN * SEQ_LEN * HEADS,
        aliases=aliases,
    )


def mid_kernel(o_ref, x_ref, wo_ref, wq_ref, vec_ref, h1_ref, a2_ref, cq_ref):
    h1 = x_ref[...].astype(f32) + dot_nn(o_ref[...], wo_ref[...]) + vec_ref[3:4]
    h1_ref[...] = h1
    normed, _ = normed_of(h1)
    a2 = (normed * vec_ref[9:10] + vec_ref[12:13]).astype(bf16)
    a2_ref[...] = a2
    cq_ref[...] = (dot_nn(a2, wq_ref[...]) + vec_ref[4:5]).astype(bf16)


def mid_forward(o, x, mid, vec):
    rows = x.shape[0]
    block = pl.BlockSpec((ROWS, D), lambda r: (r, 0))
    return call(
        mid_kernel,
        "mid_forward",
        (rows // ROWS,),
        (o, x, mid, mid, vec),
        [
            block,
            block,
            pl.BlockSpec((D, D), lambda r: (0, 2)),
            pl.BlockSpec((D, D), lambda r: (0, 3)),
            whole(vec.shape),
        ],
        (like((rows, D), f32), like((rows, D), bf16), like((rows, D), bf16)),
        (block, block, block),
        4 * rows * D * D,
    )


def ckv_kernel(n_ref, w_ref, vec_ref, out_ref):
    mixed = dot_nn(n_ref[...], w_ref[...])
    out_ref[:, :D] = mixed[:, :D].astype(bf16)
    out_ref[:, D:] = (mixed[:, D:] + vec_ref[5:6]).astype(bf16)


def ckv_project(n, mid, vec):
    rows = n.shape[0]
    return call(
        ckv_kernel,
        "ckv_project",
        (rows // ROWS,),
        (n, mid, vec),
        [
            pl.BlockSpec((ROWS, D), lambda r: (r, 0)),
            pl.BlockSpec((D, 2 * D), lambda r: (0, 0)),
            whole(vec.shape),
        ],
        like((rows, 2 * D), bf16),
        pl.BlockSpec((ROWS, 2 * D), lambda r: (r, 0)),
        4 * rows * D * D,
    )


def slots(chosen_ref, seq, span):
    found = []
    for i in range(K_NBR):
        entry = chosen_ref[seq, span * K_NBR + i]
        found.append(pl.multiple_of(entry * NBR_LEN, NBR_LEN))
    return found


def chosen_rows(ref, starts, lanes=slice(None)):
    return jnp.concatenate([ref[pl.ds(start, NBR_LEN), lanes] for start in starts], 0)


def cross_kernel(chosen_ref, q_ref, k_ref, v_ref, o_ref):
    seq = pl.program_id(0)
    keep = lane_halves(bf16)
    low_lane = lax.broadcasted_iota(jnp.int32, (1, LANES), 1) < HEAD_DIM
    starts = [slots(chosen_ref, seq, c) for c in range(SPANS)]
    spans = [slice(c * SPAN, (c + 1) * SPAN) for c in range(SPANS)]
    ones = jnp.ones((K_NBR * NBR_LEN, LANES), bf16)
    for c in range(0, q_ref.shape[1], LANES):
        lanes = slice(c, c + LANES)
        query = q_ref[:, lanes] * scale
        halves = [query * keep[h] for h in range(2)]
        both = [jnp.concatenate([half[span] for half in halves], 0) for span in spans]
        scores = [dot_nt(b, chosen_rows(k_ref, at, lanes)) for b, at in zip(both, starts)]
        tops = [jnp.max(s, -1, keepdims=True) for s in scores]
        weights = [jnp.exp(s - top).astype(bf16) for s, top in zip(scores, tops)]
        outs = [
            dot_nn(w, jnp.concatenate([chosen_rows(v_ref, at, lanes), ones], 1))
            for w, at in zip(weights, starts)
        ]
        for span, out in zip(spans, outs):
            total = jnp.where(low_lane, out[:SPAN, LANES:], out[SPAN:, LANES:])
            out = jnp.where(low_lane, out[:SPAN, :LANES], out[SPAN:, :LANES]) / total
            o_ref[span, lanes] = out.astype(bf16)


def cross_attend(chosen, cq, ckv):
    rows = cq.shape[0]
    seqs = rows // SEQ_LEN
    width = WIDE * LANES
    steps = PAIRS // WIDE

    def at(offset):
        return pl.BlockSpec((SEQ_LEN, width), lambda s, p, _: (s, offset + p))

    return call(
        cross_kernel,
        "cross_attend",
        (seqs, steps),
        (cq, ckv, ckv),
        [at(0), at(0), at(steps)],
        like((rows, D), bf16),
        at(0),
        2 * rows * SEQ_LEN * D,
        scalars=(chosen,),
        exps=rows * K_NBR * NBR_LEN * HEADS,
    )


def cross_back_kernel(
    chosen_ref, q_ref, k_ref, v_ref, do_ref, dq_ref, dkv_ref, sums_ref, dk_ref, dv_ref, acc_ref
):
    seq, pair = pl.program_id(0), pl.program_id(1)
    keep = lane_halves(bf16)
    low_lane = lax.broadcasted_iota(jnp.int32, (1, LANES), 1) < HEAD_DIM
    starts = [slots(chosen_ref, seq, c) for c in range(SPANS)]
    spans = [slice(c * SPAN, (c + 1) * SPAN) for c in range(SPANS)]

    def stacked(ref):
        halves = [ref[...] * keep[h] for h in range(2)]
        return [jnp.concatenate([half[span] for half in halves], 0) for span in spans]

    queries, upstreams = stacked(q_ref), stacked(do_ref)
    keys = [chosen_rows(k_ref, at) for at in starts]
    scores = jnp.concatenate([dot_nt(k, q) for k, q in zip(keys, queries)], 1) * scale
    dprob = jnp.concatenate(
        [dot_nt(chosen_rows(v_ref, at), up) for at, up in zip(starts, upstreams)], 1
    )
    exponent = jnp.exp(scores - jnp.max(scores, 0, keepdims=True))
    prob = exponent * (1.0 / jnp.sum(exponent, 0, keepdims=True))
    inner = jnp.sum(prob * dprob, 0, keepdims=True)
    dscore = (prob * (dprob - inner)).astype(bf16)
    prob = prob.astype(bf16)
    for c in range(SPANS):
        columns = slice(c * LANES, (c + 1) * LANES)
        dv_ref[c] = dot_nn(prob[:, columns], upstreams[c])
        dk_ref[c] = dot_nn(dscore[:, columns], queries[c])
    dqs = [
        dot_tn(dscore[:, c * LANES : (c + 1) * LANES], keys[c]) * scale for c in range(SPANS)
    ]
    for span, dq in zip(spans, dqs):
        dq_ref[span] = jnp.where(low_lane, dq[:SPAN], dq[SPAN:]).astype(bf16)
    for part, found_ref in enumerate((dk_ref, dv_ref)):
        acc_ref[...] = jnp.zeros_like(acc_ref)
        for c in range(SPANS):
            for i, start in enumerate(starts[c]):
                rows = slice(i * NBR_LEN, (i + 1) * NBR_LEN)
                acc_ref[pl.ds(start, NBR_LEN), :] += found_ref[c, rows]
        column = pl.multiple_of((part * PAIRS + pair) * LANES, LANES)
        total = acc_ref[...] * scale if part == 0 else acc_ref[...]
        rounded = total.astype(bf16)
        dkv_ref[:, pl.ds(column, LANES)] = rounded
    sums_ref[...] = jnp.broadcast_to(sum_rows(rounded.astype(f32)), sums_ref.shape)


def cross_back(chosen, cq, ckv, dco):
    rows = cq.shape[0]
    seqs = rows // SEQ_LEN
    block = (SEQ_LEN, LANES)

    def at(offset):
        return pl.BlockSpec(block, lambda s, p, _: (s, offset + p))

    return call(
        cross_back_kernel,
        "cross_back",
        (seqs, PAIRS),
        (cq, ckv, ckv, dco),
        [at(0), at(0), at(PAIRS), at(0)],
        (like((rows, D), bf16), like((rows, 2 * D), bf16), like((8 * seqs, D), f32)),
        (
            at(0),
            pl.BlockSpec((SEQ_LEN, 2 * D), lambda s, p, _: (s, 0)),
            pl.BlockSpec((8, LANES), lambda s, p, _: (s, p)),
        ),
        5 * rows * SEQ_LEN * D,
        scratch=[
            pltpu.VMEM((SPANS, K_NBR * NBR_LEN, LANES), f32),
            pltpu.VMEM((SPANS, K_NBR * NBR_LEN, LANES), f32),
            pltpu.VMEM(block, f32),
        ],
        scalars=(chosen,),
        exps=rows * K_NBR * NBR_LEN * HEADS,
    )


def gelu_pair(hidden):
    root_coeff = math.sqrt(2.0 / math.pi)
    square = hidden * hidden
    tangent = jnp.tanh(root_coeff * hidden * (1.0 + gelu_coeff * square))
    upper = 0.5 * (1.0 + tangent)
    slope = upper + (0.5 * root_coeff) * hidden * (1.0 - tangent * tangent) * (
        1.0 + (3.0 * gelu_coeff) * square
    )
    return hidden * upper, slope


def mlp_kernel(
    h1_ref,
    co_ref,
    dy_ref,
    wco_ref,
    wu_ref,
    wd_ref,
    bu_ref,
    vec_ref,
    a3_ref,
    g_ref,
    du_ref,
    out_ref,
    dh2_ref,
    e2_ref,
    dco_ref,
    sums_ref,
    dbu_ref,
    y_acc,
    da_acc,
    h2_ref,
):
    step = pl.program_id(0)
    rows = h1_ref.shape[0]
    chunks = rows // MLP_ROWS
    nothing = jnp.zeros((1, D), f32)

    def part_of(i, size=EDGE_ROWS):
        return pl.ds(pl.multiple_of(i * size, size), size)

    @pl.when(step == 0)
    def _():
        def enter(i, _):
            part = part_of(i)
            h2 = h1_ref[part] + dot_nn(co_ref[part], wco_ref[...]) + vec_ref[6:7]
            h2_ref[part] = h2
            normed, _ = normed_of(h2)
            a3_ref[part] = (normed * vec_ref[10:11] + vec_ref[13:14]).astype(bf16)
            y_acc[part] = h2 + vec_ref[7:8]
            da_acc[part] = jnp.zeros_like(h2)
            return 0

        lax.fori_loop(0, rows // EDGE_ROWS, enter, 0)

    def body(i, bias_sum):
        part = part_of(i, MLP_ROWS)
        hidden = dot_nn(a3_ref[part], wu_ref[...]) + bu_ref[...]
        dg = dot_nt(dy_ref[part], wd_ref[...])
        value, slope = gelu_pair(hidden)
        g = value.astype(bf16)
        du = (dg * slope).astype(bf16)
        g_ref[part] = g
        du_ref[part] = du
        y_acc[part] += dot_nn(g, wd_ref[...])
        da_acc[part] += dot_nt(du, wu_ref[...])
        return bias_sum + sum_rows(du.astype(f32))

    dbu_ref[...] = lax.fori_loop(0, chunks, body, jnp.zeros(dbu_ref.shape, f32))

    @pl.when(step == pl.num_programs(0) - 1)
    def _():
        def leave(i, sums):
            part = part_of(i)
            out_ref[part] = y_acc[part].astype(bf16)
            normed, inverse = normed_of(h2_ref[part])
            da3 = da_acc[part]
            upstream = dy_ref[part].astype(f32)
            dh2 = upstream + norm_back(da3, normed, inverse, vec_ref[10:11])
            dh2_ref[part] = dh2
            e2 = dh2.astype(bf16)
            e2_ref[part] = e2
            dco_ref[part] = dot_nt(e2, wco_ref[...]).astype(bf16)
            found = (da3 * normed, da3, e2.astype(f32), upstream)
            return tuple(total + sum_rows(value) for total, value in zip(sums, found))

        found = lax.fori_loop(0, rows // EDGE_ROWS, leave, (nothing,) * 4)
        for i, total in enumerate(found):
            sums_ref[i : i + 1] = total


def mlp_both(h1, co, dy, mid, wu, wd, bu, vec):
    rows = h1.shape[0]
    full = whole((rows, D))
    wide = pl.BlockSpec((rows, TILE_F), lambda f: (0, f))
    return call(
        mlp_kernel,
        "mlp_both",
        (FF // TILE_F,),
        (h1, co, dy, mid, wu, wd, bu, vec),
        [
            full,
            full,
            full,
            pl.BlockSpec((D, D), lambda f: (0, 4)),
            pl.BlockSpec((D, TILE_F), lambda f: (0, f)),
            pl.BlockSpec((TILE_F, D), lambda f: (f, 0)),
            pl.BlockSpec((1, TILE_F), lambda f: (0, f)),
            whole(vec.shape),
        ],
        (
            like((rows, D), bf16),
            like((rows, FF), bf16),
            like((rows, FF), bf16),
            like((rows, D), bf16),
            like((rows, D), f32),
            like((rows, D), bf16),
            like((rows, D), bf16),
            like((8, D), f32),
            like((1, FF), f32),
        ),
        (
            full,
            wide,
            wide,
            full,
            full,
            full,
            full,
            whole((8, D)),
            pl.BlockSpec((1, TILE_F), lambda f: (0, f)),
        ),
        2 * rows * D * (4 * FF + 2 * D),
        scratch=[pltpu.VMEM((rows, D), f32)] * 3,
        exps=rows * FF,
    )


def mid_back_kernel(
    dcq_ref, dh2_ref, h1_ref, wq_ref, wo_ref, vec_ref, dh1_ref, e1_ref, do_ref, sums_ref
):
    @pl.when(pl.program_id(0) == 0)
    def _():
        sums_ref[...] = jnp.zeros_like(sums_ref)

    da2 = dot_nt(dcq_ref[...], wq_ref[...])
    normed, inverse = normed_of(h1_ref[...])
    dh1 = dh2_ref[...] + norm_back(da2, normed, inverse, vec_ref[9:10])
    dh1_ref[...] = dh1
    e1 = dh1.astype(bf16)
    e1_ref[...] = e1
    do_ref[...] = dot_nt(e1, wo_ref[...]).astype(bf16)
    sums_ref[0:1] += sum_rows(da2 * normed)
    sums_ref[1:2] += sum_rows(da2)
    sums_ref[2:3] += sum_rows(dcq_ref[...].astype(f32))
    sums_ref[3:4] += sum_rows(e1.astype(f32))


def mid_back(dcq, dh2, h1, mid, vec):
    rows = h1.shape[0]
    block = pl.BlockSpec((ROWS, D), lambda r: (r, 0))
    return call(
        mid_back_kernel,
        "mid_back",
        (rows // ROWS,),
        (dcq, dh2, h1, mid, mid, vec),
        [
            block,
            block,
            block,
            pl.BlockSpec((D, D), lambda r: (0, 3)),
            pl.BlockSpec((D, D), lambda r: (0, 2)),
            whole(vec.shape),
        ],
        (
            like((rows, D), f32),
            like((rows, D), bf16),
            like((rows, D), bf16),
            like((8, D), f32),
        ),
        (block, block, block, whole((8, D))),
        4 * rows * D * D,
    )


def token_back_kernel(dqkv_ref, dh1_ref, x_ref, w_ref, vec_ref, dx_ref, sums_ref, qkv_sums_ref):
    @pl.when(pl.program_id(0) == 0)
    def _():
        sums_ref[...] = jnp.zeros_like(sums_ref)
        qkv_sums_ref[...] = jnp.zeros_like(qkv_sums_ref)

    da1 = dot_nt(dqkv_ref[...], w_ref[...])
    normed, inverse = normed_of(x_ref[...].astype(f32))
    dx_ref[...] = dh1_ref[...] + norm_back(da1, normed, inverse, vec_ref[8:9])
    sums_ref[0:1] += sum_rows(da1 * normed)
    sums_ref[1:2] += sum_rows(da1)
    qkv_sums_ref[...] += sum_rows(dqkv_ref[...].astype(f32))


def token_back(dqkv, dh1, x, weight, vec):
    rows = x.shape[0]
    block = pl.BlockSpec((ROWS, D), lambda r: (r, 0))
    return call(
        token_back_kernel,
        "token_back",
        (rows // ROWS,),
        (dqkv, dh1, x, weight, vec),
        [
            pl.BlockSpec((ROWS, 3 * D), lambda r: (r, 0)),
            block,
            block,
            pl.BlockSpec((D, 3 * D), lambda r: (0, 0)),
            whole(vec.shape),
        ],
        (like((rows, D), f32), like((8, D), f32), like((1, 3 * D), f32)),
        (block, whole((8, D)), whole((1, 3 * D))),
        6 * rows * D * D,
    )


def neighbour_kernel(dkv_ref, w_ref, dn_ref):
    dn_ref[...] = dot_nt(dkv_ref[...], w_ref[...])


def neighbour_back(dckv, mid):
    rows = dckv.shape[0]
    return call(
        neighbour_kernel,
        "neighbour_back",
        (rows // ROWS,),
        (dckv, mid),
        [
            pl.BlockSpec((ROWS, 2 * D), lambda r: (r, 0)),
            pl.BlockSpec((D, 2 * D), lambda r: (0, 0)),
        ],
        like((rows, D), f32),
        pl.BlockSpec((ROWS, D), lambda r: (r, 0)),
        4 * rows * D * D,
    )


def weight_grad(left, right):
    return dot_tn(left, right).astype(bf16)


def grad_kernel(sizes, stack, me_ref, left_ref, right_ref, *refs):
    keep_ref, send_ref, acc_ref = refs[-3:]
    nz, ny, nx, nc = sizes
    rows = keep_ref.shape[3]
    acc_ref[...] = dot_tn(left_ref[...], right_ref[...])
    for z in range(keep_ref.shape[0]):
        at_z = lax.rem(me_ref[0] + z, nz) if keep_ref.shape[0] > 1 else 0
        for y in range(ny):
            for x in range(nx):
                at = at_z * ny + lax.rem(me_ref[1] + y, ny)
                at = (at * nx + lax.rem(me_ref[2] + x, nx)) * nc
                for out_ref, core in ((keep_ref, me_ref[3]), (send_ref, nc - 1 - me_ref[3])):
                    for m in range(stack):
                        row = pl.multiple_of(((at + core) * stack + m) * rows, 8)
                        part = acc_ref[pl.ds(row, rows), :]
                        out_ref[z, y, x, :, m * D : (m + 1) * D] = part.astype(bf16)


def grad_blocks(left, right, sizes, me, width, column=0, earlier=()):
    nz, ny, nx, _ = sizes
    rows = D // math.prod(sizes)
    stack = left.shape[1] // D
    count = left.shape[0]
    if stack == 1:
        grid = (right.shape[1] // D,)
        left_spec = whole(left.shape)
        right_spec = pl.BlockSpec((count, D), lambda j, _: (0, j))
        block = pl.BlockSpec((nz, ny, nx, rows, D), lambda j, _: (0, 0, 0, 0, column // D + j))
        held = D
    else:
        grid = (nz,)
        held = left.shape[1] // nz
        left_spec = pl.BlockSpec(
            (count, held), lambda z, me_ref: (0, lax.rem(me_ref[0] + z, nz))
        )
        right_spec = whole(right.shape)
        block = pl.BlockSpec(
            (1, ny, nx, rows, stack * D), lambda z, _: (z, 0, 0, 0, column // (stack * D))
        )
    shape = like((nz, ny, nx, rows, width), bf16)
    earlier = list(earlier)
    return call(
        functools.partial(grad_kernel, sizes, stack),
        "grad_blocks",
        grid,
        [left, right] + earlier,
        [left_spec, right_spec] + [pl.BlockSpec(memory_space=pl.ANY)] * len(earlier),
        [shape, shape],
        [block, block],
        0,
        scratch=[pltpu.VMEM((held, D), f32)],
        scalars=(me,),
        aliases={3: 0, 4: 1} if earlier else {},
    )


def many_kernel(sizes, plan, count, me_ref, *refs):
    arrays = refs[:count]
    keep_ref, send_ref, left_buf, right_buf, acc_ref, sems = refs[count:]
    step = pl.program_id(0)

    def copies(k, slot):
        left, right, column = plan[k]
        source = arrays[right].at[:, column : column + D]
        return (
            pltpu.make_async_copy(arrays[left], left_buf.at[slot], sems.at[0, slot]),
            pltpu.make_async_copy(source, right_buf.at[slot], sems.at[1, slot]),
        )

    for k in range(len(plan)):

        @pl.when(step == max(k - 1, 0))
        def _():
            for copy in copies(k, k % 2):
                copy.start()

    slot = lax.rem(step, 2)
    for k in range(len(plan)):

        @pl.when(step == k)
        def _():
            for copy in copies(k, k % 2):
                copy.wait()

    grad_kernel(sizes, 1, me_ref, left_buf.at[slot], right_buf.at[slot], keep_ref, send_ref, acc_ref)


def many_grads(pairs, sizes, me):
    nz, ny, nx, _ = sizes
    rows = D // math.prod(sizes)
    arrays, plan = [], []
    for left, right in pairs:
        at = len(arrays)
        arrays += [left, right]
        plan += [(at, at + 1, column) for column in range(0, right.shape[1], D)]
    shape = like((nz, ny, nx, rows, len(plan) * D), bf16)
    block = pl.BlockSpec((nz, ny, nx, rows, D), lambda j, _: (0, 0, 0, 0, j))
    buffer = pltpu.VMEM((2,) + pairs[0][0].shape, bf16)
    return call(
        functools.partial(many_kernel, sizes, plan, len(arrays)),
        "many_grads",
        (len(plan),),
        arrays,
        [pl.BlockSpec(memory_space=pl.ANY)] * len(arrays),
        [shape, shape],
        [block, block],
        0,
        scratch=[buffer, buffer, pltpu.VMEM((D, D), f32), pltpu.SemaphoreType.DMA((2, 2))],
        scalars=(me,),
    )


def grads(pairs, sizes, me, width, column=0, earlier=()):
    if all(left.shape[1] == D for left, _ in pairs) and len(pairs) > 1:
        return many_grads(pairs, sizes, me)
    for left, right in pairs:
        earlier = grad_blocks(left, right, sizes, me, width, column, earlier)
        column += left.shape[1] // D * right.shape[1]
    return earlier


def local(
    sizes,
    tokens,
    neighbours,
    block_lengths,
    chosen,
    cotangent,
    w_qkv,
    w_out,
    w_cross_q,
    w_cross_kv,
    w_cross_out,
    w_up,
    w_down,
    biases,
    up_bias,
    norm_gains,
    norm_shifts,
):
    me = coords_of(lax.axis_index("fsdp"), sizes)
    me_array = jnp.stack(me).astype(jnp.int32)
    shard = w_qkv.shape[0]
    small = jnp.concatenate(
        [biases.T, norm_gains.T, norm_shifts.T, up_bias.reshape(shard, FF // D)], 1
    )
    small = jnp.pad(small, ((0, 0), (0, LANES - SMALL)))
    first = jnp.concatenate([w_qkv, small], 1)
    middle = jnp.concatenate([w_cross_kv, w_out, w_cross_q, w_cross_out], 1)
    quarters = jnp.split(w_down, FF // D, 0)
    last = jnp.concatenate(quarters + [w_up], 1)
    cosine, sine = rotary_tables()
    picks = chosen.reshape(chosen.shape[0], SPANS * K_NBR)

    first_own = gather_z(first, sizes)
    first_side = gather_side(first_own, sizes)
    middle_own = gather_z(after(middle, first_own), sizes)
    first_pieces = near_pieces(first_own, first_side)
    first_corner = gather_corner(first_side, sizes)
    first_core = gather_core(first_pieces, sizes)
    middle_own = after(middle_own, first_corner)
    middle_side = gather_side(middle_own, sizes)
    last_own = gather_z(after(last, middle_own), sizes)
    first_pieces.update(first_corner)
    first_core.update(gather_core(first_corner, sizes))
    first_core.update({(0,) + key: held for key, held in first_pieces.items()})
    qkv_weight = place(first_core, sizes, me_array)
    gathered = qkv_weight[:, 3 * D :]
    vec = gathered[:, :16].T.astype(f32)
    up_shift = gathered[:, 14:SMALL].reshape(1, FF).astype(f32)

    a1, qkv = qkv_project(after(tokens, middle_own), qkv_weight, vec, cosine, sine)
    middle_side = after(middle_side, qkv)
    middle_pieces = near_pieces(middle_own, middle_side)
    middle_corner = gather_corner(middle_side, sizes)
    middle_core = gather_core(middle_pieces, sizes)
    o, lse = self_attend(block_lengths, after(qkv, middle_side, last_own))
    last_side = gather_side(after(last_own, o), sizes)
    middle_corner, middle_core = after((middle_corner, middle_core), o)
    middle_core.update(gather_core(middle_corner, sizes))
    middle_pieces.update(middle_corner)
    middle_core.update({(0,) + key: held for key, held in middle_pieces.items()})
    mid = place(middle_core, sizes, me_array)
    ckv = ckv_project(neighbours, mid, vec)
    h1, a2, cq = mid_forward(o, tokens, mid, vec)
    last_side = after(last_side, cq, ckv)
    last_pieces = near_pieces(last_own, last_side)
    last_corner = gather_corner(last_side, sizes)
    last_core = gather_core(last_pieces, sizes)
    co = cross_attend(picks, after(cq, last_side), ckv)
    last_corner, last_core = after((last_corner, last_core), co)
    last_core.update(gather_core(last_corner, sizes))
    last_pieces.update(last_corner)
    last_core.update({(0,) + key: held for key, held in last_pieces.items()})
    down_weight, up_weight = place(last_core, sizes, me_array, split=True)

    a3, g, du, output, dh2, e2, dco, sums3, grad_bu = mlp_both(
        h1, co, cotangent, mid, up_weight, down_weight, up_shift, vec
    )

    aligned = shard % 8 == 0

    def group(pairs, split=False):
        if aligned:
            width = sum(a.shape[1] // D * b.shape[1] for a, b in pairs)
            return grads(pairs, sizes, me_array, width)
        return spread([weight_grad(a, b) for a, b in pairs], sizes, me_array, split)

    last_kept, last_sent = group([(g, cotangent), (a3, du)], True)
    last_got = shift(last_sent, sizes, 3, 1)
    dcq, dckv, value_sums = cross_back(picks, cq, ckv, after(dco, last_sent))
    last_parts = fold_core(last_kept, after(last_got, dcq), sizes, me_array)
    last_got = send_side(last_parts, sizes)
    dh1, e1, do, sums2 = mid_back(after(dcq, last_parts), dh2, h1, mid, vec)
    middle_kept, middle_sent = group(
        [(after(neighbours, last_parts), dckv), (o, e1), (a2, dcq), (co, e2)]
    )
    middle_got = shift(middle_sent, sizes, 3, 1)
    last_parts = fold_side(after(last_got, middle_sent), sizes)
    last_got = send_corner(last_parts, sizes)
    do = after(do, middle_sent, last_parts)
    dqkv = self_back(0, block_lengths, qkv, do, lse, cosine, sine)
    last_parts = fold_corner(after(last_got, dqkv), sizes)
    last_got = send_z(last_parts, sizes)
    middle_parts = fold_core(middle_kept, after(middle_got, dqkv), sizes, me_array)
    middle_got = send_side(middle_parts, sizes)
    do = after(do, last_parts, middle_parts)
    dqkv = self_back(1, block_lengths, qkv, do, lse, cosine, sine, dqkv)
    middle_parts = fold_side(after(middle_got, dqkv), sizes)
    middle_got = send_corner(middle_parts, sizes)
    first_kept, first_sent = group([(after(a1, middle_parts), dqkv)])
    first_got = shift(first_sent, sizes, 3, 1)
    down_sum, up_sum = fold_z(after(last_got, first_sent), ((0, FF, FF // D), (FF, FF, 1)))
    middle_parts = fold_corner(after(middle_got, down_sum), sizes)
    middle_got = send_z(middle_parts, sizes)
    dqkv = after(dqkv, first_sent, middle_parts)
    token_grad, sums1, qkv_sums = token_back(dqkv, dh1, tokens, qkv_weight, vec)

    rows = jnp.concatenate(
        [
            qkv_sums.reshape(3, D),
            sums2[3:4],
            sums2[2:3],
            sum_rows(value_sums[::8]),
            sums3[2:4],
            sums1[0:1],
            sums2[0:1],
            sums3[0:1],
            sums1[1:2],
            sums2[1:2],
            sums3[1:2],
        ],
        0,
    )
    small_grad = jnp.concatenate([rows.T, grad_bu.reshape(D, FF // D)], 1)
    small_grad = jnp.pad(small_grad, ((0, 0), (0, LANES - SMALL)))
    small_got = shift(small_grad, sizes, 3, 1)
    first_parts = fold_core(
        first_kept, after(first_got, token_grad), sizes, me_array, (small_grad, small_got)
    )
    first_got = send_side(first_parts, sizes)
    neighbour_grad = neighbour_back(after(dckv, first_parts), mid)
    first_parts = fold_side(after(first_got, neighbour_grad), sizes)
    first_got = send_corner(first_parts, sizes)
    kv_sum, out_sum, cq_sum, co_sum = fold_z(
        after(middle_got, first_parts),
        ((0, 2 * D, 1), (2 * D, D, 1), (3 * D, D, 1), (4 * D, D, 1)),
    )
    first_got = send_z(fold_corner(after(first_got, kv_sum), sizes), sizes)
    first_sum, small_sum = fold_z(first_got, ((0, 3 * D, 1), (3 * D, LANES, 0)))

    return (
        output,
        token_grad,
        neighbour_grad,
        first_sum,
        out_sum,
        cq_sum,
        kv_sum,
        co_sum,
        up_sum,
        down_sum,
        small_sum[:8],
        small_sum[14:SMALL].T.reshape(-1),
        small_sum[8:11],
        small_sum[11:14],
    )


def solution(mesh):
    rowwise, columnwise = P("fsdp", None), P(None, "fsdp")
    return jax.shard_map(
        functools.partial(local, geometry(mesh.shape["fsdp"])),
        mesh=mesh,
        in_specs=(rowwise,) * 3
        + (P("fsdp", None, None),)
        + (rowwise,) * 8
        + (columnwise, P("fsdp"), columnwise, columnwise),
        out_specs=(rowwise,) * 10 + (columnwise, P("fsdp"), columnwise, columnwise),
        check_vma=False,
    )
```
